256 devices in a mesh: tm: 32 (over z, x), fsdp: 8 (over y, core).
Axes of the slice: x: 4, y: 4, z: 8, core: 2. Of those that a mesh axis runs over, the one named last changes fastest.
Arguments:
- frames: bfloat16 [64, 64, 256, 128], P('tm', None, 'fsdp'), may hold values from -6 to 6
- conv_weight: bfloat16 [3, 3, 3, 128, 128], P(None, None, None, None, 'fsdp'), may hold values from -0.109375 to 0.109375
- mix_weight: bfloat16 [3, 128, 128], P(None, None, 'fsdp'), may hold values from -0.3125 to 0.3125
- cotangent: bfloat16 [32, 64, 256, 128], P(None, 'tm', 'fsdp'), may hold values from -0.008239746 to 0.008239746
Outputs:
- encoded: bfloat16 [32, 64, 256, 128], P(None, 'tm', 'fsdp')
- mix_grad: float32 [49152], P(('tm', 'fsdp'))
The draws below stay inside these ranges and needn't reach their ends.
All inputs are finite; a program needn't handle non-finite values.
Results may differ from the reference program's by a relative error of at most 0.0058.
Values may be sent and summed in bfloat16 or wider, within the bound.
A program may use at most 64 MiB of HBM per device.

```python
import jax
import jax.numpy as jnp
from jax import lax

C = 128
FR = 64
FR2 = 32
HT = 64
WD = 256


def level_of(key, extent, cuts, least, top_value):
    loudness, own = 1.0, jax.random.fold_in(key, 6)
    for position, shards_of in cuts:
        steps = jnp.exp(jax.random.uniform(jax.random.fold_in(own, position), (shards_of,), jnp.float32, least / len(cuts), top_value / len(cuts)))
        loudness = loudness * jnp.repeat(steps, extent[position] // shards_of).reshape([-1 if axis == position else 1 for axis in range(len(extent))])
    return loudness


def scatter_about(rng, dims, scale, reach, shards=(), dtype=jnp.bfloat16):
    array = scale * jax.random.normal(rng, dims, jnp.float32)
    if shards:
        array = array * level_of(rng, dims, shards, -0.22, 0.18)
    return jnp.clip(array, -reach, reach).astype(dtype)


def setup_inputs(seed: int = 0) -> dict:
    splits = jax.random.split(jax.random.key(seed), 5)
    frames = scatter_about(splits[0], (FR, HT, WD, C), 1.0, 6.0, ((0, 32), (2, 8)))
    conv_weight = scatter_about(splits[1], (3, 3, 3, C, C), (27 * C) ** -0.5, 0.109375, ((4, 8),))
    mix_weight = scatter_about(splits[2], (3, C, C), (3 * C) ** -0.5, 0.3125, ((2, 8),))
    cotangent = scatter_about(splits[3], (FR2, HT, WD, C), (1.0 / (FR2 * HT * WD) ** 0.5), 0.008239746, ((1, 32), (2, 8)))
    return {"frames": frames, "conv_weight": conv_weight, "mix_weight": mix_weight, "cotangent": cotangent}


def pool_pairs(hidden):
    shaped = hidden.reshape((hidden.shape[0] // 2, 2) + hidden.shape[1:]).astype(jnp.float32)
    return ((shaped[:, 0] + shaped[:, 1]) * 0.5).astype(jnp.bfloat16)


def delayed(block, offset):
    return jnp.pad(block, ((offset, 0), (0, 0), (0, 0), (0, 0)))[:block.shape[0]]


def reference(frames, conv_weight, mix_weight, cotangent):
    accum = lax.conv_general_dilated(
        frames.astype(jnp.float32)[None], conv_weight.astype(jnp.float32),
        window_strides=(1, 1, 1), padding=((2, 0), (1, 1), (1, 1)),
        dimension_numbers=("NDHWC", "DHWIO", "NDHWC"),
        precision=lax.Precision.HIGHEST)[0]
    hidden = jax.nn.silu(accum).astype(jnp.bfloat16)
    pooled = pool_pairs(hidden)
    branch = pooled.astype(jnp.float32)
    grads = []
    for offset in range(3):
        lagged = delayed(pooled, offset).astype(jnp.float32)
        branch = branch + jnp.einsum("thwc,cd->thwd", lagged, mix_weight[offset].astype(jnp.float32), precision=lax.Precision.HIGHEST)
        grads.append(jnp.einsum("thwc,thwd->cd", lagged, cotangent.astype(jnp.float32), precision=lax.Precision.HIGHEST))
    encoded = branch.astype(jnp.bfloat16)
    return encoded, jnp.stack(grads).reshape(-1)
```

```python
import jax
import jax.numpy as jnp
from jax import lax
from jax.sharding import PartitionSpec as P


def from_behind(block, axis, distance):
    devices = range(lax.axis_size(axis))
    route = [(i - distance, i) for i in devices if i - distance in devices]
    return lax.ppermute(block, axis, route)


def with_halo(cells, sides, width):
    for axis, dim in sides:
        count = lax.axis_size(axis)
        ends = count - 1
        head = lax.slice_in_dim(cells, 0, width, axis=dim)
        tail = lax.slice_in_dim(cells, cells.shape[dim] - width, cells.shape[dim], axis=dim)
        cells = jnp.concatenate(
            [
                lax.ppermute(tail, axis, [(i, (i + 1) % count) for i in range(ends)]),
                cells,
                lax.ppermute(head, axis, [((i + 1) % count, i) for i in range(ends)]),
            ],
            axis=dim,
        )
    return cells


def pool_pairs(hidden):
    shaped = hidden.reshape((hidden.shape[0] // 2, 2) + hidden.shape[1:]).astype(jnp.float32)
    return ((shaped[:, 0] + shaped[:, 1]) * 0.5).astype(jnp.bfloat16)


def delayed(block, offset):
    return jnp.pad(block, ((offset, 0), (0, 0), (0, 0), (0, 0)))[: block.shape[0]]


def local(frames, conv_weight, mix_weight, cotangent):
    full_conv, full_mix = (
        lax.all_gather(conv_weight, "fsdp", axis=4, tiled=True),
        lax.all_gather(mix_weight, "fsdp", axis=2, tiled=True),
    )
    count_frames, height, width, channels = frames.shape
    previous = from_behind(frames, "tm", 1)
    timed = jnp.concatenate([previous, frames], axis=0)
    padded = with_halo(timed, (("fsdp", 2),), 1)
    padded = jnp.pad(padded, ((0, 0), (1, 1), (0, 0), (0, 0)))
    accum = jnp.zeros((count_frames * height * width, channels), jnp.float32)
    for row_tap in range(3):
        for col_tap in range(3):
            stacked = jnp.concatenate(
                [
                    padded[
                        step : step + count_frames,
                        row_tap : row_tap + height,
                        col_tap : col_tap + width,
                        :,
                    ]
                    for step in range(3)
                ],
                axis=3,
            ).reshape(-1, 3 * channels)
            kernel = full_conv[:, row_tap, col_tap].reshape(3 * channels, channels)
            accum = accum + jnp.dot(stacked, kernel, preferred_element_type=jnp.float32)
    hidden = jax.nn.silu(accum).astype(jnp.bfloat16).reshape(count_frames, height, width, channels)
    pooled = lax.all_to_all(pool_pairs(hidden), "tm", split_axis=1, concat_axis=0, tiled=True)
    branch = pooled.astype(jnp.float32).reshape(-1, channels)
    flat_cot = cotangent.reshape(-1, channels)
    grad_terms = []
    for offset in range(3):
        lagged = delayed(pooled, offset).reshape(-1, channels)
        branch = branch + jnp.dot(lagged, full_mix[offset], preferred_element_type=jnp.float32)
        grad_terms.append(
            lax.dot_general(
                lagged, flat_cot, (((0,), (0,)), ((), ())), preferred_element_type=jnp.float32
            )
        )
    encoded = branch.astype(jnp.bfloat16).reshape(pooled.shape)
    parts = lax.axis_size("tm") * lax.axis_size("fsdp")
    mix_grad = lax.all_to_all(
        jnp.stack(grad_terms).reshape(parts, -1), ("tm", "fsdp"), 0, 0, tiled=True
    ).sum(0)
    return (encoded, mix_grad)


def solution(mesh):
    return jax.shard_map(
        local,
        mesh=mesh,
        in_specs=(
            P("tm", None, "fsdp", None),
            P(None, None, None, None, "fsdp"),
            P(None, None, "fsdp"),
            P(None, "tm", "fsdp", None),
        ),
        out_specs=(P(None, "tm", "fsdp", None), P(("tm", "fsdp"))),
        check_vma=False,
    )
```

```python
import jax
import jax.numpy as jnp
from jax import lax
from jax.sharding import PartitionSpec as P


def from_behind(block, axis, distance):
    devices = range(lax.axis_size(axis))
    route = [(i - distance, i) for i in devices if i - distance in devices]
    return lax.ppermute(block, axis, route)


def with_halo(cells, sides, width):
    for axis, dim in sides:
        count = lax.axis_size(axis)
        ends = count - 1
        head = lax.slice_in_dim(cells, 0, width, axis=dim)
        tail = lax.slice_in_dim(cells, cells.shape[dim] - width, cells.shape[dim], axis=dim)
        cells = jnp.concatenate(
            [
                lax.ppermute(tail, axis, [(i, (i + 1) % count) for i in range(ends)]),
                cells,
                lax.ppermute(head, axis, [((i + 1) % count, i) for i in range(ends)]),
            ],
            axis=dim,
        )
    return cells


def pool_pairs(hidden):
    shaped = hidden.reshape((hidden.shape[0] // 2, 2) + hidden.shape[1:]).astype(jnp.float32)
    return ((shaped[:, 0] + shaped[:, 1]) * 0.5).astype(jnp.bfloat16)


def delayed(block, offset):
    return jnp.pad(block, ((offset, 0), (0, 0), (0, 0), (0, 0)))[: block.shape[0]]


def local(frames, conv_weight, mix_weight, cotangent):
    channels_out = conv_weight.shape[-1]
    shards = jnp.concatenate(
        [conv_weight.reshape(-1, channels_out), mix_weight.reshape(-1, channels_out)], axis=0
    )
    gathered = lax.all_gather(shards, "fsdp", axis=0, tiled=False)
    gathered = jnp.transpose(gathered, (1, 0, 2)).reshape(shards.shape[0], -1)
    split = conv_weight.size // channels_out
    full_conv = gathered[:split].reshape(conv_weight.shape[:-1] + (-1,))
    full_mix = gathered[split:].reshape(mix_weight.shape[:-1] + (-1,))
    count_frames, height, width, channels = frames.shape
    previous = from_behind(frames, "tm", 1)
    timed = jnp.concatenate([previous, frames], axis=0)
    padded = with_halo(timed, (("fsdp", 2),), 1)
    padded = jnp.pad(padded, ((0, 0), (1, 1), (0, 0), (0, 0)))
    accum = jnp.zeros((count_frames * height * width, channels), jnp.float32)
    for row_tap in range(3):
        for col_tap in range(3):
            stacked = jnp.concatenate(
                [
                    padded[
                        step : step + count_frames,
                        row_tap : row_tap + height,
                        col_tap : col_tap + width,
                        :,
                    ]
                    for step in range(3)
                ],
                axis=3,
            ).reshape(-1, 3 * channels)
            kernel = full_conv[:, row_tap, col_tap].reshape(3 * channels, channels)
            accum = accum + jnp.dot(stacked, kernel, preferred_element_type=jnp.float32)
    hidden = jax.nn.silu(accum).astype(jnp.bfloat16).reshape(count_frames, height, width, channels)
    pooled = lax.all_to_all(pool_pairs(hidden), "tm", split_axis=1, concat_axis=0, tiled=True)
    branch = pooled.astype(jnp.float32).reshape(-1, channels)
    flat_cot = cotangent.reshape(-1, channels)
    grad_terms = []
    for offset in range(3):
        lagged = delayed(pooled, offset).reshape(-1, channels)
        branch = branch + jnp.dot(lagged, full_mix[offset], preferred_element_type=jnp.float32)
        grad_terms.append(
            lax.dot_general(
                lagged, flat_cot, (((0,), (0,)), ((), ())), preferred_element_type=jnp.float32
            )
        )
    encoded = branch.astype(jnp.bfloat16).reshape(pooled.shape)
    parts = lax.axis_size("tm") * lax.axis_size("fsdp")
    mix_grad = lax.all_to_all(
        jnp.stack(grad_terms).reshape(parts, -1), ("tm", "fsdp"), 0, 0, tiled=True
    ).sum(0)
    return (encoded, mix_grad)


def solution(mesh):
    return jax.shard_map(
        local,
        mesh=mesh,
        in_specs=(
            P("tm", None, "fsdp", None),
            P(None, None, None, None, "fsdp"),
            P(None, None, "fsdp"),
            P(None, "tm", "fsdp", None),
        ),
        out_specs=(P(None, "tm", "fsdp", None), P(("tm", "fsdp"))),
        check_vma=False,
    )
```

```python
import jax
import jax.numpy as jnp
from jax import lax
from jax.experimental import pallas as pl
from jax.experimental.pallas import tpu as pltpu
from jax.sharding import PartitionSpec as P

MESH = pl.DeviceIdType.MESH


def from_behind(block, axis, distance):
    devices = range(lax.axis_size(axis))
    route = [(i - distance, i) for i in devices if i - distance in devices]
    return lax.ppermute(block, axis, route)


def with_halo(cells, sides, width):
    for axis, dim in sides:
        count = lax.axis_size(axis)
        ends = count - 1
        head = lax.slice_in_dim(cells, 0, width, axis=dim)
        tail = lax.slice_in_dim(cells, cells.shape[dim] - width, cells.shape[dim], axis=dim)
        cells = jnp.concatenate(
            [
                lax.ppermute(tail, axis, [(i, (i + 1) % count) for i in range(ends)]),
                cells,
                lax.ppermute(head, axis, [((i + 1) % count, i) for i in range(ends)]),
            ],
            axis=dim,
        )
    return cells


def pool_pairs(hidden):
    shaped = hidden.reshape((hidden.shape[0] // 2, 2) + hidden.shape[1:]).astype(jnp.float32)
    return ((shaped[:, 0] + shaped[:, 1]) * 0.5).astype(jnp.bfloat16)


def delayed(block, offset):
    return jnp.pad(block, ((offset, 0), (0, 0), (0, 0), (0, 0)))[: block.shape[0]]


def exchange_kernel(x_ref, o_ref, send_sem, recv_sem, local_sem):
    count, rows = o_ref.shape[0], o_ref.shape[1]
    me = lax.axis_index("tm")
    barrier = pltpu.get_barrier_semaphore()
    for k in range(1, count):
        pl.semaphore_signal(
            barrier, inc=1, device_id={"tm": lax.rem(me + k, count)}, device_id_type=MESH
        )
    pl.semaphore_wait(barrier, count - 1)
    local = pltpu.make_async_copy(
        x_ref.at[0, pl.ds(me * rows, rows)], o_ref.at[me], local_sem
    )
    local.start()
    copies = []
    for k in range(1, count):
        peer = lax.rem(me + k, count)
        copy = pltpu.make_async_remote_copy(
            src_ref=x_ref.at[0, pl.ds(peer * rows, rows)],
            dst_ref=o_ref.at[me],
            send_sem=send_sem.at[k],
            recv_sem=recv_sem.at[k],
            device_id={"tm": peer},
            device_id_type=MESH,
        )
        copy.start()
        copies.append(copy)
    local.wait()
    for copy in copies:
        copy.wait()


def exchange_rows(block):
    count = lax.axis_size("tm")
    _, height, width, channels = block.shape
    return pl.pallas_call(
        exchange_kernel,
        out_shape=jax.ShapeDtypeStruct((count, height // count, width, channels), block.dtype),
        in_specs=[pl.BlockSpec(memory_space=pltpu.VMEM)],
        out_specs=pl.BlockSpec(memory_space=pltpu.VMEM),
        scratch_shapes=[
            pltpu.SemaphoreType.DMA((count,)),
            pltpu.SemaphoreType.DMA((count,)),
            pltpu.SemaphoreType.DMA,
        ],
        compiler_params=pltpu.CompilerParams(collective_id=0, has_side_effects=True),
    )(block)


def scatter_kernel(p_ref, o_ref, first, second, summed, s1, r1, s2, r2, l1, l2):
    groups, count = first.shape[0], second.shape[0]
    f, t = lax.axis_index("fsdp"), lax.axis_index("tm")
    barrier = pltpu.get_barrier_semaphore()
    for k in range(1, groups):
        pl.semaphore_signal(
            barrier, inc=1, device_id={"fsdp": lax.rem(f + k, groups)}, device_id_type=MESH
        )
    for k in range(1, count):
        pl.semaphore_signal(
            barrier, inc=1, device_id={"tm": lax.rem(t + k, count)}, device_id_type=MESH
        )
    pl.semaphore_wait(barrier, groups - 1 + count - 1)
    local = pltpu.make_async_copy(p_ref.at[f], first.at[f], l1)
    local.start()
    copies = []
    for k in range(1, groups):
        peer = lax.rem(f + k, groups)
        copy = pltpu.make_async_remote_copy(
            src_ref=p_ref.at[peer],
            dst_ref=first.at[f],
            send_sem=s1.at[k],
            recv_sem=r1.at[k],
            device_id={"fsdp": peer},
            device_id_type=MESH,
        )
        copy.start()
        copies.append(copy)
    local.wait()
    for copy in copies:
        copy.wait()
    summed[...] = jnp.sum(first[...], axis=0)
    local = pltpu.make_async_copy(summed.at[t], second.at[t], l2)
    local.start()
    copies = []
    for k in range(1, count):
        peer = lax.rem(t + k, count)
        copy = pltpu.make_async_remote_copy(
            src_ref=summed.at[peer],
            dst_ref=second.at[t],
            send_sem=s2.at[k],
            recv_sem=r2.at[k],
            device_id={"tm": peer},
            device_id_type=MESH,
        )
        copy.start()
        copies.append(copy)
    local.wait()
    for copy in copies:
        copy.wait()
    o_ref[...] = jnp.sum(second[...], axis=0)


def scatter_sum(partial):
    groups, count = lax.axis_size("fsdp"), lax.axis_size("tm")
    piece = partial.size // (groups * count)
    arranged = jnp.transpose(partial.reshape(count, groups, 1, piece), (1, 0, 2, 3))
    out = pl.pallas_call(
        scatter_kernel,
        out_shape=jax.ShapeDtypeStruct((1, piece), jnp.float32),
        in_specs=[pl.BlockSpec(memory_space=pltpu.VMEM)],
        out_specs=pl.BlockSpec(memory_space=pltpu.VMEM),
        scratch_shapes=[
            pltpu.VMEM((groups, count, 1, piece), jnp.float32),
            pltpu.VMEM((count, 1, piece), jnp.float32),
            pltpu.VMEM((count, 1, piece), jnp.float32),
            pltpu.SemaphoreType.DMA((groups,)),
            pltpu.SemaphoreType.DMA((groups,)),
            pltpu.SemaphoreType.DMA((count,)),
            pltpu.SemaphoreType.DMA((count,)),
            pltpu.SemaphoreType.DMA,
            pltpu.SemaphoreType.DMA,
        ],
        compiler_params=pltpu.CompilerParams(collective_id=1, has_side_effects=True),
    )(arranged)
    return out.reshape(piece)


def local(frames, conv_weight, mix_weight, cotangent):
    full_conv, full_mix = (
        lax.all_gather(conv_weight, "fsdp", axis=4, tiled=True),
        lax.all_gather(mix_weight, "fsdp", axis=2, tiled=True),
    )
    count_frames, height, width, channels = frames.shape
    previous = from_behind(frames, "tm", 1)
    timed = jnp.concatenate([previous, frames], axis=0)
    padded = with_halo(timed, (("fsdp", 2),), 1)
    padded = jnp.pad(padded, ((0, 0), (1, 1), (0, 0), (0, 0)))
    accum = jnp.zeros((count_frames * height * width, channels), jnp.float32)
    for row_tap in range(3):
        for col_tap in range(3):
            stacked = jnp.concatenate(
                [
                    padded[
                        step : step + count_frames,
                        row_tap : row_tap + height,
                        col_tap : col_tap + width,
                        :,
                    ]
                    for step in range(3)
                ],
                axis=3,
            ).reshape(-1, 3 * channels)
            kernel = full_conv[:, row_tap, col_tap].reshape(3 * channels, channels)
            accum = accum + jnp.dot(stacked, kernel, preferred_element_type=jnp.float32)
    hidden = jax.nn.silu(accum).astype(jnp.bfloat16).reshape(count_frames, height, width, channels)
    pooled = exchange_rows(pool_pairs(hidden))
    branch = pooled.astype(jnp.float32).reshape(-1, channels)
    flat_cot = cotangent.reshape(-1, channels)
    grad_terms = []
    for offset in range(3):
        lagged = delayed(pooled, offset).reshape(-1, channels)
        branch = branch + jnp.dot(lagged, full_mix[offset], preferred_element_type=jnp.float32)
        grad_terms.append(
            lax.dot_general(
                lagged, flat_cot, (((0,), (0,)), ((), ())), preferred_element_type=jnp.float32
            )
        )
    encoded = branch.astype(jnp.bfloat16).reshape(pooled.shape)
    mix_grad = scatter_sum(jnp.stack(grad_terms).reshape(-1))
    return (encoded, mix_grad)


def solution(mesh):
    return jax.shard_map(
        local,
        mesh=mesh,
        in_specs=(
            P("tm", None, "fsdp", None),
            P(None, None, None, None, "fsdp"),
            P(None, None, "fsdp"),
            P(None, "tm", "fsdp", None),
        ),
        out_specs=(P(None, "tm", "fsdp", None), P(("tm", "fsdp"))),
        check_vma=False,
    )
```

```python
import jax
import jax.numpy as jnp
from jax import lax
from jax.experimental import pallas as pl
from jax.experimental.pallas import tpu as pltpu
from jax.sharding import PartitionSpec as P

MESH = pl.DeviceIdType.MESH


def from_behind(block, axis, distance):
    devices = range(lax.axis_size(axis))
    route = [(i - distance, i) for i in devices if i - distance in devices]
    return lax.ppermute(block, axis, route)


def with_halo(cells, sides, width):
    for axis, dim in sides:
        count = lax.axis_size(axis)
        ends = count - 1
        head = lax.slice_in_dim(cells, 0, width, axis=dim)
        tail = lax.slice_in_dim(cells, cells.shape[dim] - width, cells.shape[dim], axis=dim)
        cells = jnp.concatenate(
            [
                lax.ppermute(tail, axis, [(i, (i + 1) % count) for i in range(ends)]),
                cells,
                lax.ppermute(head, axis, [((i + 1) % count, i) for i in range(ends)]),
            ],
            axis=dim,
        )
    return cells


def pool_pairs(hidden):
    shaped = hidden.reshape((hidden.shape[0] // 2, 2) + hidden.shape[1:]).astype(jnp.float32)
    return ((shaped[:, 0] + shaped[:, 1]) * 0.5).astype(jnp.bfloat16)


def delayed(block, offset):
    return jnp.pad(block, ((offset, 0), (0, 0), (0, 0), (0, 0)))[: block.shape[0]]


def exchange_kernel(x_ref, o_ref, send_sem, recv_sem, local_sem):
    count, rows = o_ref.shape[0], o_ref.shape[1]
    me = lax.axis_index("tm")
    barrier = pltpu.get_barrier_semaphore()
    for k in range(1, count):
        pl.semaphore_signal(
            barrier, inc=1, device_id={"tm": lax.rem(me + k, count)}, device_id_type=MESH
        )
    pl.semaphore_wait(barrier, count - 1)
    local = pltpu.make_async_copy(
        x_ref.at[0, pl.ds(me * rows, rows)], o_ref.at[me], local_sem
    )
    local.start()
    copies = []
    for k in range(1, count):
        peer = lax.rem(me + k, count)
        copy = pltpu.make_async_remote_copy(
            src_ref=x_ref.at[0, pl.ds(peer * rows, rows)],
            dst_ref=o_ref.at[me],
            send_sem=send_sem.at[k],
            recv_sem=recv_sem.at[k],
            device_id={"tm": peer},
            device_id_type=MESH,
        )
        copy.start()
        copies.append(copy)
    local.wait()
    for copy in copies:
        copy.wait()


def exchange_rows(block):
    count = lax.axis_size("tm")
    _, height, width, channels = block.shape
    return pl.pallas_call(
        exchange_kernel,
        out_shape=jax.ShapeDtypeStruct((count, height // count, width, channels), block.dtype),
        in_specs=[pl.BlockSpec(memory_space=pltpu.VMEM)],
        out_specs=pl.BlockSpec(memory_space=pltpu.VMEM),
        scratch_shapes=[
            pltpu.SemaphoreType.DMA((count,)),
            pltpu.SemaphoreType.DMA((count,)),
            pltpu.SemaphoreType.DMA,
        ],
        compiler_params=pltpu.CompilerParams(collective_id=0, has_side_effects=True),
    )(block)


def scatter_kernel(p_ref, o_ref, first, second, summed, s1, r1, s2, r2, l1, l2):
    groups, count = first.shape[0], second.shape[0]
    f, t = lax.axis_index("fsdp"), lax.axis_index("tm")
    barrier = pltpu.get_barrier_semaphore()
    for k in range(1, groups):
        pl.semaphore_signal(
            barrier, inc=1, device_id={"fsdp": lax.rem(f + k, groups)}, device_id_type=MESH
        )
    for k in range(1, count):
        pl.semaphore_signal(
            barrier, inc=1, device_id={"tm": lax.rem(t + k, count)}, device_id_type=MESH
        )
    pl.semaphore_wait(barrier, groups - 1 + count - 1)
    local = pltpu.make_async_copy(p_ref.at[f], first.at[f], l1)
    local.start()
    copies = []
    for k in range(1, groups):
        peer = lax.rem(f + k, groups)
        copy = pltpu.make_async_remote_copy(
            src_ref=p_ref.at[peer],
            dst_ref=first.at[f],
            send_sem=s1.at[k],
            recv_sem=r1.at[k],
            device_id={"fsdp": peer},
            device_id_type=MESH,
        )
        copy.start()
        copies.append(copy)
    local.wait()
    for copy in copies:
        copy.wait()
    summed[...] = jnp.sum(first[...], axis=0)
    local = pltpu.make_async_copy(summed.at[t], second.at[t], l2)
    local.start()
    copies = []
    for k in range(1, count):
        peer = lax.rem(t + k, count)
        copy = pltpu.make_async_remote_copy(
            src_ref=summed.at[peer],
            dst_ref=second.at[t],
            send_sem=s2.at[k],
            recv_sem=r2.at[k],
            device_id={"tm": peer},
            device_id_type=MESH,
        )
        copy.start()
        copies.append(copy)
    local.wait()
    for copy in copies:
        copy.wait()
    o_ref[...] = jnp.sum(second[...], axis=0)


def scatter_sum(partial):
    groups, count = lax.axis_size("fsdp"), lax.axis_size("tm")
    piece = partial.size // (groups * count)
    arranged = jnp.transpose(partial.reshape(count, groups, 1, piece), (1, 0, 2, 3))
    out = pl.pallas_call(
        scatter_kernel,
        out_shape=jax.ShapeDtypeStruct((1, piece), jnp.float32),
        in_specs=[pl.BlockSpec(memory_space=pltpu.VMEM)],
        out_specs=pl.BlockSpec(memory_space=pltpu.VMEM),
        scratch_shapes=[
            pltpu.VMEM((groups, count, 1, piece), jnp.float32),
            pltpu.VMEM((count, 1, piece), jnp.float32),
            pltpu.VMEM((count, 1, piece), jnp.float32),
            pltpu.SemaphoreType.DMA((groups,)),
            pltpu.SemaphoreType.DMA((groups,)),
            pltpu.SemaphoreType.DMA((count,)),
            pltpu.SemaphoreType.DMA((count,)),
            pltpu.SemaphoreType.DMA,
            pltpu.SemaphoreType.DMA,
        ],
        compiler_params=pltpu.CompilerParams(collective_id=1, has_side_effects=True),
    )(arranged)
    return out.reshape(piece)


def prologue_kernel(x_ref, lcol_ref, rcol_ref, w_ref, halo_ref, left_ref, right_ref, wall_ref, sends, recvs, wsends, wrecvs, local_sem):
    count, groups = lax.axis_size("tm"), lax.axis_size("fsdp")
    t, f = lax.axis_index("tm"), lax.axis_index("fsdp")
    t_next, t_prev = lax.rem(t + 1, count), lax.rem(t + count - 1, count)
    f_next, f_prev = lax.rem(f + 1, groups), lax.rem(f + groups - 1, groups)
    peers = [(t_next, f), (t_prev, f)]
    peers += [(t, lax.rem(f + k, groups)) for k in range(1, groups)]
    peers += [(a, b) for a in (t_next, t_prev) for b in (f_next, f_prev)]
    barrier = pltpu.get_barrier_semaphore()
    for a, b in peers:
        pl.semaphore_signal(barrier, inc=1, device_id=(a, b), device_id_type=MESH)
    pl.semaphore_wait(barrier, len(peers))
    depth = x_ref.shape[0]
    plan = [
        (x_ref, halo_ref, (t_next, f)),
        (rcol_ref, left_ref.at[pl.ds(depth, depth)], (t, f_next)),
        (rcol_ref, left_ref.at[pl.ds(0, depth)], (t_next, f_next)),
        (lcol_ref, right_ref.at[pl.ds(depth, depth)], (t, f_prev)),
        (lcol_ref, right_ref.at[pl.ds(0, depth)], (t_next, f_prev)),
    ]
    copies = []
    for i, (src, dst, dev) in enumerate(plan):
        copy = pltpu.make_async_remote_copy(
            src_ref=src, dst_ref=dst, send_sem=sends.at[i], recv_sem=recvs.at[i],
            device_id=dev, device_id_type=MESH,
        )
        copy.start()
        copies.append(copy)
    local = pltpu.make_async_copy(w_ref, wall_ref.at[f], local_sem)
    local.start()
    for k in range(1, groups):
        copy = pltpu.make_async_remote_copy(
            src_ref=w_ref, dst_ref=wall_ref.at[f], send_sem=wsends.at[k], recv_sem=wrecvs.at[k],
            device_id=(t, lax.rem(f + k, groups)), device_id_type=MESH,
        )
        copy.start()
        copies.append(copy)
    local.wait()
    for copy in copies:
        copy.wait()


def prologue(frames, shard):
    groups = lax.axis_size("fsdp")
    depth, height, width, channels = frames.shape
    lcol = frames[:, :, 0, :]
    rcol = frames[:, :, width - 1, :]
    edge = jax.ShapeDtypeStruct((2 * depth, height, channels), frames.dtype)
    vmem = pl.BlockSpec(memory_space=pltpu.VMEM)
    return pl.pallas_call(
        prologue_kernel,
        out_shape=(
            jax.ShapeDtypeStruct(frames.shape, frames.dtype),
            edge,
            edge,
            jax.ShapeDtypeStruct((groups,) + shard.shape, shard.dtype),
        ),
        in_specs=[vmem] * 4,
        out_specs=(vmem,) * 4,
        scratch_shapes=[
            pltpu.SemaphoreType.DMA((5,)),
            pltpu.SemaphoreType.DMA((5,)),
            pltpu.SemaphoreType.DMA((groups,)),
            pltpu.SemaphoreType.DMA((groups,)),
            pltpu.SemaphoreType.DMA,
        ],
        compiler_params=pltpu.CompilerParams(collective_id=2, has_side_effects=True),
    )(frames, lcol, rcol, shard)


def local(frames, conv_weight, mix_weight, cotangent):
    groups = lax.axis_size("fsdp")
    t, f = lax.axis_index("tm"), lax.axis_index("fsdp")
    part = conv_weight.shape[-1]
    shard = jnp.concatenate(
        [conv_weight.reshape(-1, part), mix_weight.reshape(-1, part)], axis=0
    ).reshape(-1, 128)
    halo, left, right, wall = prologue(frames, shard)
    wall = wall.reshape(groups, -1, part)
    wall = jnp.transpose(wall, (1, 0, 2)).reshape(wall.shape[1], groups * part)
    split = conv_weight.size // part
    full_conv = wall[:split].reshape(conv_weight.shape[:-1] + (-1,))
    full_mix = wall[split:].reshape(mix_weight.shape[:-1] + (-1,))
    count_frames, height, width, channels = frames.shape
    zero = jnp.zeros((), frames.dtype)
    halo = jnp.where(t > 0, halo, zero)
    timed = jnp.concatenate([halo, frames], axis=0)
    first = jnp.arange(2 * count_frames)[:, None, None] >= count_frames
    left = jnp.where((f > 0) & ((t > 0) | first), left, zero)
    right = jnp.where((f < groups - 1) & ((t > 0) | first), right, zero)
    padded = jnp.concatenate([left[:, :, None], timed, right[:, :, None]], axis=2)
    padded = jnp.pad(padded, ((0, 0), (1, 1), (0, 0), (0, 0)))
    accum = jnp.zeros((count_frames * height * width, channels), jnp.float32)
    for row_tap in range(3):
        for col_tap in range(3):
            stacked = jnp.concatenate(
                [
                    padded[
                        step : step + count_frames,
                        row_tap : row_tap + height,
                        col_tap : col_tap + width,
                        :,
                    ]
                    for step in range(3)
                ],
                axis=3,
            ).reshape(-1, 3 * channels)
            kernel = full_conv[:, row_tap, col_tap].reshape(3 * channels, channels)
            accum = accum + jnp.dot(stacked, kernel, preferred_element_type=jnp.float32)
    hidden = jax.nn.silu(accum).astype(jnp.bfloat16).reshape(count_frames, height, width, channels)
    pooled = exchange_rows(pool_pairs(hidden))
    branch = pooled.astype(jnp.float32).reshape(-1, channels)
    flat_cot = cotangent.reshape(-1, channels)
    grad_terms = []
    for offset in range(3):
        lagged = delayed(pooled, offset).reshape(-1, channels)
        branch = branch + jnp.dot(lagged, full_mix[offset], preferred_element_type=jnp.float32)
        grad_terms.append(
            lax.dot_general(
                lagged, flat_cot, (((0,), (0,)), ((), ())), preferred_element_type=jnp.float32
            )
        )
    encoded = branch.astype(jnp.bfloat16).reshape(pooled.shape)
    mix_grad = scatter_sum(jnp.stack(grad_terms).reshape(-1))
    return (encoded, mix_grad)


def solution(mesh):
    return jax.shard_map(
        local,
        mesh=mesh,
        in_specs=(
            P("tm", None, "fsdp", None),
            P(None, None, None, None, "fsdp"),
            P(None, None, "fsdp"),
            P(None, "tm", "fsdp", None),
        ),
        out_specs=(P(None, "tm", "fsdp", None), P(("tm", "fsdp"))),
        check_vma=False,
    )
```

```python
import jax
import jax.numpy as jnp
from jax import lax
from jax.experimental import pallas as pl
from jax.experimental.pallas import tpu as pltpu
from jax.sharding import PartitionSpec as P

MESH = pl.DeviceIdType.MESH


def from_behind(block, axis, distance):
    devices = range(lax.axis_size(axis))
    route = [(i - distance, i) for i in devices if i - distance in devices]
    return lax.ppermute(block, axis, route)


def with_halo(cells, sides, width):
    for axis, dim in sides:
        count = lax.axis_size(axis)
        ends = count - 1
        head = lax.slice_in_dim(cells, 0, width, axis=dim)
        tail = lax.slice_in_dim(cells, cells.shape[dim] - width, cells.shape[dim], axis=dim)
        cells = jnp.concatenate(
            [
                lax.ppermute(tail, axis, [(i, (i + 1) % count) for i in range(ends)]),
                cells,
                lax.ppermute(head, axis, [((i + 1) % count, i) for i in range(ends)]),
            ],
            axis=dim,
        )
    return cells


def pool_pairs(hidden):
    shaped = hidden.reshape((hidden.shape[0] // 2, 2) + hidden.shape[1:]).astype(jnp.float32)
    return ((shaped[:, 0] + shaped[:, 1]) * 0.5).astype(jnp.bfloat16)


def delayed(block, offset):
    return jnp.pad(block, ((offset, 0), (0, 0), (0, 0), (0, 0)))[: block.shape[0]]


def scatter_kernel(p_ref, o_ref, first, second, summed, s1, r1, s2, r2, l1, l2):
    groups, count = first.shape[0], second.shape[0]
    f, t = lax.axis_index("fsdp"), lax.axis_index("tm")
    barrier = pltpu.get_barrier_semaphore()
    for k in range(1, groups):
        pl.semaphore_signal(
            barrier, inc=1, device_id={"fsdp": lax.rem(f + k, groups)}, device_id_type=MESH
        )
    for k in range(1, count):
        pl.semaphore_signal(
            barrier, inc=1, device_id={"tm": lax.rem(t + k, count)}, device_id_type=MESH
        )
    pl.semaphore_wait(barrier, groups - 1 + count - 1)
    local = pltpu.make_async_copy(p_ref.at[f], first.at[f], l1)
    local.start()
    copies = []
    for k in range(1, groups):
        peer = lax.rem(f + k, groups)
        copy = pltpu.make_async_remote_copy(
            src_ref=p_ref.at[peer],
            dst_ref=first.at[f],
            send_sem=s1.at[k],
            recv_sem=r1.at[k],
            device_id={"fsdp": peer},
            device_id_type=MESH,
        )
        copy.start()
        copies.append(copy)
    local.wait()
    for copy in copies:
        copy.wait()
    summed[...] = jnp.sum(first[...], axis=0)
    local = pltpu.make_async_copy(summed.at[t], second.at[t], l2)
    local.start()
    copies = []
    for k in range(1, count):
        peer = lax.rem(t + k, count)
        copy = pltpu.make_async_remote_copy(
            src_ref=summed.at[peer],
            dst_ref=second.at[t],
            send_sem=s2.at[k],
            recv_sem=r2.at[k],
            device_id={"tm": peer},
            device_id_type=MESH,
        )
        copy.start()
        copies.append(copy)
    local.wait()
    for copy in copies:
        copy.wait()
    o_ref[...] = jnp.sum(second[...], axis=0)


def scatter_sum(partial):
    groups, count = lax.axis_size("fsdp"), lax.axis_size("tm")
    piece = partial.size // (groups * count)
    arranged = jnp.transpose(partial.reshape(count, groups, 1, piece), (1, 0, 2, 3))
    out = pl.pallas_call(
        scatter_kernel,
        out_shape=jax.ShapeDtypeStruct((1, piece), jnp.float32),
        in_specs=[pl.BlockSpec(memory_space=pltpu.VMEM)],
        out_specs=pl.BlockSpec(memory_space=pltpu.VMEM),
        scratch_shapes=[
            pltpu.VMEM((groups, count, 1, piece), jnp.float32),
            pltpu.VMEM((count, 1, piece), jnp.float32),
            pltpu.VMEM((count, 1, piece), jnp.float32),
            pltpu.SemaphoreType.DMA((groups,)),
            pltpu.SemaphoreType.DMA((groups,)),
            pltpu.SemaphoreType.DMA((count,)),
            pltpu.SemaphoreType.DMA((count,)),
            pltpu.SemaphoreType.DMA,
            pltpu.SemaphoreType.DMA,
        ],
        compiler_params=pltpu.CompilerParams(collective_id=1, has_side_effects=True),
    )(arranged)
    return out.reshape(piece)


def local(frames, conv_weight, mix_weight, cotangent):
    full_conv, full_mix = (
        lax.all_gather(conv_weight, "fsdp", axis=4, tiled=True),
        lax.all_gather(mix_weight, "fsdp", axis=2, tiled=True),
    )
    count_frames, height, width, channels = frames.shape
    previous = from_behind(frames, "tm", 1)
    timed = jnp.concatenate([previous, frames], axis=0)
    padded = with_halo(timed, (("fsdp", 2),), 1)
    padded = jnp.pad(padded, ((0, 0), (1, 1), (0, 0), (0, 0)))
    accum = jnp.zeros((count_frames * height * width, channels), jnp.float32)
    for row_tap in range(3):
        for col_tap in range(3):
            stacked = jnp.concatenate(
                [
                    padded[
                        step : step + count_frames,
                        row_tap : row_tap + height,
                        col_tap : col_tap + width,
                        :,
                    ]
                    for step in range(3)
                ],
                axis=3,
            ).reshape(-1, 3 * channels)
            kernel = full_conv[:, row_tap, col_tap].reshape(3 * channels, channels)
            accum = accum + jnp.dot(stacked, kernel, preferred_element_type=jnp.float32)
    hidden = jax.nn.silu(accum).astype(jnp.bfloat16).reshape(count_frames, height, width, channels)
    pooled = lax.all_to_all(pool_pairs(hidden), "tm", split_axis=1, concat_axis=0, tiled=True)
    branch = pooled.astype(jnp.float32).reshape(-1, channels)
    flat_cot = cotangent.reshape(-1, channels)
    grad_terms = []
    for offset in range(3):
        lagged = delayed(pooled, offset).reshape(-1, channels)
        branch = branch + jnp.dot(lagged, full_mix[offset], preferred_element_type=jnp.float32)
        grad_terms.append(
            lax.dot_general(
                lagged, flat_cot, (((0,), (0,)), ((), ())), preferred_element_type=jnp.float32
            )
        )
    encoded = branch.astype(jnp.bfloat16).reshape(pooled.shape)
    mix_grad = scatter_sum(jnp.stack(grad_terms).reshape(-1))
    return (encoded, mix_grad)


def solution(mesh):
    return jax.shard_map(
        local,
        mesh=mesh,
        in_specs=(
            P("tm", None, "fsdp", None),
            P(None, None, None, None, "fsdp"),
            P(None, None, "fsdp"),
            P(None, "tm", "fsdp", None),
        ),
        out_specs=(P(None, "tm", "fsdp", None), P(("tm", "fsdp"))),
        check_vma=False,
    )
```

```python
import jax
import jax.numpy as jnp
from jax import lax
from jax.experimental import pallas as pl
from jax.experimental.pallas import tpu as pltpu
from jax.sharding import PartitionSpec as P

MESH = pl.DeviceIdType.MESH


def from_behind(block, axis, distance):
    devices = range(lax.axis_size(axis))
    route = [(i - distance, i) for i in devices if i - distance in devices]
    return lax.ppermute(block, axis, route)


def with_halo(cells, sides, width):
    for axis, dim in sides:
        count = lax.axis_size(axis)
        ends = count - 1
        head = lax.slice_in_dim(cells, 0, width, axis=dim)
        tail = lax.slice_in_dim(cells, cells.shape[dim] - width, cells.shape[dim], axis=dim)
        cells = jnp.concatenate(
            [
                lax.ppermute(tail, axis, [(i, (i + 1) % count) for i in range(ends)]),
                cells,
                lax.ppermute(head, axis, [((i + 1) % count, i) for i in range(ends)]),
            ],
            axis=dim,
        )
    return cells


def pool_pairs(hidden):
    shaped = hidden.reshape((hidden.shape[0] // 2, 2) + hidden.shape[1:]).astype(jnp.float32)
    return ((shaped[:, 0] + shaped[:, 1]) * 0.5).astype(jnp.bfloat16)


def delayed(block, offset):
    return jnp.pad(block, ((offset, 0), (0, 0), (0, 0), (0, 0)))[: block.shape[0]]


def scatter_kernel(p_ref, o_ref, first, second, summed, s1, r1, s2, r2, l1, l2):
    groups, count = first.shape[0], second.shape[0]
    f, t = lax.axis_index("fsdp"), lax.axis_index("tm")
    barrier = pltpu.get_barrier_semaphore()
    for k in range(1, groups):
        pl.semaphore_signal(
            barrier, inc=1, device_id={"fsdp": lax.rem(f + k, groups)}, device_id_type=MESH
        )
    for k in range(1, count):
        pl.semaphore_signal(
            barrier, inc=1, device_id={"tm": lax.rem(t + k, count)}, device_id_type=MESH
        )
    pl.semaphore_wait(barrier, groups - 1 + count - 1)
    local = pltpu.make_async_copy(p_ref.at[f], first.at[f], l1)
    local.start()
    copies = []
    for k in range(1, groups):
        peer = lax.rem(f + k, groups)
        copy = pltpu.make_async_remote_copy(
            src_ref=p_ref.at[peer],
            dst_ref=first.at[f],
            send_sem=s1.at[k],
            recv_sem=r1.at[k],
            device_id={"fsdp": peer},
            device_id_type=MESH,
        )
        copy.start()
        copies.append(copy)
    local.wait()
    for copy in copies:
        copy.wait()
    summed[...] = jnp.sum(first[...], axis=0)
    local = pltpu.make_async_copy(summed.at[t], second.at[t], l2)
    local.start()
    copies = []
    for k in range(1, count):
        peer = lax.rem(t + k, count)
        copy = pltpu.make_async_remote_copy(
            src_ref=summed.at[peer],
            dst_ref=second.at[t],
            send_sem=s2.at[k],
            recv_sem=r2.at[k],
            device_id={"tm": peer},
            device_id_type=MESH,
        )
        copy.start()
        copies.append(copy)
    local.wait()
    for copy in copies:
        copy.wait()
    o_ref[...] = jnp.sum(second[...], axis=0)


def scatter_sum(partial):
    groups, count = lax.axis_size("fsdp"), lax.axis_size("tm")
    piece = partial.size // (groups * count)
    arranged = jnp.transpose(partial.reshape(count, groups, 1, piece), (1, 0, 2, 3))
    out = pl.pallas_call(
        scatter_kernel,
        out_shape=jax.ShapeDtypeStruct((1, piece), jnp.float32),
        in_specs=[pl.BlockSpec(memory_space=pltpu.VMEM)],
        out_specs=pl.BlockSpec(memory_space=pltpu.VMEM),
        scratch_shapes=[
            pltpu.VMEM((groups, count, 1, piece), jnp.float32),
            pltpu.VMEM((count, 1, piece), jnp.float32),
            pltpu.VMEM((count, 1, piece), jnp.float32),
            pltpu.SemaphoreType.DMA((groups,)),
            pltpu.SemaphoreType.DMA((groups,)),
            pltpu.SemaphoreType.DMA((count,)),
            pltpu.SemaphoreType.DMA((count,)),
            pltpu.SemaphoreType.DMA,
            pltpu.SemaphoreType.DMA,
        ],
        compiler_params=pltpu.CompilerParams(collective_id=1, has_side_effects=True),
    )(arranged)
    return out.reshape(piece)


def conv_pool_kernel(xs_ref, w_ref, o_ref):
    height, width, channels = o_ref.shape
    rows = 8

    def body(r, carry):
        top = pl.multiple_of(r * rows, rows)
        hidden = []
        for j in range(2):
            acc = jnp.zeros((rows * width, channels), jnp.float32)
            for b in range(3):
                for c in range(3):
                    taps = [xs_ref[c, j + a, pl.ds(top + b, rows)] for a in range(3)]
                    lhs = jnp.concatenate(taps, axis=-1).reshape(rows * width, 3 * channels)
                    acc = acc + jnp.dot(lhs, w_ref[b * 3 + c], preferred_element_type=jnp.float32)
            silu = acc / (1.0 + jnp.exp(-acc))
            hidden.append(silu.astype(jnp.bfloat16).astype(jnp.float32))
        pooled = ((hidden[0] + hidden[1]) * 0.5).astype(o_ref.dtype)
        o_ref[pl.ds(top, rows)] = pooled.reshape(rows, width, channels)
        return carry

    lax.fori_loop(0, height // rows, body, 0)


def conv_pool(shifted, weights):
    _, _, rows, width, channels = shifted.shape
    height = rows - 2
    vmem = pl.BlockSpec(memory_space=pltpu.VMEM)
    flops = 2 * 2 * height * width * weights.shape[0] * weights.shape[1] * channels
    return pl.pallas_call(
        conv_pool_kernel,
        out_shape=jax.ShapeDtypeStruct((height, width, channels), jnp.bfloat16),
        in_specs=[vmem, vmem],
        out_specs=vmem,
        cost_estimate=pl.CostEstimate(
            flops=flops,
            transcendentals=2 * height * width * channels,
            bytes_accessed=shifted.size * 2 + weights.size * 2 + height * width * channels * 2,
        ),
    )(shifted, weights)


def local(frames, conv_weight, mix_weight, cotangent):
    full_conv, full_mix = (
        lax.all_gather(conv_weight, "fsdp", axis=4, tiled=True),
        lax.all_gather(mix_weight, "fsdp", axis=2, tiled=True),
    )
    count_frames, height, width, channels = frames.shape
    previous = from_behind(frames, "tm", 1)
    timed = jnp.concatenate([previous, frames], axis=0)
    padded = with_halo(timed, (("fsdp", 2),), 1)
    padded = jnp.pad(padded, ((0, 0), (1, 1), (0, 0), (0, 0)))
    shifted = jnp.stack([padded[:, :, c : c + width] for c in range(3)])
    weights = jnp.transpose(full_conv, (1, 2, 0, 3, 4)).reshape(9, 3 * channels, -1)
    pooled = conv_pool(shifted, weights)[None]
    pooled = lax.all_to_all(pooled, "tm", split_axis=1, concat_axis=0, tiled=True)
    branch = pooled.astype(jnp.float32).reshape(-1, channels)
    flat_cot = cotangent.reshape(-1, channels)
    grad_terms = []
    for offset in range(3):
        lagged = delayed(pooled, offset).reshape(-1, channels)
        branch = branch + jnp.dot(lagged, full_mix[offset], preferred_element_type=jnp.float32)
        grad_terms.append(
            lax.dot_general(
                lagged, flat_cot, (((0,), (0,)), ((), ())), preferred_element_type=jnp.float32
            )
        )
    encoded = branch.astype(jnp.bfloat16).reshape(pooled.shape)
    mix_grad = scatter_sum(jnp.stack(grad_terms).reshape(-1))
    return (encoded, mix_grad)


def solution(mesh):
    return jax.shard_map(
        local,
        mesh=mesh,
        in_specs=(
            P("tm", None, "fsdp", None),
            P(None, None, None, None, "fsdp"),
            P(None, None, "fsdp"),
            P(None, "tm", "fsdp", None),
        ),
        out_specs=(P(None, "tm", "fsdp", None), P(("tm", "fsdp"))),
        check_vma=False,
    )
```

```python
import jax
import jax.numpy as jnp
from jax import lax
from jax.experimental import pallas as pl
from jax.experimental.pallas import tpu as pltpu
from jax.sharding import PartitionSpec as P

MESH = pl.DeviceIdType.MESH


def from_behind(block, axis, distance):
    devices = range(lax.axis_size(axis))
    route = [(i - distance, i) for i in devices if i - distance in devices]
    return lax.ppermute(block, axis, route)


def with_halo(cells, sides, width):
    for axis, dim in sides:
        count = lax.axis_size(axis)
        ends = count - 1
        head = lax.slice_in_dim(cells, 0, width, axis=dim)
        tail = lax.slice_in_dim(cells, cells.shape[dim] - width, cells.shape[dim], axis=dim)
        cells = jnp.concatenate(
            [
                lax.ppermute(tail, axis, [(i, (i + 1) % count) for i in range(ends)]),
                cells,
                lax.ppermute(head, axis, [((i + 1) % count, i) for i in range(ends)]),
            ],
            axis=dim,
        )
    return cells


def pool_pairs(hidden):
    shaped = hidden.reshape((hidden.shape[0] // 2, 2) + hidden.shape[1:]).astype(jnp.float32)
    return ((shaped[:, 0] + shaped[:, 1]) * 0.5).astype(jnp.bfloat16)


def delayed(block, offset):
    return jnp.pad(block, ((offset, 0), (0, 0), (0, 0), (0, 0)))[: block.shape[0]]


def scatter_kernel(p_ref, o_ref, first, second, summed, s1, r1, s2, r2, l1, l2):
    groups, count = first.shape[0], second.shape[0]
    f, t = lax.axis_index("fsdp"), lax.axis_index("tm")
    barrier = pltpu.get_barrier_semaphore()
    for k in range(1, groups):
        pl.semaphore_signal(
            barrier, inc=1, device_id={"fsdp": lax.rem(f + k, groups)}, device_id_type=MESH
        )
    for k in range(1, count):
        pl.semaphore_signal(
            barrier, inc=1, device_id={"tm": lax.rem(t + k, count)}, device_id_type=MESH
        )
    pl.semaphore_wait(barrier, groups - 1 + count - 1)
    local = pltpu.make_async_copy(p_ref.at[f], first.at[f], l1)
    local.start()
    copies = []
    for k in range(1, groups):
        peer = lax.rem(f + k, groups)
        copy = pltpu.make_async_remote_copy(
            src_ref=p_ref.at[peer],
            dst_ref=first.at[f],
            send_sem=s1.at[k],
            recv_sem=r1.at[k],
            device_id={"fsdp": peer},
            device_id_type=MESH,
        )
        copy.start()
        copies.append(copy)
    local.wait()
    for copy in copies:
        copy.wait()
    summed[...] = jnp.sum(first[...], axis=0)
    local = pltpu.make_async_copy(summed.at[t], second.at[t], l2)
    local.start()
    copies = []
    for k in range(1, count):
        peer = lax.rem(t + k, count)
        copy = pltpu.make_async_remote_copy(
            src_ref=summed.at[peer],
            dst_ref=second.at[t],
            send_sem=s2.at[k],
            recv_sem=r2.at[k],
            device_id={"tm": peer},
            device_id_type=MESH,
        )
        copy.start()
        copies.append(copy)
    local.wait()
    for copy in copies:
        copy.wait()
    o_ref[...] = jnp.sum(second[...], axis=0)


def scatter_sum(partial):
    groups, count = lax.axis_size("fsdp"), lax.axis_size("tm")
    piece = partial.size // (groups * count)
    arranged = jnp.transpose(partial.reshape(count, groups, 1, piece), (1, 0, 2, 3))
    out = pl.pallas_call(
        scatter_kernel,
        out_shape=jax.ShapeDtypeStruct((1, piece), jnp.float32),
        in_specs=[pl.BlockSpec(memory_space=pltpu.VMEM)],
        out_specs=pl.BlockSpec(memory_space=pltpu.VMEM),
        scratch_shapes=[
            pltpu.VMEM((groups, count, 1, piece), jnp.float32),
            pltpu.VMEM((count, 1, piece), jnp.float32),
            pltpu.VMEM((count, 1, piece), jnp.float32),
            pltpu.SemaphoreType.DMA((groups,)),
            pltpu.SemaphoreType.DMA((groups,)),
            pltpu.SemaphoreType.DMA((count,)),
            pltpu.SemaphoreType.DMA((count,)),
            pltpu.SemaphoreType.DMA,
            pltpu.SemaphoreType.DMA,
        ],
        compiler_params=pltpu.CompilerParams(collective_id=1, has_side_effects=True),
    )(arranged)
    return out.reshape(piece)


def conv_pool_kernel(xs_ref, w_ref, o_ref):
    height, width, channels = o_ref.shape
    rows = 8

    def body(r, carry):
        top = pl.multiple_of(r * rows, rows)
        hidden = []
        for j in range(2):
            acc = jnp.zeros((rows * width, channels), jnp.float32)
            for b in range(3):
                for c in range(3):
                    taps = [xs_ref[c, j + a, pl.ds(top + b, rows)] for a in range(3)]
                    lhs = jnp.concatenate(taps, axis=-1).reshape(rows * width, 3 * channels)
                    acc = acc + jnp.dot(lhs, w_ref[b * 3 + c], preferred_element_type=jnp.float32)
            silu = acc / (1.0 + jnp.exp(-acc))
            hidden.append(silu.astype(jnp.bfloat16).astype(jnp.float32))
        pooled = ((hidden[0] + hidden[1]) * 0.5).astype(o_ref.dtype)
        o_ref[pl.ds(top, rows)] = pooled.reshape(rows, width, channels)
        return carry

    lax.fori_loop(0, height // rows, body, 0)


def conv_pool(shifted, weights):
    _, _, rows, width, channels = shifted.shape
    height = rows - 2
    vmem = pl.BlockSpec(memory_space=pltpu.VMEM)
    flops = 2 * 2 * height * width * weights.shape[0] * weights.shape[1] * channels
    return pl.pallas_call(
        conv_pool_kernel,
        out_shape=jax.ShapeDtypeStruct((height, width, channels), jnp.bfloat16),
        in_specs=[vmem, vmem],
        out_specs=vmem,
        cost_estimate=pl.CostEstimate(
            flops=flops,
            transcendentals=2 * height * width * channels,
            bytes_accessed=shifted.size * 2 + weights.size * 2 + height * width * channels * 2,
        ),
    )(shifted, weights)


def local(frames, conv_weight, mix_weight, cotangent):
    groups = lax.axis_size("fsdp")
    f = lax.axis_index("fsdp")
    shards = [conv_weight] + [
        lax.ppermute(conv_weight, "fsdp", [((g + k) % groups, g) for g in range(groups)])
        for k in range(1, groups)
    ]
    stacked = jnp.stack(shards)
    order = lax.rem(jnp.arange(groups) - f + groups, groups)
    full_conv = jnp.concatenate([stacked[order[g]] for g in range(groups)], axis=-1)
    full_mix = lax.all_gather(mix_weight, "fsdp", axis=2, tiled=True)
    count_frames, height, width, channels = frames.shape
    previous = from_behind(frames, "tm", 1)
    timed = jnp.concatenate([previous, frames], axis=0)
    padded = with_halo(timed, (("fsdp", 2),), 1)
    padded = jnp.pad(padded, ((0, 0), (1, 1), (0, 0), (0, 0)))
    shifted = jnp.stack([padded[:, :, c : c + width] for c in range(3)])
    weights = jnp.transpose(full_conv, (1, 2, 0, 3, 4)).reshape(9, 3 * channels, -1)
    pooled = conv_pool(shifted, weights)[None]
    pooled = lax.all_to_all(pooled, "tm", split_axis=1, concat_axis=0, tiled=True)
    branch = pooled.astype(jnp.float32).reshape(-1, channels)
    flat_cot = cotangent.reshape(-1, channels)
    grad_terms = []
    for offset in range(3):
        lagged = delayed(pooled, offset).reshape(-1, channels)
        branch = branch + jnp.dot(lagged, full_mix[offset], preferred_element_type=jnp.float32)
        grad_terms.append(
            lax.dot_general(
                lagged, flat_cot, (((0,), (0,)), ((), ())), preferred_element_type=jnp.float32
            )
        )
    encoded = branch.astype(jnp.bfloat16).reshape(pooled.shape)
    mix_grad = scatter_sum(jnp.stack(grad_terms).reshape(-1))
    return (encoded, mix_grad)


def solution(mesh):
    return jax.shard_map(
        local,
        mesh=mesh,
        in_specs=(
            P("tm", None, "fsdp", None),
            P(None, None, None, None, "fsdp"),
            P(None, None, "fsdp"),
            P(None, "tm", "fsdp", None),
        ),
        out_specs=(P(None, "tm", "fsdp", None), P(("tm", "fsdp"))),
        check_vma=False,
    )
```

```python
import jax
import jax.numpy as jnp
from jax import lax
from jax.experimental import pallas as pl
from jax.experimental.pallas import tpu as pltpu
from jax.sharding import PartitionSpec as P

MESH = pl.DeviceIdType.MESH


def from_behind(block, axis, distance):
    devices = range(lax.axis_size(axis))
    route = [(i - distance, i) for i in devices if i - distance in devices]
    return lax.ppermute(block, axis, route)


def with_halo(cells, sides, width):
    for axis, dim in sides:
        count = lax.axis_size(axis)
        ends = count - 1
        head = lax.slice_in_dim(cells, 0, width, axis=dim)
        tail = lax.slice_in_dim(cells, cells.shape[dim] - width, cells.shape[dim], axis=dim)
        cells = jnp.concatenate(
            [
                lax.ppermute(tail, axis, [(i, (i + 1) % count) for i in range(ends)]),
                cells,
                lax.ppermute(head, axis, [((i + 1) % count, i) for i in range(ends)]),
            ],
            axis=dim,
        )
    return cells


def pool_pairs(hidden):
    shaped = hidden.reshape((hidden.shape[0] // 2, 2) + hidden.shape[1:]).astype(jnp.float32)
    return ((shaped[:, 0] + shaped[:, 1]) * 0.5).astype(jnp.bfloat16)


def delayed(block, offset):
    return jnp.pad(block, ((offset, 0), (0, 0), (0, 0), (0, 0)))[: block.shape[0]]


def scatter_kernel(p_ref, o_ref, first, second, summed, s1, r1, s2, r2, l1, l2):
    groups, count = first.shape[0], second.shape[0]
    f, t = lax.axis_index("fsdp"), lax.axis_index("tm")
    barrier = pltpu.get_barrier_semaphore()
    for k in range(1, groups):
        pl.semaphore_signal(
            barrier, inc=1, device_id={"fsdp": lax.rem(f + k, groups)}, device_id_type=MESH
        )
    for k in range(1, count):
        pl.semaphore_signal(
            barrier, inc=1, device_id={"tm": lax.rem(t + k, count)}, device_id_type=MESH
        )
    pl.semaphore_wait(barrier, groups - 1 + count - 1)
    local = pltpu.make_async_copy(p_ref.at[f], first.at[f], l1)
    local.start()
    copies = []
    for k in range(1, groups):
        peer = lax.rem(f + k, groups)
        copy = pltpu.make_async_remote_copy(
            src_ref=p_ref.at[peer],
            dst_ref=first.at[f],
            send_sem=s1.at[k],
            recv_sem=r1.at[k],
            device_id={"fsdp": peer},
            device_id_type=MESH,
        )
        copy.start()
        copies.append(copy)
    local.wait()
    for copy in copies:
        copy.wait()
    summed[...] = jnp.sum(first[...], axis=0)
    local = pltpu.make_async_copy(summed.at[t], second.at[t], l2)
    local.start()
    copies = []
    for k in range(1, count):
        peer = lax.rem(t + k, count)
        copy = pltpu.make_async_remote_copy(
            src_ref=summed.at[peer],
            dst_ref=second.at[t],
            send_sem=s2.at[k],
            recv_sem=r2.at[k],
            device_id={"tm": peer},
            device_id_type=MESH,
        )
        copy.start()
        copies.append(copy)
    local.wait()
    for copy in copies:
        copy.wait()
    o_ref[...] = jnp.sum(second[...], axis=0)


def scatter_sum(partial):
    groups, count = lax.axis_size("fsdp"), lax.axis_size("tm")
    piece = partial.size // (groups * count)
    arranged = jnp.transpose(partial.reshape(count, groups, 1, piece), (1, 0, 2, 3))
    out = pl.pallas_call(
        scatter_kernel,
        out_shape=jax.ShapeDtypeStruct((1, piece), jnp.float32),
        in_specs=[pl.BlockSpec(memory_space=pltpu.VMEM)],
        out_specs=pl.BlockSpec(memory_space=pltpu.VMEM),
        scratch_shapes=[
            pltpu.VMEM((groups, count, 1, piece), jnp.float32),
            pltpu.VMEM((count, 1, piece), jnp.float32),
            pltpu.VMEM((count, 1, piece), jnp.float32),
            pltpu.SemaphoreType.DMA((groups,)),
            pltpu.SemaphoreType.DMA((groups,)),
            pltpu.SemaphoreType.DMA((count,)),
            pltpu.SemaphoreType.DMA((count,)),
            pltpu.SemaphoreType.DMA,
            pltpu.SemaphoreType.DMA,
        ],
        compiler_params=pltpu.CompilerParams(collective_id=1, has_side_effects=True),
    )(arranged)
    return out.reshape(piece)


def conv_pool_kernel(xs_ref, w_ref, o_ref):
    height, width, channels = o_ref.shape
    rows = 8

    def body(r, carry):
        top = pl.multiple_of(r * rows, rows)
        hidden = []
        for j in range(2):
            acc = jnp.zeros((rows * width, channels), jnp.float32)
            for b in range(3):
                for c in range(3):
                    taps = [xs_ref[c, j + a, pl.ds(top + b, rows)] for a in range(3)]
                    lhs = jnp.concatenate(taps, axis=-1).reshape(rows * width, 3 * channels)
                    acc = acc + jnp.dot(lhs, w_ref[b * 3 + c], preferred_element_type=jnp.float32)
            silu = acc / (1.0 + jnp.exp(-acc))
            hidden.append(silu.astype(jnp.bfloat16).astype(jnp.float32))
        pooled = ((hidden[0] + hidden[1]) * 0.5).astype(o_ref.dtype)
        o_ref[pl.ds(top, rows)] = pooled.reshape(rows, width, channels)
        return carry

    lax.fori_loop(0, height // rows, body, 0)


def conv_pool(shifted, weights):
    _, _, rows, width, channels = shifted.shape
    height = rows - 2
    vmem = pl.BlockSpec(memory_space=pltpu.VMEM)
    flops = 2 * 2 * height * width * weights.shape[0] * weights.shape[1] * channels
    return pl.pallas_call(
        conv_pool_kernel,
        out_shape=jax.ShapeDtypeStruct((height, width, channels), jnp.bfloat16),
        in_specs=[vmem, vmem],
        out_specs=vmem,
        cost_estimate=pl.CostEstimate(
            flops=flops,
            transcendentals=2 * height * width * channels,
            bytes_accessed=shifted.size * 2 + weights.size * 2 + height * width * channels * 2,
        ),
    )(shifted, weights)


def prologue_kernel(x_ref, w_ref, m_ref, halo_ref, wall_ref, mall_ref, sends, recvs, wsends, wrecvs, msends, mrecvs, lsems):
    count, groups = lax.axis_size("tm"), lax.axis_size("fsdp")
    t, f = lax.axis_index("tm"), lax.axis_index("fsdp")
    t_next, t_prev = lax.rem(t + 1, count), lax.rem(t + count - 1, count)
    peers = [(t_next, f), (t_prev, f)] + [(t, lax.rem(f + k, groups)) for k in range(1, groups)]
    barrier = pltpu.get_barrier_semaphore()
    for dev in peers:
        pl.semaphore_signal(barrier, inc=1, device_id=dev, device_id_type=MESH)
    pl.semaphore_wait(barrier, len(peers))
    copies = [
        pltpu.make_async_remote_copy(
            src_ref=x_ref, dst_ref=halo_ref, send_sem=sends.at[0], recv_sem=recvs.at[0],
            device_id=(t_next, f), device_id_type=MESH,
        )
    ]
    copies[0].start()
    locals_ = [
        pltpu.make_async_copy(w_ref, wall_ref.at[f], lsems.at[0]),
        pltpu.make_async_copy(m_ref, mall_ref.at[f], lsems.at[1]),
    ]
    for copy in locals_:
        copy.start()
    for k in range(1, groups):
        dev = (t, lax.rem(f + k, groups))
        for src, dst, ss, rs in ((w_ref, wall_ref, wsends, wrecvs), (m_ref, mall_ref, msends, mrecvs)):
            copy = pltpu.make_async_remote_copy(
                src_ref=src, dst_ref=dst.at[f], send_sem=ss.at[k], recv_sem=rs.at[k],
                device_id=dev, device_id_type=MESH,
            )
            copy.start()
            copies.append(copy)
    for copy in locals_:
        copy.wait()
    for copy in copies:
        copy.wait()


def prologue(frames, conv_shard, mix_shard):
    groups = lax.axis_size("fsdp")
    vmem = pl.BlockSpec(memory_space=pltpu.VMEM)
    return pl.pallas_call(
        prologue_kernel,
        out_shape=(
            jax.ShapeDtypeStruct(frames.shape, frames.dtype),
            jax.ShapeDtypeStruct((groups,) + conv_shard.shape, conv_shard.dtype),
            jax.ShapeDtypeStruct((groups,) + mix_shard.shape, mix_shard.dtype),
        ),
        in_specs=[vmem] * 3,
        out_specs=(vmem,) * 3,
        scratch_shapes=[
            pltpu.SemaphoreType.DMA((1,)),
            pltpu.SemaphoreType.DMA((1,)),
            pltpu.SemaphoreType.DMA((groups,)),
            pltpu.SemaphoreType.DMA((groups,)),
            pltpu.SemaphoreType.DMA((groups,)),
            pltpu.SemaphoreType.DMA((groups,)),
            pltpu.SemaphoreType.DMA((2,)),
        ],
        compiler_params=pltpu.CompilerParams(collective_id=2, has_side_effects=True),
    )(frames, conv_shard, mix_shard)


def local(frames, conv_weight, mix_weight, cotangent):
    t = lax.axis_index("tm")
    count_frames, height, width, channels = frames.shape
    part = conv_weight.shape[-1]
    conv_shard = jnp.swapaxes(conv_weight, 3, 4).reshape(-1, part, channels)
    mix_shard = jnp.swapaxes(mix_weight, 1, 2)
    previous, wall, mall = prologue(frames, conv_shard, mix_shard)
    full_conv = jnp.transpose(wall, (1, 3, 0, 2)).reshape(conv_weight.shape[:-1] + (-1,))
    full_mix = jnp.transpose(mall, (1, 3, 0, 2)).reshape(mix_weight.shape[:-1] + (-1,))
    previous = jnp.where(t > 0, previous, jnp.zeros((), previous.dtype))
    timed = jnp.concatenate([previous, frames], axis=0)
    padded = with_halo(timed, (("fsdp", 2),), 1)
    padded = jnp.pad(padded, ((0, 0), (1, 1), (0, 0), (0, 0)))
    shifted = jnp.stack([padded[:, :, c : c + width] for c in range(3)])
    weights = jnp.transpose(full_conv, (1, 2, 0, 3, 4)).reshape(9, 3 * channels, -1)
    pooled = conv_pool(shifted, weights)[None]
    pooled = lax.all_to_all(pooled, "tm", split_axis=1, concat_axis=0, tiled=True)
    branch = pooled.astype(jnp.float32).reshape(-1, channels)
    flat_cot = cotangent.reshape(-1, channels)
    grad_terms = []
    for offset in range(3):
        lagged = delayed(pooled, offset).reshape(-1, channels)
        branch = branch + jnp.dot(lagged, full_mix[offset], preferred_element_type=jnp.float32)
        grad_terms.append(
            lax.dot_general(
                lagged, flat_cot, (((0,), (0,)), ((), ())), preferred_element_type=jnp.float32
            )
        )
    encoded = branch.astype(jnp.bfloat16).reshape(pooled.shape)
    mix_grad = scatter_sum(jnp.stack(grad_terms).reshape(-1))
    return (encoded, mix_grad)


def solution(mesh):
    return jax.shard_map(
        local,
        mesh=mesh,
        in_specs=(
            P("tm", None, "fsdp", None),
            P(None, None, None, None, "fsdp"),
            P(None, None, "fsdp"),
            P(None, "tm", "fsdp", None),
        ),
        out_specs=(P(None, "tm", "fsdp", None), P(("tm", "fsdp"))),
        check_vma=False,
    )
```

```python
import jax
import jax.numpy as jnp
from jax import lax
from jax.experimental import pallas as pl
from jax.experimental.pallas import tpu as pltpu
from jax.sharding import PartitionSpec as P

MESH = pl.DeviceIdType.MESH


def from_behind(block, axis, distance):
    devices = range(lax.axis_size(axis))
    route = [(i - distance, i) for i in devices if i - distance in devices]
    return lax.ppermute(block, axis, route)


def with_halo(cells, sides, width):
    for axis, dim in sides:
        count = lax.axis_size(axis)
        ends = count - 1
        head = lax.slice_in_dim(cells, 0, width, axis=dim)
        tail = lax.slice_in_dim(cells, cells.shape[dim] - width, cells.shape[dim], axis=dim)
        cells = jnp.concatenate(
            [
                lax.ppermute(tail, axis, [(i, (i + 1) % count) for i in range(ends)]),
                cells,
                lax.ppermute(head, axis, [((i + 1) % count, i) for i in range(ends)]),
            ],
            axis=dim,
        )
    return cells


def pool_pairs(hidden):
    shaped = hidden.reshape((hidden.shape[0] // 2, 2) + hidden.shape[1:]).astype(jnp.float32)
    return ((shaped[:, 0] + shaped[:, 1]) * 0.5).astype(jnp.bfloat16)


def delayed(block, offset):
    return jnp.pad(block, ((offset, 0), (0, 0), (0, 0), (0, 0)))[: block.shape[0]]


def scatter_kernel(p_ref, o_ref, first, second, summed, s1, r1, s2, r2, l1, l2):
    groups, count = first.shape[0], second.shape[0]
    f, t = lax.axis_index("fsdp"), lax.axis_index("tm")
    barrier = pltpu.get_barrier_semaphore()
    for k in range(1, groups):
        pl.semaphore_signal(
            barrier, inc=1, device_id={"fsdp": lax.rem(f + k, groups)}, device_id_type=MESH
        )
    for k in range(1, count):
        pl.semaphore_signal(
            barrier, inc=1, device_id={"tm": lax.rem(t + k, count)}, device_id_type=MESH
        )
    pl.semaphore_wait(barrier, groups - 1 + count - 1)
    local = pltpu.make_async_copy(p_ref.at[f], first.at[f], l1)
    local.start()
    copies = []
    for k in range(1, groups):
        peer = lax.rem(f + k, groups)
        copy = pltpu.make_async_remote_copy(
            src_ref=p_ref.at[peer],
            dst_ref=first.at[f],
            send_sem=s1.at[k],
            recv_sem=r1.at[k],
            device_id={"fsdp": peer},
            device_id_type=MESH,
        )
        copy.start()
        copies.append(copy)
    local.wait()
    for copy in copies:
        copy.wait()
    summed[...] = jnp.sum(first[...], axis=0)
    local = pltpu.make_async_copy(summed.at[t], second.at[t], l2)
    local.start()
    copies = []
    for k in range(1, count):
        peer = lax.rem(t + k, count)
        copy = pltpu.make_async_remote_copy(
            src_ref=summed.at[peer],
            dst_ref=second.at[t],
            send_sem=s2.at[k],
            recv_sem=r2.at[k],
            device_id={"tm": peer},
            device_id_type=MESH,
        )
        copy.start()
        copies.append(copy)
    local.wait()
    for copy in copies:
        copy.wait()
    o_ref[...] = jnp.sum(second[...], axis=0)


def scatter_sum(partial):
    groups, count = lax.axis_size("fsdp"), lax.axis_size("tm")
    piece = partial.size // (groups * count)
    arranged = jnp.transpose(partial.reshape(count, groups, 1, piece), (1, 0, 2, 3))
    out = pl.pallas_call(
        scatter_kernel,
        out_shape=jax.ShapeDtypeStruct((1, piece), jnp.float32),
        in_specs=[pl.BlockSpec(memory_space=pltpu.VMEM)],
        out_specs=pl.BlockSpec(memory_space=pltpu.VMEM),
        scratch_shapes=[
            pltpu.VMEM((groups, count, 1, piece), jnp.float32),
            pltpu.VMEM((count, 1, piece), jnp.float32),
            pltpu.VMEM((count, 1, piece), jnp.float32),
            pltpu.SemaphoreType.DMA((groups,)),
            pltpu.SemaphoreType.DMA((groups,)),
            pltpu.SemaphoreType.DMA((count,)),
            pltpu.SemaphoreType.DMA((count,)),
            pltpu.SemaphoreType.DMA,
            pltpu.SemaphoreType.DMA,
        ],
        compiler_params=pltpu.CompilerParams(collective_id=1, has_side_effects=True),
    )(arranged)
    return out.reshape(piece)


def conv_pool_kernel(xs_ref, w_ref, o_ref):
    height, width, channels = o_ref.shape
    rows = 8

    def body(r, carry):
        top = pl.multiple_of(r * rows, rows)
        hidden = []
        for j in range(2):
            acc = jnp.zeros((rows * width, channels), jnp.float32)
            for b in range(3):
                for c in range(3):
                    taps = [xs_ref[c, j + a, pl.ds(top + b, rows)] for a in range(3)]
                    lhs = jnp.concatenate(taps, axis=-1).reshape(rows * width, 3 * channels)
                    acc = acc + jnp.dot(lhs, w_ref[b * 3 + c], preferred_element_type=jnp.float32)
            silu = acc / (1.0 + jnp.exp(-acc))
            hidden.append(silu.astype(jnp.bfloat16).astype(jnp.float32))
        pooled = ((hidden[0] + hidden[1]) * 0.5).astype(o_ref.dtype)
        o_ref[pl.ds(top, rows)] = pooled.reshape(rows, width, channels)
        return carry

    lax.fori_loop(0, height // rows, body, 0)


def conv_pool(shifted, weights):
    _, _, rows, width, channels = shifted.shape
    height = rows - 2
    vmem = pl.BlockSpec(memory_space=pltpu.VMEM)
    flops = 2 * 2 * height * width * weights.shape[0] * weights.shape[1] * channels
    return pl.pallas_call(
        conv_pool_kernel,
        out_shape=jax.ShapeDtypeStruct((height, width, channels), jnp.bfloat16),
        in_specs=[vmem, vmem],
        out_specs=vmem,
        cost_estimate=pl.CostEstimate(
            flops=flops,
            transcendentals=2 * height * width * channels,
            bytes_accessed=shifted.size * 2 + weights.size * 2 + height * width * channels * 2,
        ),
    )(shifted, weights)


def prologue_kernel(x_ref, w_ref, m_ref, halo_ref, wall_ref, mall_ref, sends, recvs, wsends, wrecvs, msends, mrecvs, lsems):
    count, groups = lax.axis_size("tm"), lax.axis_size("fsdp")
    t, f = lax.axis_index("tm"), lax.axis_index("fsdp")
    t_next, t_prev = lax.rem(t + 1, count), lax.rem(t + count - 1, count)
    peers = [(t_next, f), (t_prev, f)] + [(t, lax.rem(f + k, groups)) for k in range(1, groups)]
    barrier = pltpu.get_barrier_semaphore()
    for dev in peers:
        pl.semaphore_signal(barrier, inc=1, device_id=dev, device_id_type=MESH)
    pl.semaphore_wait(barrier, len(peers))
    pieces = sends.shape[0]
    rows = x_ref.shape[1] // pieces
    halo = [
        pltpu.make_async_remote_copy(
            src_ref=x_ref.at[:, pl.ds(i * rows, rows)],
            dst_ref=halo_ref.at[:, pl.ds(i * rows, rows)],
            send_sem=sends.at[i], recv_sem=recvs.at[i],
            device_id=(t_next, f), device_id_type=MESH,
        )
        for i in range(pieces)
    ]

    @pl.when(t < count - 1)
    def _():
        for copy in halo:
            copy.start()

    copies = []
    locals_ = [
        pltpu.make_async_copy(w_ref, wall_ref.at[f], lsems.at[0]),
        pltpu.make_async_copy(m_ref, mall_ref.at[f], lsems.at[1]),
    ]
    for copy in locals_:
        copy.start()
    for k in range(1, groups):
        dev = (t, lax.rem(f + k, groups))
        for src, dst, ss, rs in ((w_ref, wall_ref, wsends, wrecvs), (m_ref, mall_ref, msends, mrecvs)):
            copy = pltpu.make_async_remote_copy(
                src_ref=src, dst_ref=dst.at[f], send_sem=ss.at[k], recv_sem=rs.at[k],
                device_id=dev, device_id_type=MESH,
            )
            copy.start()
            copies.append(copy)
    for copy in locals_:
        copy.wait()
    for copy in copies:
        copy.wait()

    @pl.when(t < count - 1)
    def _():
        for copy in halo:
            copy.wait_send()

    @pl.when(t > 0)
    def _():
        for copy in halo:
            copy.wait_recv()


def prologue(frames, conv_shard, mix_shard):
    groups = lax.axis_size("fsdp")
    vmem = pl.BlockSpec(memory_space=pltpu.VMEM)
    return pl.pallas_call(
        prologue_kernel,
        out_shape=(
            jax.ShapeDtypeStruct(frames.shape, frames.dtype),
            jax.ShapeDtypeStruct((groups,) + conv_shard.shape, conv_shard.dtype),
            jax.ShapeDtypeStruct((groups,) + mix_shard.shape, mix_shard.dtype),
        ),
        in_specs=[vmem] * 3,
        out_specs=(vmem,) * 3,
        scratch_shapes=[
            pltpu.SemaphoreType.DMA((4,)),
            pltpu.SemaphoreType.DMA((4,)),
            pltpu.SemaphoreType.DMA((groups,)),
            pltpu.SemaphoreType.DMA((groups,)),
            pltpu.SemaphoreType.DMA((groups,)),
            pltpu.SemaphoreType.DMA((groups,)),
            pltpu.SemaphoreType.DMA((2,)),
        ],
        compiler_params=pltpu.CompilerParams(collective_id=2, has_side_effects=True),
    )(frames, conv_shard, mix_shard)


def local(frames, conv_weight, mix_weight, cotangent):
    t = lax.axis_index("tm")
    count_frames, height, width, channels = frames.shape
    part = conv_weight.shape[-1]
    conv_shard = jnp.swapaxes(conv_weight, 3, 4).reshape(-1, part, channels)
    mix_shard = jnp.swapaxes(mix_weight, 1, 2)
    previous, wall, mall = prologue(frames, conv_shard, mix_shard)
    full_conv = jnp.transpose(wall, (1, 3, 0, 2)).reshape(conv_weight.shape[:-1] + (-1,))
    full_mix = jnp.transpose(mall, (1, 3, 0, 2)).reshape(mix_weight.shape[:-1] + (-1,))
    previous = jnp.where(t > 0, previous, jnp.zeros((), previous.dtype))
    timed = jnp.concatenate([previous, frames], axis=0)
    padded = with_halo(timed, (("fsdp", 2),), 1)
    padded = jnp.pad(padded, ((0, 0), (1, 1), (0, 0), (0, 0)))
    shifted = jnp.stack([padded[:, :, c : c + width] for c in range(3)])
    weights = jnp.transpose(full_conv, (1, 2, 0, 3, 4)).reshape(9, 3 * channels, -1)
    pooled = conv_pool(shifted, weights)[None]
    pooled = lax.all_to_all(pooled, "tm", split_axis=1, concat_axis=0, tiled=True)
    branch = pooled.astype(jnp.float32).reshape(-1, channels)
    flat_cot = cotangent.reshape(-1, channels)
    grad_terms = []
    for offset in range(3):
        lagged = delayed(pooled, offset).reshape(-1, channels)
        branch = branch + jnp.dot(lagged, full_mix[offset], preferred_element_type=jnp.float32)
        grad_terms.append(
            lax.dot_general(
                lagged, flat_cot, (((0,), (0,)), ((), ())), preferred_element_type=jnp.float32
            )
        )
    encoded = branch.astype(jnp.bfloat16).reshape(pooled.shape)
    mix_grad = scatter_sum(jnp.stack(grad_terms).reshape(-1))
    return (encoded, mix_grad)


def solution(mesh):
    return jax.shard_map(
        local,
        mesh=mesh,
        in_specs=(
            P("tm", None, "fsdp", None),
            P(None, None, None, None, "fsdp"),
            P(None, None, "fsdp"),
            P(None, "tm", "fsdp", None),
        ),
        out_specs=(P(None, "tm", "fsdp", None), P(("tm", "fsdp"))),
        check_vma=False,
    )
```

```python
import jax
import jax.numpy as jnp
from jax import lax
from jax.experimental import pallas as pl
from jax.experimental.pallas import tpu as pltpu
from jax.sharding import PartitionSpec as P

MESH = pl.DeviceIdType.MESH


def from_behind(block, axis, distance):
    devices = range(lax.axis_size(axis))
    route = [(i - distance, i) for i in devices if i - distance in devices]
    return lax.ppermute(block, axis, route)


def with_halo(cells, sides, width):
    for axis, dim in sides:
        count = lax.axis_size(axis)
        ends = count - 1
        head = lax.slice_in_dim(cells, 0, width, axis=dim)
        tail = lax.slice_in_dim(cells, cells.shape[dim] - width, cells.shape[dim], axis=dim)
        cells = jnp.concatenate(
            [
                lax.ppermute(tail, axis, [(i, (i + 1) % count) for i in range(ends)]),
                cells,
                lax.ppermute(head, axis, [((i + 1) % count, i) for i in range(ends)]),
            ],
            axis=dim,
        )
    return cells


def pool_pairs(hidden):
    shaped = hidden.reshape((hidden.shape[0] // 2, 2) + hidden.shape[1:]).astype(jnp.float32)
    return ((shaped[:, 0] + shaped[:, 1]) * 0.5).astype(jnp.bfloat16)


def delayed(block, offset):
    return jnp.pad(block, ((offset, 0), (0, 0), (0, 0), (0, 0)))[: block.shape[0]]


def scatter_kernel(p_ref, o_ref, first, second, summed, s1, r1, s2, r2, l1, l2):
    groups, count = first.shape[0], second.shape[0]
    f, t = lax.axis_index("fsdp"), lax.axis_index("tm")
    barrier = pltpu.get_barrier_semaphore()
    for k in range(1, groups):
        pl.semaphore_signal(
            barrier, inc=1, device_id={"fsdp": lax.rem(f + k, groups)}, device_id_type=MESH
        )
    for k in range(1, count):
        pl.semaphore_signal(
            barrier, inc=1, device_id={"tm": lax.rem(t + k, count)}, device_id_type=MESH
        )
    pl.semaphore_wait(barrier, groups - 1 + count - 1)
    local = pltpu.make_async_copy(p_ref.at[f], first.at[f], l1)
    local.start()
    copies = []
    for k in range(1, groups):
        peer = lax.rem(f + k, groups)
        copy = pltpu.make_async_remote_copy(
            src_ref=p_ref.at[peer],
            dst_ref=first.at[f],
            send_sem=s1.at[k],
            recv_sem=r1.at[k],
            device_id={"fsdp": peer},
            device_id_type=MESH,
        )
        copy.start()
        copies.append(copy)
    local.wait()
    for copy in copies:
        copy.wait()
    summed[...] = jnp.sum(first[...], axis=0)
    local = pltpu.make_async_copy(summed.at[t], second.at[t], l2)
    local.start()
    copies = []
    for k in range(1, count):
        peer = lax.rem(t + k, count)
        copy = pltpu.make_async_remote_copy(
            src_ref=summed.at[peer],
            dst_ref=second.at[t],
            send_sem=s2.at[k],
            recv_sem=r2.at[k],
            device_id={"tm": peer},
            device_id_type=MESH,
        )
        copy.start()
        copies.append(copy)
    local.wait()
    for copy in copies:
        copy.wait()
    o_ref[...] = jnp.sum(second[...], axis=0)


def scatter_sum(partial):
    groups, count = lax.axis_size("fsdp"), lax.axis_size("tm")
    piece = partial.size // (groups * count)
    arranged = jnp.transpose(partial.reshape(count, groups, 1, piece), (1, 0, 2, 3))
    out = pl.pallas_call(
        scatter_kernel,
        out_shape=jax.ShapeDtypeStruct((1, piece), jnp.float32),
        in_specs=[pl.BlockSpec(memory_space=pltpu.VMEM)],
        out_specs=pl.BlockSpec(memory_space=pltpu.VMEM),
        scratch_shapes=[
            pltpu.VMEM((groups, count, 1, piece), jnp.float32),
            pltpu.VMEM((count, 1, piece), jnp.float32),
            pltpu.VMEM((count, 1, piece), jnp.float32),
            pltpu.SemaphoreType.DMA((groups,)),
            pltpu.SemaphoreType.DMA((groups,)),
            pltpu.SemaphoreType.DMA((count,)),
            pltpu.SemaphoreType.DMA((count,)),
            pltpu.SemaphoreType.DMA,
            pltpu.SemaphoreType.DMA,
        ],
        compiler_params=pltpu.CompilerParams(collective_id=1, has_side_effects=True),
    )(arranged)
    return out.reshape(piece)


def conv_pool_kernel(p_ref, w_ref, o_ref, xs_ref):
    height, width, channels = o_ref.shape
    frames = p_ref.shape[0]
    rows = 8
    band = 8

    def shift(i, carry):
        q, r = i // (p_ref.shape[1] // band), i % (p_ref.shape[1] // band)
        top = pl.multiple_of(r * band, band)
        block = p_ref[q, pl.ds(top, band)].astype(jnp.float32)
        for c in range(3):
            xs_ref[c, q, pl.ds(top, band)] = block[:, c : c + width].astype(xs_ref.dtype)
        return carry

    lax.fori_loop(0, frames * (p_ref.shape[1] // band), shift, 0)

    def body(r, carry):
        top = pl.multiple_of(r * rows, rows)
        hidden = []
        for j in range(2):
            acc = jnp.zeros((rows * width, channels), jnp.float32)
            for b in range(3):
                for c in range(3):
                    taps = [xs_ref[c, j + a, pl.ds(top + b, rows)] for a in range(3)]
                    lhs = jnp.concatenate(taps, axis=-1).reshape(rows * width, 3 * channels)
                    acc = acc + jnp.dot(lhs, w_ref[b * 3 + c], preferred_element_type=jnp.float32)
            silu = acc / (1.0 + jnp.exp(-acc))
            hidden.append(silu.astype(jnp.bfloat16).astype(jnp.float32))
        pooled = ((hidden[0] + hidden[1]) * 0.5).astype(o_ref.dtype)
        o_ref[pl.ds(top, rows)] = pooled.reshape(rows, width, channels)
        return carry

    lax.fori_loop(0, height // rows, body, 0)


def conv_pool(padded, weights):
    frames, rows, wide, channels = padded.shape
    height, width = rows - 8, wide - 2
    vmem = pl.BlockSpec(memory_space=pltpu.VMEM)
    flops = 2 * 2 * height * width * weights.shape[0] * weights.shape[1] * channels
    return pl.pallas_call(
        conv_pool_kernel,
        out_shape=jax.ShapeDtypeStruct((height, width, channels), jnp.bfloat16),
        in_specs=[vmem, vmem],
        out_specs=vmem,
        scratch_shapes=[pltpu.VMEM((3, frames, rows, width, channels), padded.dtype)],
        cost_estimate=pl.CostEstimate(
            flops=flops,
            transcendentals=2 * height * width * channels,
            bytes_accessed=padded.size * 2 + weights.size * 2 + height * width * channels * 2,
        ),
    )(padded, weights)


def prologue_kernel(x_ref, w_ref, m_ref, halo_ref, wall_ref, mall_ref, sends, recvs, wsends, wrecvs, msends, mrecvs, lsems):
    count, groups = lax.axis_size("tm"), lax.axis_size("fsdp")
    t, f = lax.axis_index("tm"), lax.axis_index("fsdp")
    t_next, t_prev = lax.rem(t + 1, count), lax.rem(t + count - 1, count)
    peers = [(t_next, f), (t_prev, f)] + [(t, lax.rem(f + k, groups)) for k in range(1, groups)]
    barrier = pltpu.get_barrier_semaphore()
    for dev in peers:
        pl.semaphore_signal(barrier, inc=1, device_id=dev, device_id_type=MESH)
    pl.semaphore_wait(barrier, len(peers))
    pieces = sends.shape[0]
    rows = x_ref.shape[1] // pieces
    halo = [
        pltpu.make_async_remote_copy(
            src_ref=x_ref.at[:, pl.ds(i * rows, rows)],
            dst_ref=halo_ref.at[:, pl.ds(i * rows, rows)],
            send_sem=sends.at[i], recv_sem=recvs.at[i],
            device_id=(t_next, f), device_id_type=MESH,
        )
        for i in range(pieces)
    ]

    @pl.when(t < count - 1)
    def _():
        for copy in halo:
            copy.start()

    copies = []
    locals_ = [
        pltpu.make_async_copy(w_ref, wall_ref.at[f], lsems.at[0]),
        pltpu.make_async_copy(m_ref, mall_ref.at[f], lsems.at[1]),
    ]
    for copy in locals_:
        copy.start()
    for k in range(1, groups):
        dev = (t, lax.rem(f + k, groups))
        for src, dst, ss, rs in ((w_ref, wall_ref, wsends, wrecvs), (m_ref, mall_ref, msends, mrecvs)):
            copy = pltpu.make_async_remote_copy(
                src_ref=src, dst_ref=dst.at[f], send_sem=ss.at[k], recv_sem=rs.at[k],
                device_id=dev, device_id_type=MESH,
            )
            copy.start()
            copies.append(copy)
    for copy in locals_:
        copy.wait()
    for copy in copies:
        copy.wait()

    @pl.when(t < count - 1)
    def _():
        for copy in halo:
            copy.wait_send()

    @pl.when(t > 0)
    def _():
        for copy in halo:
            copy.wait_recv()


def prologue(frames, conv_shard, mix_shard):
    groups = lax.axis_size("fsdp")
    vmem = pl.BlockSpec(memory_space=pltpu.VMEM)
    return pl.pallas_call(
        prologue_kernel,
        out_shape=(
            jax.ShapeDtypeStruct(frames.shape, frames.dtype),
            jax.ShapeDtypeStruct((groups,) + conv_shard.shape, conv_shard.dtype),
            jax.ShapeDtypeStruct((groups,) + mix_shard.shape, mix_shard.dtype),
        ),
        in_specs=[vmem] * 3,
        out_specs=(vmem,) * 3,
        scratch_shapes=[
            pltpu.SemaphoreType.DMA((4,)),
            pltpu.SemaphoreType.DMA((4,)),
            pltpu.SemaphoreType.DMA((groups,)),
            pltpu.SemaphoreType.DMA((groups,)),
            pltpu.SemaphoreType.DMA((groups,)),
            pltpu.SemaphoreType.DMA((groups,)),
            pltpu.SemaphoreType.DMA((2,)),
        ],
        compiler_params=pltpu.CompilerParams(collective_id=2, has_side_effects=True),
    )(frames, conv_shard, mix_shard)


def local(frames, conv_weight, mix_weight, cotangent):
    t = lax.axis_index("tm")
    count_frames, height, width, channels = frames.shape
    part = conv_weight.shape[-1]
    conv_shard = jnp.swapaxes(conv_weight, 3, 4).reshape(-1, part, channels)
    mix_shard = jnp.swapaxes(mix_weight, 1, 2)
    previous, wall, mall = prologue(frames, conv_shard, mix_shard)
    full_conv = jnp.transpose(wall, (1, 3, 0, 2)).reshape(conv_weight.shape[:-1] + (-1,))
    full_mix = jnp.transpose(mall, (1, 3, 0, 2)).reshape(mix_weight.shape[:-1] + (-1,))
    previous = jnp.where(t > 0, previous, jnp.zeros((), previous.dtype))
    timed = jnp.concatenate([previous, frames], axis=0)
    padded = with_halo(timed, (("fsdp", 2),), 1)
    padded = jnp.pad(padded, ((0, 0), (1, 7), (0, 0), (0, 0)))
    weights = jnp.transpose(full_conv, (1, 2, 0, 3, 4)).reshape(9, 3 * channels, -1)
    pooled = conv_pool(padded, weights)[None]
    pooled = lax.all_to_all(pooled, "tm", split_axis=1, concat_axis=0, tiled=True)
    branch = pooled.astype(jnp.float32).reshape(-1, channels)
    flat_cot = cotangent.reshape(-1, channels)
    grad_terms = []
    for offset in range(3):
        lagged = delayed(pooled, offset).reshape(-1, channels)
        branch = branch + jnp.dot(lagged, full_mix[offset], preferred_element_type=jnp.float32)
        grad_terms.append(
            lax.dot_general(
                lagged, flat_cot, (((0,), (0,)), ((), ())), preferred_element_type=jnp.float32
            )
        )
    encoded = branch.astype(jnp.bfloat16).reshape(pooled.shape)
    mix_grad = scatter_sum(jnp.stack(grad_terms).reshape(-1))
    return (encoded, mix_grad)


def solution(mesh):
    return jax.shard_map(
        local,
        mesh=mesh,
        in_specs=(
            P("tm", None, "fsdp", None),
            P(None, None, None, None, "fsdp"),
            P(None, None, "fsdp"),
            P(None, "tm", "fsdp", None),
        ),
        out_specs=(P(None, "tm", "fsdp", None), P(("tm", "fsdp"))),
        check_vma=False,
    )
```

```python
import jax
import jax.numpy as jnp
from jax import lax
from jax.experimental import pallas as pl
from jax.experimental.pallas import tpu as pltpu
from jax.sharding import PartitionSpec as P

MESH = pl.DeviceIdType.MESH


def from_behind(block, axis, distance):
    devices = range(lax.axis_size(axis))
    route = [(i - distance, i) for i in devices if i - distance in devices]
    return lax.ppermute(block, axis, route)


def with_halo(cells, sides, width):
    for axis, dim in sides:
        count = lax.axis_size(axis)
        ends = count - 1
        head = lax.slice_in_dim(cells, 0, width, axis=dim)
        tail = lax.slice_in_dim(cells, cells.shape[dim] - width, cells.shape[dim], axis=dim)
        cells = jnp.concatenate(
            [
                lax.ppermute(tail, axis, [(i, (i + 1) % count) for i in range(ends)]),
                cells,
                lax.ppermute(head, axis, [((i + 1) % count, i) for i in range(ends)]),
            ],
            axis=dim,
        )
    return cells


def pool_pairs(hidden):
    shaped = hidden.reshape((hidden.shape[0] // 2, 2) + hidden.shape[1:]).astype(jnp.float32)
    return ((shaped[:, 0] + shaped[:, 1]) * 0.5).astype(jnp.bfloat16)


def delayed(block, offset):
    return jnp.pad(block, ((offset, 0), (0, 0), (0, 0), (0, 0)))[: block.shape[0]]


def scatter_kernel(p_ref, o_ref, first, second, summed, s1, r1, s2, r2, l1, l2):
    groups, count = first.shape[0], second.shape[0]
    f, t = lax.axis_index("fsdp"), lax.axis_index("tm")
    barrier = pltpu.get_barrier_semaphore()
    for k in range(1, groups):
        pl.semaphore_signal(
            barrier, inc=1, device_id={"fsdp": lax.rem(f + k, groups)}, device_id_type=MESH
        )
    for k in range(1, count):
        pl.semaphore_signal(
            barrier, inc=1, device_id={"tm": lax.rem(t + k, count)}, device_id_type=MESH
        )
    pl.semaphore_wait(barrier, groups - 1 + count - 1)
    local = pltpu.make_async_copy(p_ref.at[f], first.at[f], l1)
    local.start()
    copies = []
    for k in range(1, groups):
        peer = lax.rem(f + k, groups)
        copy = pltpu.make_async_remote_copy(
            src_ref=p_ref.at[peer],
            dst_ref=first.at[f],
            send_sem=s1.at[k],
            recv_sem=r1.at[k],
            device_id={"fsdp": peer},
            device_id_type=MESH,
        )
        copy.start()
        copies.append(copy)
    local.wait()
    for copy in copies:
        copy.wait()
    summed[...] = jnp.sum(first[...], axis=0)
    local = pltpu.make_async_copy(summed.at[t], second.at[t], l2)
    local.start()
    copies = []
    for k in range(1, count):
        peer = lax.rem(t + k, count)
        copy = pltpu.make_async_remote_copy(
            src_ref=summed.at[peer],
            dst_ref=second.at[t],
            send_sem=s2.at[k],
            recv_sem=r2.at[k],
            device_id={"tm": peer},
            device_id_type=MESH,
        )
        copy.start()
        copies.append(copy)
    local.wait()
    for copy in copies:
        copy.wait()
    o_ref[...] = jnp.sum(second[...], axis=0)


def scatter_sum(partial):
    groups, count = lax.axis_size("fsdp"), lax.axis_size("tm")
    piece = partial.size // (groups * count)
    arranged = jnp.transpose(partial.reshape(count, groups, 1, piece), (1, 0, 2, 3))
    out = pl.pallas_call(
        scatter_kernel,
        out_shape=jax.ShapeDtypeStruct((1, piece), jnp.float32),
        in_specs=[pl.BlockSpec(memory_space=pltpu.VMEM)],
        out_specs=pl.BlockSpec(memory_space=pltpu.VMEM),
        scratch_shapes=[
            pltpu.VMEM((groups, count, 1, piece), jnp.float32),
            pltpu.VMEM((count, 1, piece), jnp.float32),
            pltpu.VMEM((count, 1, piece), jnp.float32),
            pltpu.SemaphoreType.DMA((groups,)),
            pltpu.SemaphoreType.DMA((groups,)),
            pltpu.SemaphoreType.DMA((count,)),
            pltpu.SemaphoreType.DMA((count,)),
            pltpu.SemaphoreType.DMA,
            pltpu.SemaphoreType.DMA,
        ],
        compiler_params=pltpu.CompilerParams(collective_id=1, has_side_effects=True),
    )(arranged)
    return out.reshape(piece)


def conv_pool_kernel(p_ref, w_ref, o_ref, xs_ref):
    height, width, channels = o_ref.shape
    frames = p_ref.shape[0]
    rows = 8
    band = 8

    def shift(i, carry):
        q, r = i // (p_ref.shape[1] // band), i % (p_ref.shape[1] // band)
        top = pl.multiple_of(r * band, band)
        block = p_ref[q, pl.ds(top, band)].astype(jnp.float32)
        for c in range(3):
            xs_ref[c, q, pl.ds(top, band)] = block[:, c : c + width].astype(xs_ref.dtype)
        return carry

    lax.fori_loop(0, frames * (p_ref.shape[1] // band), shift, 0)

    def body(r, carry):
        top = pl.multiple_of(r * rows, rows)
        span = rows * width
        acc = jnp.zeros((2 * span, channels), jnp.float32)
        for b in range(3):
            for c in range(3):
                lhs = jnp.concatenate(
                    [
                        jnp.concatenate(
                            [xs_ref[c, j + a, pl.ds(top + b, rows)] for a in range(3)], axis=-1
                        ).reshape(span, 3 * channels)
                        for j in range(2)
                    ],
                    axis=0,
                )
                acc = acc + jnp.dot(lhs, w_ref[b * 3 + c], preferred_element_type=jnp.float32)
        silu = (acc / (1.0 + jnp.exp(-acc))).astype(jnp.bfloat16).astype(jnp.float32)
        pooled = ((silu[:span] + silu[span:]) * 0.5).astype(o_ref.dtype)
        o_ref[pl.ds(top, rows)] = pooled.reshape(rows, width, channels)
        return carry

    lax.fori_loop(0, height // rows, body, 0)


def conv_pool(padded, weights):
    frames, rows, wide, channels = padded.shape
    height, width = rows - 8, wide - 2
    vmem = pl.BlockSpec(memory_space=pltpu.VMEM)
    flops = 2 * 2 * height * width * weights.shape[0] * weights.shape[1] * channels
    return pl.pallas_call(
        conv_pool_kernel,
        out_shape=jax.ShapeDtypeStruct((height, width, channels), jnp.bfloat16),
        in_specs=[vmem, vmem],
        out_specs=vmem,
        scratch_shapes=[pltpu.VMEM((3, frames, rows, width, channels), padded.dtype)],
        cost_estimate=pl.CostEstimate(
            flops=flops,
            transcendentals=2 * height * width * channels,
            bytes_accessed=padded.size * 2 + weights.size * 2 + height * width * channels * 2,
        ),
    )(padded, weights)


def prologue_kernel(x_ref, w_ref, m_ref, halo_ref, wall_ref, mall_ref, sends, recvs, wsends, wrecvs, msends, mrecvs, lsems):
    count, groups = lax.axis_size("tm"), lax.axis_size("fsdp")
    t, f = lax.axis_index("tm"), lax.axis_index("fsdp")
    t_next, t_prev = lax.rem(t + 1, count), lax.rem(t + count - 1, count)
    peers = [(t_next, f), (t_prev, f)] + [(t, lax.rem(f + k, groups)) for k in range(1, groups)]
    barrier = pltpu.get_barrier_semaphore()
    for dev in peers:
        pl.semaphore_signal(barrier, inc=1, device_id=dev, device_id_type=MESH)
    pl.semaphore_wait(barrier, len(peers))
    pieces = sends.shape[0]
    rows = x_ref.shape[1] // pieces
    halo = [
        pltpu.make_async_remote_copy(
            src_ref=x_ref.at[:, pl.ds(i * rows, rows)],
            dst_ref=halo_ref.at[:, pl.ds(i * rows, rows)],
            send_sem=sends.at[i], recv_sem=recvs.at[i],
            device_id=(t_next, f), device_id_type=MESH,
        )
        for i in range(pieces)
    ]

    @pl.when(t < count - 1)
    def _():
        for copy in halo:
            copy.start()

    copies = []
    locals_ = [
        pltpu.make_async_copy(w_ref, wall_ref.at[f], lsems.at[0]),
        pltpu.make_async_copy(m_ref, mall_ref.at[f], lsems.at[1]),
    ]
    for copy in locals_:
        copy.start()
    for k in range(1, groups):
        dev = (t, lax.rem(f + k, groups))
        for src, dst, ss, rs in ((w_ref, wall_ref, wsends, wrecvs), (m_ref, mall_ref, msends, mrecvs)):
            copy = pltpu.make_async_remote_copy(
                src_ref=src, dst_ref=dst.at[f], send_sem=ss.at[k], recv_sem=rs.at[k],
                device_id=dev, device_id_type=MESH,
            )
            copy.start()
            copies.append(copy)
    for copy in locals_:
        copy.wait()
    for copy in copies:
        copy.wait()

    @pl.when(t < count - 1)
    def _():
        for copy in halo:
            copy.wait_send()

    @pl.when(t > 0)
    def _():
        for copy in halo:
            copy.wait_recv()


def prologue(frames, conv_shard, mix_shard):
    groups = lax.axis_size("fsdp")
    vmem = pl.BlockSpec(memory_space=pltpu.VMEM)
    return pl.pallas_call(
        prologue_kernel,
        out_shape=(
            jax.ShapeDtypeStruct(frames.shape, frames.dtype),
            jax.ShapeDtypeStruct((groups,) + conv_shard.shape, conv_shard.dtype),
            jax.ShapeDtypeStruct((groups,) + mix_shard.shape, mix_shard.dtype),
        ),
        in_specs=[vmem] * 3,
        out_specs=(vmem,) * 3,
        scratch_shapes=[
            pltpu.SemaphoreType.DMA((4,)),
            pltpu.SemaphoreType.DMA((4,)),
            pltpu.SemaphoreType.DMA((groups,)),
            pltpu.SemaphoreType.DMA((groups,)),
            pltpu.SemaphoreType.DMA((groups,)),
            pltpu.SemaphoreType.DMA((groups,)),
            pltpu.SemaphoreType.DMA((2,)),
        ],
        compiler_params=pltpu.CompilerParams(collective_id=2, has_side_effects=True),
    )(frames, conv_shard, mix_shard)


def local(frames, conv_weight, mix_weight, cotangent):
    t = lax.axis_index("tm")
    count_frames, height, width, channels = frames.shape
    part = conv_weight.shape[-1]
    conv_shard = jnp.swapaxes(conv_weight, 3, 4).reshape(-1, part, channels)
    mix_shard = jnp.swapaxes(mix_weight, 1, 2)
    previous, wall, mall = prologue(frames, conv_shard, mix_shard)
    full_conv = jnp.transpose(wall, (1, 3, 0, 2)).reshape(conv_weight.shape[:-1] + (-1,))
    full_mix = jnp.transpose(mall, (1, 3, 0, 2)).reshape(mix_weight.shape[:-1] + (-1,))
    previous = jnp.where(t > 0, previous, jnp.zeros((), previous.dtype))
    timed = jnp.concatenate([previous, frames], axis=0)
    padded = with_halo(timed, (("fsdp", 2),), 1)
    padded = jnp.pad(padded, ((0, 0), (1, 7), (0, 0), (0, 0)))
    weights = jnp.transpose(full_conv, (1, 2, 0, 3, 4)).reshape(9, 3 * channels, -1)
    pooled = conv_pool(padded, weights)[None]
    pooled = lax.all_to_all(pooled, "tm", split_axis=1, concat_axis=0, tiled=True)
    branch = pooled.astype(jnp.float32).reshape(-1, channels)
    flat_cot = cotangent.reshape(-1, channels)
    grad_terms = []
    for offset in range(3):
        lagged = delayed(pooled, offset).reshape(-1, channels)
        branch = branch + jnp.dot(lagged, full_mix[offset], preferred_element_type=jnp.float32)
        grad_terms.append(
            lax.dot_general(
                lagged, flat_cot, (((0,), (0,)), ((), ())), preferred_element_type=jnp.float32
            )
        )
    encoded = branch.astype(jnp.bfloat16).reshape(pooled.shape)
    mix_grad = scatter_sum(jnp.stack(grad_terms).reshape(-1))
    return (encoded, mix_grad)


def solution(mesh):
    return jax.shard_map(
        local,
        mesh=mesh,
        in_specs=(
            P("tm", None, "fsdp", None),
            P(None, None, None, None, "fsdp"),
            P(None, None, "fsdp"),
            P(None, "tm", "fsdp", None),
        ),
        out_specs=(P(None, "tm", "fsdp", None), P(("tm", "fsdp"))),
        check_vma=False,
    )
```

```python
import jax
import jax.numpy as jnp
from jax import lax
from jax.experimental import pallas as pl
from jax.experimental.pallas import tpu as pltpu
from jax.sharding import PartitionSpec as P

MESH = pl.DeviceIdType.MESH


def from_behind(block, axis, distance):
    devices = range(lax.axis_size(axis))
    route = [(i - distance, i) for i in devices if i - distance in devices]
    return lax.ppermute(block, axis, route)


def with_halo(cells, sides, width):
    for axis, dim in sides:
        count = lax.axis_size(axis)
        ends = count - 1
        head = lax.slice_in_dim(cells, 0, width, axis=dim)
        tail = lax.slice_in_dim(cells, cells.shape[dim] - width, cells.shape[dim], axis=dim)
        cells = jnp.concatenate(
            [
                lax.ppermute(tail, axis, [(i, (i + 1) % count) for i in range(ends)]),
                cells,
                lax.ppermute(head, axis, [((i + 1) % count, i) for i in range(ends)]),
            ],
            axis=dim,
        )
    return cells


def pool_pairs(hidden):
    shaped = hidden.reshape((hidden.shape[0] // 2, 2) + hidden.shape[1:]).astype(jnp.float32)
    return ((shaped[:, 0] + shaped[:, 1]) * 0.5).astype(jnp.bfloat16)


def delayed(block, offset):
    return jnp.pad(block, ((offset, 0), (0, 0), (0, 0), (0, 0)))[: block.shape[0]]


def scatter_kernel(p_ref, o_ref, held, sends, recvs, local_sem):
    groups, total = lax.axis_size("fsdp"), held.shape[0]
    me = lax.axis_index("tm") * groups + lax.axis_index("fsdp")

    def device(k):
        peer = lax.rem(me + k, total)
        return (peer // groups, lax.rem(peer, groups))

    def copy_of(k):
        return pltpu.make_async_remote_copy(
            src_ref=p_ref.at[lax.rem(me + k, total)],
            dst_ref=held.at[me],
            send_sem=sends.at[k],
            recv_sem=recvs.at[k],
            device_id=device(k),
            device_id_type=MESH,
        )

    barrier = pltpu.get_barrier_semaphore()

    @pl.loop(1, total)
    def _(k):
        pl.semaphore_signal(barrier, inc=1, device_id=device(k), device_id_type=MESH)

    pl.semaphore_wait(barrier, total - 1)
    local = pltpu.make_async_copy(p_ref.at[me], held.at[me], local_sem)
    local.start()

    @pl.loop(1, total)
    def _(k):
        copy_of(k).start()

    local.wait()

    @pl.loop(1, total)
    def _(k):
        copy_of(k).wait()

    o_ref[...] = jnp.sum(held[...], axis=0)


def scatter_sum(partial):
    total = lax.axis_size("fsdp") * lax.axis_size("tm")
    piece = partial.size // total
    out = pl.pallas_call(
        scatter_kernel,
        out_shape=jax.ShapeDtypeStruct((1, piece), jnp.float32),
        in_specs=[pl.BlockSpec(memory_space=pltpu.VMEM)],
        out_specs=pl.BlockSpec(memory_space=pltpu.VMEM),
        scratch_shapes=[
            pltpu.VMEM((total, 1, piece), jnp.float32),
            pltpu.SemaphoreType.DMA((total,)),
            pltpu.SemaphoreType.DMA((total,)),
            pltpu.SemaphoreType.DMA,
        ],
        compiler_params=pltpu.CompilerParams(collective_id=1, has_side_effects=True),
    )(partial.reshape(total, 1, piece))
    return out.reshape(piece)


def conv_pool_kernel(p_ref, w_ref, o_ref, xs_ref):
    height, width, channels = o_ref.shape
    frames = p_ref.shape[0]
    rows = 8
    band = 8

    def shift(i, carry):
        q, r = i // (p_ref.shape[1] // band), i % (p_ref.shape[1] // band)
        top = pl.multiple_of(r * band, band)
        block = p_ref[q, pl.ds(top, band)].astype(jnp.float32)
        for c in range(3):
            xs_ref[c, q, pl.ds(top, band)] = block[:, c : c + width].astype(xs_ref.dtype)
        return carry

    lax.fori_loop(0, frames * (p_ref.shape[1] // band), shift, 0)

    def body(r, carry):
        top = pl.multiple_of(r * rows, rows)
        span = rows * width
        acc = jnp.zeros((2 * span, channels), jnp.float32)
        for b in range(3):
            for c in range(3):
                lhs = jnp.concatenate(
                    [
                        jnp.concatenate(
                            [xs_ref[c, j + a, pl.ds(top + b, rows)] for a in range(3)], axis=-1
                        ).reshape(span, 3 * channels)
                        for j in range(2)
                    ],
                    axis=0,
                )
                acc = acc + jnp.dot(lhs, w_ref[b * 3 + c], preferred_element_type=jnp.float32)
        silu = (acc / (1.0 + jnp.exp(-acc))).astype(jnp.bfloat16).astype(jnp.float32)
        pooled = ((silu[:span] + silu[span:]) * 0.5).astype(o_ref.dtype)
        o_ref[pl.ds(top, rows)] = pooled.reshape(rows, width, channels)
        return carry

    lax.fori_loop(0, height // rows, body, 0)


def conv_pool(padded, weights):
    frames, rows, wide, channels = padded.shape
    height, width = rows - 8, wide - 2
    vmem = pl.BlockSpec(memory_space=pltpu.VMEM)
    flops = 2 * 2 * height * width * weights.shape[0] * weights.shape[1] * channels
    return pl.pallas_call(
        conv_pool_kernel,
        out_shape=jax.ShapeDtypeStruct((height, width, channels), jnp.bfloat16),
        in_specs=[vmem, vmem],
        out_specs=vmem,
        scratch_shapes=[pltpu.VMEM((3, frames, rows, width, channels), padded.dtype)],
        cost_estimate=pl.CostEstimate(
            flops=flops,
            transcendentals=2 * height * width * channels,
            bytes_accessed=padded.size * 2 + weights.size * 2 + height * width * channels * 2,
        ),
    )(padded, weights)


def prologue_kernel(x_ref, w_ref, m_ref, halo_ref, wall_ref, mall_ref, sends, recvs, wsends, wrecvs, msends, mrecvs, lsems):
    count, groups = lax.axis_size("tm"), lax.axis_size("fsdp")
    t, f = lax.axis_index("tm"), lax.axis_index("fsdp")
    t_next, t_prev = lax.rem(t + 1, count), lax.rem(t + count - 1, count)
    peers = [(t_next, f), (t_prev, f)] + [(t, lax.rem(f + k, groups)) for k in range(1, groups)]
    barrier = pltpu.get_barrier_semaphore()
    for dev in peers:
        pl.semaphore_signal(barrier, inc=1, device_id=dev, device_id_type=MESH)
    pl.semaphore_wait(barrier, len(peers))
    pieces = sends.shape[0]
    rows = x_ref.shape[1] // pieces
    halo = [
        pltpu.make_async_remote_copy(
            src_ref=x_ref.at[:, pl.ds(i * rows, rows)],
            dst_ref=halo_ref.at[:, pl.ds(i * rows, rows)],
            send_sem=sends.at[i], recv_sem=recvs.at[i],
            device_id=(t_next, f), device_id_type=MESH,
        )
        for i in range(pieces)
    ]

    @pl.when(t < count - 1)
    def _():
        for copy in halo:
            copy.start()

    copies = []
    locals_ = [
        pltpu.make_async_copy(w_ref, wall_ref.at[f], lsems.at[0]),
        pltpu.make_async_copy(m_ref, mall_ref.at[f], lsems.at[1]),
    ]
    for copy in locals_:
        copy.start()
    for k in range(1, groups):
        dev = (t, lax.rem(f + k, groups))
        for src, dst, ss, rs in ((w_ref, wall_ref, wsends, wrecvs), (m_ref, mall_ref, msends, mrecvs)):
            copy = pltpu.make_async_remote_copy(
                src_ref=src, dst_ref=dst.at[f], send_sem=ss.at[k], recv_sem=rs.at[k],
                device_id=dev, device_id_type=MESH,
            )
            copy.start()
            copies.append(copy)
    for copy in locals_:
        copy.wait()
    for copy in copies:
        copy.wait()

    @pl.when(t < count - 1)
    def _():
        for copy in halo:
            copy.wait_send()

    @pl.when(t > 0)
    def _():
        for copy in halo:
            copy.wait_recv()


def prologue(frames, conv_shard, mix_shard):
    groups = lax.axis_size("fsdp")
    vmem = pl.BlockSpec(memory_space=pltpu.VMEM)
    return pl.pallas_call(
        prologue_kernel,
        out_shape=(
            jax.ShapeDtypeStruct(frames.shape, frames.dtype),
            jax.ShapeDtypeStruct((groups,) + conv_shard.shape, conv_shard.dtype),
            jax.ShapeDtypeStruct((groups,) + mix_shard.shape, mix_shard.dtype),
        ),
        in_specs=[vmem] * 3,
        out_specs=(vmem,) * 3,
        scratch_shapes=[
            pltpu.SemaphoreType.DMA((4,)),
            pltpu.SemaphoreType.DMA((4,)),
            pltpu.SemaphoreType.DMA((groups,)),
            pltpu.SemaphoreType.DMA((groups,)),
            pltpu.SemaphoreType.DMA((groups,)),
            pltpu.SemaphoreType.DMA((groups,)),
            pltpu.SemaphoreType.DMA((2,)),
        ],
        compiler_params=pltpu.CompilerParams(collective_id=2, has_side_effects=True),
    )(frames, conv_shard, mix_shard)


def local(frames, conv_weight, mix_weight, cotangent):
    t = lax.axis_index("tm")
    count_frames, height, width, channels = frames.shape
    part = conv_weight.shape[-1]
    conv_shard = jnp.swapaxes(conv_weight, 3, 4).reshape(-1, part, channels)
    mix_shard = jnp.swapaxes(mix_weight, 1, 2)
    previous, wall, mall = prologue(frames, conv_shard, mix_shard)
    full_conv = jnp.transpose(wall, (1, 3, 0, 2)).reshape(conv_weight.shape[:-1] + (-1,))
    full_mix = jnp.transpose(mall, (1, 3, 0, 2)).reshape(mix_weight.shape[:-1] + (-1,))
    previous = jnp.where(t > 0, previous, jnp.zeros((), previous.dtype))
    timed = jnp.concatenate([previous, frames], axis=0)
    padded = with_halo(timed, (("fsdp", 2),), 1)
    padded = jnp.pad(padded, ((0, 0), (1, 7), (0, 0), (0, 0)))
    weights = jnp.transpose(full_conv, (1, 2, 0, 3, 4)).reshape(9, 3 * channels, -1)
    pooled = conv_pool(padded, weights)[None]
    pooled = lax.all_to_all(pooled, "tm", split_axis=1, concat_axis=0, tiled=True)
    branch = pooled.astype(jnp.float32).reshape(-1, channels)
    flat_cot = cotangent.reshape(-1, channels)
    grad_terms = []
    for offset in range(3):
        lagged = delayed(pooled, offset).reshape(-1, channels)
        branch = branch + jnp.dot(lagged, full_mix[offset], preferred_element_type=jnp.float32)
        grad_terms.append(
            lax.dot_general(
                lagged, flat_cot, (((0,), (0,)), ((), ())), preferred_element_type=jnp.float32
            )
        )
    encoded = branch.astype(jnp.bfloat16).reshape(pooled.shape)
    mix_grad = scatter_sum(jnp.stack(grad_terms).reshape(-1))
    return (encoded, mix_grad)


def solution(mesh):
    return jax.shard_map(
        local,
        mesh=mesh,
        in_specs=(
            P("tm", None, "fsdp", None),
            P(None, None, None, None, "fsdp"),
            P(None, None, "fsdp"),
            P(None, "tm", "fsdp", None),
        ),
        out_specs=(P(None, "tm", "fsdp", None), P(("tm", "fsdp"))),
        check_vma=False,
    )
```

```python
import jax
import jax.numpy as jnp
from jax import lax
from jax.experimental import pallas as pl
from jax.experimental.pallas import tpu as pltpu
from jax.sharding import PartitionSpec as P

MESH = pl.DeviceIdType.MESH


def from_behind(block, axis, distance):
    devices = range(lax.axis_size(axis))
    route = [(i - distance, i) for i in devices if i - distance in devices]
    return lax.ppermute(block, axis, route)


def with_halo(cells, sides, width):
    for axis, dim in sides:
        count = lax.axis_size(axis)
        ends = count - 1
        head = lax.slice_in_dim(cells, 0, width, axis=dim)
        tail = lax.slice_in_dim(cells, cells.shape[dim] - width, cells.shape[dim], axis=dim)
        cells = jnp.concatenate(
            [
                lax.ppermute(tail, axis, [(i, (i + 1) % count) for i in range(ends)]),
                cells,
                lax.ppermute(head, axis, [((i + 1) % count, i) for i in range(ends)]),
            ],
            axis=dim,
        )
    return cells


def pool_pairs(hidden):
    shaped = hidden.reshape((hidden.shape[0] // 2, 2) + hidden.shape[1:]).astype(jnp.float32)
    return ((shaped[:, 0] + shaped[:, 1]) * 0.5).astype(jnp.bfloat16)


def delayed(block, offset):
    return jnp.pad(block, ((offset, 0), (0, 0), (0, 0), (0, 0)))[: block.shape[0]]


def scatter_kernel(p_ref, o_ref, first, second, summed, s1, r1, s2, r2, l1, l2):
    groups, count = first.shape[0], second.shape[0]
    f, t = lax.axis_index("fsdp"), lax.axis_index("tm")
    barrier = pltpu.get_barrier_semaphore()
    for k in range(1, groups):
        pl.semaphore_signal(
            barrier, inc=1, device_id={"fsdp": lax.rem(f + k, groups)}, device_id_type=MESH
        )
    for k in range(1, count):
        pl.semaphore_signal(
            barrier, inc=1, device_id={"tm": lax.rem(t + k, count)}, device_id_type=MESH
        )
    pl.semaphore_wait(barrier, groups - 1 + count - 1)
    local = pltpu.make_async_copy(p_ref.at[f], first.at[f], l1)
    local.start()
    copies = []
    for k in range(1, groups):
        peer = lax.rem(f + k, groups)
        copy = pltpu.make_async_remote_copy(
            src_ref=p_ref.at[peer],
            dst_ref=first.at[f],
            send_sem=s1.at[k],
            recv_sem=r1.at[k],
            device_id={"fsdp": peer},
            device_id_type=MESH,
        )
        copy.start()
        copies.append(copy)
    local.wait()
    for copy in copies:
        copy.wait()
    summed[...] = jnp.sum(first[...], axis=0)
    local = pltpu.make_async_copy(summed.at[t], second.at[t], l2)
    local.start()
    copies = []
    for k in range(1, count):
        peer = lax.rem(t + k, count)
        copy = pltpu.make_async_remote_copy(
            src_ref=summed.at[peer],
            dst_ref=second.at[t],
            send_sem=s2.at[k],
            recv_sem=r2.at[k],
            device_id={"tm": peer},
            device_id_type=MESH,
        )
        copy.start()
        copies.append(copy)
    local.wait()
    for copy in copies:
        copy.wait()
    o_ref[...] = jnp.sum(second[...], axis=0)


def scatter_sum(partial):
    groups, count = lax.axis_size("fsdp"), lax.axis_size("tm")
    piece = partial.size // (groups * count)
    arranged = jnp.transpose(partial.reshape(count, groups, 1, piece), (1, 0, 2, 3))
    out = pl.pallas_call(
        scatter_kernel,
        out_shape=jax.ShapeDtypeStruct((1, piece), jnp.float32),
        in_specs=[pl.BlockSpec(memory_space=pltpu.VMEM)],
        out_specs=pl.BlockSpec(memory_space=pltpu.VMEM),
        scratch_shapes=[
            pltpu.VMEM((groups, count, 1, piece), jnp.float32),
            pltpu.VMEM((count, 1, piece), jnp.float32),
            pltpu.VMEM((count, 1, piece), jnp.float32),
            pltpu.SemaphoreType.DMA((groups,)),
            pltpu.SemaphoreType.DMA((groups,)),
            pltpu.SemaphoreType.DMA((count,)),
            pltpu.SemaphoreType.DMA((count,)),
            pltpu.SemaphoreType.DMA,
            pltpu.SemaphoreType.DMA,
        ],
        compiler_params=pltpu.CompilerParams(collective_id=1, has_side_effects=True),
    )(arranged)
    return out.reshape(piece)


def conv_pool_kernel(h_ref, x_ref, l_ref, r_ref, w_ref, o_ref, xs_ref):
    height, width, channels = o_ref.shape
    depth = x_ref.shape[0]
    groups = lax.axis_size("fsdp")
    t, f = lax.axis_index("tm"), lax.axis_index("fsdp")
    rows = 8
    zero_rows = jnp.zeros((3, 2 * depth, 1, width, channels), xs_ref.dtype)
    xs_ref[:, :, pl.ds(0, 1)] = zero_rows
    xs_ref[:, :, pl.ds(height + 1, 1)] = zero_rows
    col = lax.broadcasted_iota(jnp.int32, (rows, width, channels), 1)

    def shift(r, carry):
        top = pl.multiple_of(r * rows, rows)
        for q in range(2 * depth):
            earlier = q < depth
            src = h_ref if earlier else x_ref
            block = src[q % depth, pl.ds(top, rows)].astype(jnp.float32)
            lft = l_ref[q, pl.ds(top, rows)].astype(jnp.float32)[:, None, :]
            rgt = r_ref[q, pl.ds(top, rows)].astype(jnp.float32)[:, None, :]
            lok, rok = f > 0, f < groups - 1
            if earlier:
                block = jnp.where(t > 0, block, 0.0)
                lok, rok = lok & (t > 0), rok & (t > 0)
            lft = jnp.where(lok, lft, 0.0)
            rgt = jnp.where(rok, rgt, 0.0)
            moved = [
                jnp.where(col == 0, lft, pltpu.roll(block, 1, 1)),
                block,
                jnp.where(col == width - 1, rgt, pltpu.roll(block, width - 1, 1)),
            ]
            for c in range(3):
                xs_ref[c, q, pl.ds(top + 1, rows)] = moved[c].astype(xs_ref.dtype)
        return carry

    lax.fori_loop(0, height // rows, shift, 0)

    def body(r, carry):
        top = pl.multiple_of(r * rows, rows)
        span = rows * width
        acc = jnp.zeros((2 * span, channels), jnp.float32)
        for b in range(3):
            for c in range(3):
                lhs = jnp.concatenate(
                    [
                        jnp.concatenate(
                            [xs_ref[c, j + a, pl.ds(top + b, rows)] for a in range(3)], axis=-1
                        ).reshape(span, 3 * channels)
                        for j in range(2)
                    ],
                    axis=0,
                )
                acc = acc + jnp.dot(lhs, w_ref[b * 3 + c], preferred_element_type=jnp.float32)
        silu = (acc / (1.0 + jnp.exp(-acc))).astype(jnp.bfloat16).astype(jnp.float32)
        pooled = ((silu[:span] + silu[span:]) * 0.5).astype(o_ref.dtype)
        o_ref[pl.ds(top, rows)] = pooled.reshape(rows, width, channels)
        return carry

    lax.fori_loop(0, height // rows, body, 0)


def conv_pool(halo, frames, left, right, weights):
    depth, height, width, channels = frames.shape
    vmem = pl.BlockSpec(memory_space=pltpu.VMEM)
    flops = 2 * 2 * height * width * weights.shape[0] * weights.shape[1] * channels
    return pl.pallas_call(
        conv_pool_kernel,
        out_shape=jax.ShapeDtypeStruct((height, width, channels), jnp.bfloat16),
        in_specs=[vmem] * 5,
        out_specs=vmem,
        scratch_shapes=[pltpu.VMEM((3, 2 * depth, height + 8, width, channels), frames.dtype)],
        cost_estimate=pl.CostEstimate(
            flops=flops,
            transcendentals=2 * height * width * channels,
            bytes_accessed=4 * frames.size + weights.size * 2 + height * width * channels * 2,
        ),
    )(halo, frames, left, right, weights)


def prologue_kernel(x_ref, w_ref, m_ref, lcol_ref, rcol_ref, halo_ref, wall_ref, mall_ref, left_ref, right_ref, sends, recvs, wsends, wrecvs, msends, mrecvs, lsems, esends, erecvs):
    count, groups = lax.axis_size("tm"), lax.axis_size("fsdp")
    t, f = lax.axis_index("tm"), lax.axis_index("fsdp")
    t_next, t_prev = lax.rem(t + 1, count), lax.rem(t + count - 1, count)
    f_next, f_prev = lax.rem(f + 1, groups), lax.rem(f + groups - 1, groups)
    peers = [(t_next, f), (t_prev, f)] + [(t, lax.rem(f + k, groups)) for k in range(1, groups)]
    peers += [(a, b) for a in (t_next, t_prev) for b in (f_next, f_prev)]
    barrier = pltpu.get_barrier_semaphore()
    for dev in peers:
        pl.semaphore_signal(barrier, inc=1, device_id=dev, device_id_type=MESH)
    pl.semaphore_wait(barrier, len(peers))
    pieces = sends.shape[0]
    rows = x_ref.shape[1] // pieces
    halo = [
        pltpu.make_async_remote_copy(
            src_ref=x_ref.at[:, pl.ds(i * rows, rows)],
            dst_ref=halo_ref.at[:, pl.ds(i * rows, rows)],
            send_sem=sends.at[i], recv_sem=recvs.at[i],
            device_id=(t_next, f), device_id_type=MESH,
        )
        for i in range(pieces)
    ]

    depth = x_ref.shape[0]
    edges = [
        (rcol_ref, left_ref.at[pl.ds(depth, depth)], (t, f_next)),
        (lcol_ref, right_ref.at[pl.ds(depth, depth)], (t, f_prev)),
        (rcol_ref, left_ref.at[pl.ds(0, depth)], (t_next, f_next)),
        (lcol_ref, right_ref.at[pl.ds(0, depth)], (t_next, f_prev)),
    ]
    edges = [
        pltpu.make_async_remote_copy(
            src_ref=src, dst_ref=dst, send_sem=esends.at[i], recv_sem=erecvs.at[i],
            device_id=dev, device_id_type=MESH,
        )
        for i, (src, dst, dev) in enumerate(edges)
    ]
    for copy in edges[:2]:
        copy.start()
    halo = halo + edges[2:]

    @pl.when(t < count - 1)
    def _():
        for copy in halo:
            copy.start()

    copies = []
    locals_ = [
        pltpu.make_async_copy(w_ref, wall_ref.at[f], lsems.at[0]),
        pltpu.make_async_copy(m_ref, mall_ref.at[f], lsems.at[1]),
    ]
    for copy in locals_:
        copy.start()
    for k in range(1, groups):
        dev = (t, lax.rem(f + k, groups))
        for src, dst, ss, rs in ((w_ref, wall_ref, wsends, wrecvs), (m_ref, mall_ref, msends, mrecvs)):
            copy = pltpu.make_async_remote_copy(
                src_ref=src, dst_ref=dst.at[f], send_sem=ss.at[k], recv_sem=rs.at[k],
                device_id=dev, device_id_type=MESH,
            )
            copy.start()
            copies.append(copy)
    for copy in locals_:
        copy.wait()
    for copy in copies + edges[:2]:
        copy.wait()

    @pl.when(t < count - 1)
    def _():
        for copy in halo:
            copy.wait_send()

    @pl.when(t > 0)
    def _():
        for copy in halo:
            copy.wait_recv()


def prologue(frames, conv_shard, mix_shard):
    groups = lax.axis_size("fsdp")
    depth, height, width, channels = frames.shape
    lcol = frames[:, :, 0, :]
    rcol = frames[:, :, width - 1, :]
    edge = jax.ShapeDtypeStruct((2 * depth, height, channels), frames.dtype)
    vmem = pl.BlockSpec(memory_space=pltpu.VMEM)
    return pl.pallas_call(
        prologue_kernel,
        out_shape=(
            jax.ShapeDtypeStruct(frames.shape, frames.dtype),
            jax.ShapeDtypeStruct((groups,) + conv_shard.shape, conv_shard.dtype),
            jax.ShapeDtypeStruct((groups,) + mix_shard.shape, mix_shard.dtype),
            edge,
            edge,
        ),
        in_specs=[vmem] * 5,
        out_specs=(vmem,) * 5,
        scratch_shapes=[
            pltpu.SemaphoreType.DMA((4,)),
            pltpu.SemaphoreType.DMA((4,)),
            pltpu.SemaphoreType.DMA((groups,)),
            pltpu.SemaphoreType.DMA((groups,)),
            pltpu.SemaphoreType.DMA((groups,)),
            pltpu.SemaphoreType.DMA((groups,)),
            pltpu.SemaphoreType.DMA((2,)),
            pltpu.SemaphoreType.DMA((4,)),
            pltpu.SemaphoreType.DMA((4,)),
        ],
        compiler_params=pltpu.CompilerParams(collective_id=2, has_side_effects=True),
    )(frames, conv_shard, mix_shard, lcol, rcol)


def local(frames, conv_weight, mix_weight, cotangent):
    t = lax.axis_index("tm")
    count_frames, height, width, channels = frames.shape
    part = conv_weight.shape[-1]
    conv_shard = jnp.swapaxes(conv_weight, 3, 4).reshape(-1, part, channels)
    mix_shard = jnp.swapaxes(mix_weight, 1, 2)
    previous, wall, mall, left, right = prologue(frames, conv_shard, mix_shard)
    full_conv = jnp.transpose(wall, (1, 3, 0, 2)).reshape(conv_weight.shape[:-1] + (-1,))
    full_mix = jnp.transpose(mall, (1, 3, 0, 2)).reshape(mix_weight.shape[:-1] + (-1,))
    weights = jnp.transpose(full_conv, (1, 2, 0, 3, 4)).reshape(9, 3 * channels, -1)
    pooled = conv_pool(previous, frames, left, right, weights)[None]
    pooled = lax.all_to_all(pooled, "tm", split_axis=1, concat_axis=0, tiled=True)
    branch = pooled.astype(jnp.float32).reshape(-1, channels)
    flat_cot = cotangent.reshape(-1, channels)
    grad_terms = []
    for offset in range(3):
        lagged = delayed(pooled, offset).reshape(-1, channels)
        branch = branch + jnp.dot(lagged, full_mix[offset], preferred_element_type=jnp.float32)
        grad_terms.append(
            lax.dot_general(
                lagged, flat_cot, (((0,), (0,)), ((), ())), preferred_element_type=jnp.float32
            )
        )
    encoded = branch.astype(jnp.bfloat16).reshape(pooled.shape)
    mix_grad = scatter_sum(jnp.stack(grad_terms).reshape(-1))
    return (encoded, mix_grad)


def solution(mesh):
    return jax.shard_map(
        local,
        mesh=mesh,
        in_specs=(
            P("tm", None, "fsdp", None),
            P(None, None, None, None, "fsdp"),
            P(None, None, "fsdp"),
            P(None, "tm", "fsdp", None),
        ),
        out_specs=(P(None, "tm", "fsdp", None), P(("tm", "fsdp"))),
        check_vma=False,
    )
```

```python
import jax
import jax.numpy as jnp
from jax import lax
from jax.experimental import pallas as pl
from jax.experimental.pallas import tpu as pltpu
from jax.sharding import PartitionSpec as P

MESH = pl.DeviceIdType.MESH


def from_behind(block, axis, distance):
    devices = range(lax.axis_size(axis))
    route = [(i - distance, i) for i in devices if i - distance in devices]
    return lax.ppermute(block, axis, route)


def with_halo(cells, sides, width):
    for axis, dim in sides:
        count = lax.axis_size(axis)
        ends = count - 1
        head = lax.slice_in_dim(cells, 0, width, axis=dim)
        tail = lax.slice_in_dim(cells, cells.shape[dim] - width, cells.shape[dim], axis=dim)
        cells = jnp.concatenate(
            [
                lax.ppermute(tail, axis, [(i, (i + 1) % count) for i in range(ends)]),
                cells,
                lax.ppermute(head, axis, [((i + 1) % count, i) for i in range(ends)]),
            ],
            axis=dim,
        )
    return cells


def pool_pairs(hidden):
    shaped = hidden.reshape((hidden.shape[0] // 2, 2) + hidden.shape[1:]).astype(jnp.float32)
    return ((shaped[:, 0] + shaped[:, 1]) * 0.5).astype(jnp.bfloat16)


def delayed(block, offset):
    return jnp.pad(block, ((offset, 0), (0, 0), (0, 0), (0, 0)))[: block.shape[0]]


def scatter_kernel(p_ref, o_ref, first, second, summed, s1, r1, s2, r2, l1, l2):
    groups, count = first.shape[0], second.shape[0]
    f, t = lax.axis_index("fsdp"), lax.axis_index("tm")
    barrier = pltpu.get_barrier_semaphore()
    for k in range(1, groups):
        pl.semaphore_signal(
            barrier, inc=1, device_id={"fsdp": lax.rem(f + k, groups)}, device_id_type=MESH
        )
    for k in range(1, count):
        pl.semaphore_signal(
            barrier, inc=1, device_id={"tm": lax.rem(t + k, count)}, device_id_type=MESH
        )
    pl.semaphore_wait(barrier, groups - 1 + count - 1)
    local = pltpu.make_async_copy(p_ref.at[f], first.at[f], l1)
    local.start()
    copies = []
    for k in range(1, groups):
        peer = lax.rem(f + k, groups)
        copy = pltpu.make_async_remote_copy(
            src_ref=p_ref.at[peer],
            dst_ref=first.at[f],
            send_sem=s1.at[k],
            recv_sem=r1.at[k],
            device_id={"fsdp": peer},
            device_id_type=MESH,
        )
        copy.start()
        copies.append(copy)
    local.wait()
    for copy in copies:
        copy.wait()
    summed[...] = jnp.sum(first[...], axis=0)
    local = pltpu.make_async_copy(summed.at[t], second.at[t], l2)
    local.start()
    copies = []
    for k in range(1, count):
        peer = lax.rem(t + k, count)
        copy = pltpu.make_async_remote_copy(
            src_ref=summed.at[peer],
            dst_ref=second.at[t],
            send_sem=s2.at[k],
            recv_sem=r2.at[k],
            device_id={"tm": peer},
            device_id_type=MESH,
        )
        copy.start()
        copies.append(copy)
    local.wait()
    for copy in copies:
        copy.wait()
    o_ref[...] = jnp.sum(second[...], axis=0)


def scatter_sum(partial):
    groups, count = lax.axis_size("fsdp"), lax.axis_size("tm")
    piece = partial.size // (groups * count)
    arranged = jnp.transpose(partial.reshape(count, groups, 1, piece), (1, 0, 2, 3))
    out = pl.pallas_call(
        scatter_kernel,
        out_shape=jax.ShapeDtypeStruct((1, piece), jnp.float32),
        in_specs=[pl.BlockSpec(memory_space=pltpu.VMEM)],
        out_specs=pl.BlockSpec(memory_space=pltpu.VMEM),
        scratch_shapes=[
            pltpu.VMEM((groups, count, 1, piece), jnp.float32),
            pltpu.VMEM((count, 1, piece), jnp.float32),
            pltpu.VMEM((count, 1, piece), jnp.float32),
            pltpu.SemaphoreType.DMA((groups,)),
            pltpu.SemaphoreType.DMA((groups,)),
            pltpu.SemaphoreType.DMA((count,)),
            pltpu.SemaphoreType.DMA((count,)),
            pltpu.SemaphoreType.DMA,
            pltpu.SemaphoreType.DMA,
        ],
        compiler_params=pltpu.CompilerParams(collective_id=1, has_side_effects=True),
    )(arranged)
    return out.reshape(piece)


def conv_pool_kernel(h_ref, x_ref, l_ref, r_ref, w_ref, o_ref, xs_ref, pooled_ref, sends, recvs, local_sem):
    height, width, channels = pooled_ref.shape
    count, per_dev = o_ref.shape[0], o_ref.shape[1]
    me = lax.axis_index("tm")
    barrier = pltpu.get_barrier_semaphore()
    for k in range(1, count):
        pl.semaphore_signal(
            barrier, inc=1, device_id={"tm": lax.rem(me + k, count)}, device_id_type=MESH
        )
    depth = x_ref.shape[0]
    groups = lax.axis_size("fsdp")
    t, f = lax.axis_index("tm"), lax.axis_index("fsdp")
    rows = 8
    zero_rows = jnp.zeros((3, 2 * depth, 1, width, channels), xs_ref.dtype)
    xs_ref[:, :, pl.ds(0, 1)] = zero_rows
    xs_ref[:, :, pl.ds(height + 1, 1)] = zero_rows
    col = lax.broadcasted_iota(jnp.int32, (rows, width, channels), 1)

    def shift(r, carry):
        top = pl.multiple_of(r * rows, rows)
        for q in range(2 * depth):
            earlier = q < depth
            src = h_ref if earlier else x_ref
            block = src[q % depth, pl.ds(top, rows)].astype(jnp.float32)
            lft = l_ref[q, pl.ds(top, rows)].astype(jnp.float32)[:, None, :]
            rgt = r_ref[q, pl.ds(top, rows)].astype(jnp.float32)[:, None, :]
            lok, rok = f > 0, f < groups - 1
            if earlier:
                block = jnp.where(t > 0, block, 0.0)
                lok, rok = lok & (t > 0), rok & (t > 0)
            lft = jnp.where(lok, lft, 0.0)
            rgt = jnp.where(rok, rgt, 0.0)
            moved = [
                jnp.where(col == 0, lft, pltpu.roll(block, 1, 1)),
                block,
                jnp.where(col == width - 1, rgt, pltpu.roll(block, width - 1, 1)),
            ]
            for c in range(3):
                xs_ref[c, q, pl.ds(top + 1, rows)] = moved[c].astype(xs_ref.dtype)
        return carry

    lax.fori_loop(0, height // rows, shift, 0)
    pl.semaphore_wait(barrier, count - 1)

    def body(r, carry):
        top = pl.multiple_of(r * rows, rows)
        span = rows * width
        acc = jnp.zeros((2 * span, channels), jnp.float32)
        for b in range(3):
            for c in range(3):
                lhs = jnp.concatenate(
                    [
                        jnp.concatenate(
                            [xs_ref[c, j + a, pl.ds(top + b, rows)] for a in range(3)], axis=-1
                        ).reshape(span, 3 * channels)
                        for j in range(2)
                    ],
                    axis=0,
                )
                acc = acc + jnp.dot(lhs, w_ref[b * 3 + c], preferred_element_type=jnp.float32)
        silu = (acc / (1.0 + jnp.exp(-acc))).astype(jnp.bfloat16).astype(jnp.float32)
        pooled = ((silu[:span] + silu[span:]) * 0.5).astype(o_ref.dtype)
        pooled_ref[pl.ds(top, rows)] = pooled.reshape(rows, width, channels)
        for i in range(rows // per_dev):
            dest = r * (rows // per_dev) + i
            src = pooled_ref.at[pl.ds(top + i * per_dev, per_dev)]

            @pl.when(dest != me)
            def _():
                pltpu.make_async_remote_copy(
                    src_ref=src, dst_ref=o_ref.at[me], send_sem=sends.at[dest],
                    recv_sem=recvs.at[me], device_id={"tm": dest}, device_id_type=MESH,
                ).start()

            @pl.when(dest == me)
            def _():
                local = pltpu.make_async_copy(src, o_ref.at[me], local_sem)
                local.start()
                local.wait()

        return carry

    lax.fori_loop(0, height // rows, body, 0)

    @pl.loop(1, count)
    def _(k):
        peer = lax.rem(me + k, count)
        copy = pltpu.make_async_remote_copy(
            src_ref=pooled_ref.at[pl.ds(0, per_dev)], dst_ref=o_ref.at[peer],
            send_sem=sends.at[peer], recv_sem=recvs.at[peer],
            device_id={"tm": peer}, device_id_type=MESH,
        )
        copy.wait_send()
        copy.wait_recv()


def conv_pool(halo, frames, left, right, weights):
    depth, height, width, channels = frames.shape
    count = lax.axis_size("tm")
    vmem = pl.BlockSpec(memory_space=pltpu.VMEM)
    flops = 2 * 2 * height * width * weights.shape[0] * weights.shape[1] * channels
    return pl.pallas_call(
        conv_pool_kernel,
        out_shape=jax.ShapeDtypeStruct((count, height // count, width, channels), jnp.bfloat16),
        in_specs=[vmem] * 5,
        out_specs=vmem,
        scratch_shapes=[
            pltpu.VMEM((3, 2 * depth, height + 8, width, channels), frames.dtype),
            pltpu.VMEM((height, width, channels), jnp.bfloat16),
            pltpu.SemaphoreType.DMA((count,)),
            pltpu.SemaphoreType.DMA((count,)),
            pltpu.SemaphoreType.DMA,
        ],
        cost_estimate=pl.CostEstimate(
            flops=flops,
            transcendentals=2 * height * width * channels,
            bytes_accessed=4 * frames.size + weights.size * 2 + height * width * channels * 2,
        ),
        compiler_params=pltpu.CompilerParams(collective_id=3, has_side_effects=True),
    )(halo, frames, left, right, weights)


def prologue_kernel(x_ref, w_ref, m_ref, lcol_ref, rcol_ref, halo_ref, wall_ref, mall_ref, left_ref, right_ref, sends, recvs, wsends, wrecvs, msends, mrecvs, lsems, esends, erecvs):
    count, groups = lax.axis_size("tm"), lax.axis_size("fsdp")
    t, f = lax.axis_index("tm"), lax.axis_index("fsdp")
    t_next, t_prev = lax.rem(t + 1, count), lax.rem(t + count - 1, count)
    f_next, f_prev = lax.rem(f + 1, groups), lax.rem(f + groups - 1, groups)
    peers = [(t_next, f), (t_prev, f)] + [(t, lax.rem(f + k, groups)) for k in range(1, groups)]
    peers += [(a, b) for a in (t_next, t_prev) for b in (f_next, f_prev)]
    barrier = pltpu.get_barrier_semaphore()
    for dev in peers:
        pl.semaphore_signal(barrier, inc=1, device_id=dev, device_id_type=MESH)
    pl.semaphore_wait(barrier, len(peers))
    pieces = sends.shape[0]
    rows = x_ref.shape[1] // pieces
    halo = [
        pltpu.make_async_remote_copy(
            src_ref=x_ref.at[:, pl.ds(i * rows, rows)],
            dst_ref=halo_ref.at[:, pl.ds(i * rows, rows)],
            send_sem=sends.at[i], recv_sem=recvs.at[i],
            device_id=(t_next, f), device_id_type=MESH,
        )
        for i in range(pieces)
    ]

    depth = x_ref.shape[0]
    edges = [
        (rcol_ref, left_ref.at[pl.ds(depth, depth)], (t, f_next)),
        (lcol_ref, right_ref.at[pl.ds(depth, depth)], (t, f_prev)),
        (rcol_ref, left_ref.at[pl.ds(0, depth)], (t_next, f_next)),
        (lcol_ref, right_ref.at[pl.ds(0, depth)], (t_next, f_prev)),
    ]
    edges = [
        pltpu.make_async_remote_copy(
            src_ref=src, dst_ref=dst, send_sem=esends.at[i], recv_sem=erecvs.at[i],
            device_id=dev, device_id_type=MESH,
        )
        for i, (src, dst, dev) in enumerate(edges)
    ]
    for copy in edges[:2]:
        copy.start()
    halo = halo + edges[2:]

    @pl.when(t < count - 1)
    def _():
        for copy in halo:
            copy.start()

    copies = []
    locals_ = [
        pltpu.make_async_copy(w_ref, wall_ref.at[f], lsems.at[0]),
        pltpu.make_async_copy(m_ref, mall_ref.at[f], lsems.at[1]),
    ]
    for copy in locals_:
        copy.start()
    for k in range(1, groups):
        dev = (t, lax.rem(f + k, groups))
        for src, dst, ss, rs in ((w_ref, wall_ref, wsends, wrecvs), (m_ref, mall_ref, msends, mrecvs)):
            copy = pltpu.make_async_remote_copy(
                src_ref=src, dst_ref=dst.at[f], send_sem=ss.at[k], recv_sem=rs.at[k],
                device_id=dev, device_id_type=MESH,
            )
            copy.start()
            copies.append(copy)
    for copy in locals_:
        copy.wait()
    for copy in copies + edges[:2]:
        copy.wait()

    @pl.when(t < count - 1)
    def _():
        for copy in halo:
            copy.wait_send()

    @pl.when(t > 0)
    def _():
        for copy in halo:
            copy.wait_recv()


def prologue(frames, conv_shard, mix_shard):
    groups = lax.axis_size("fsdp")
    depth, height, width, channels = frames.shape
    lcol = frames[:, :, 0, :]
    rcol = frames[:, :, width - 1, :]
    edge = jax.ShapeDtypeStruct((2 * depth, height, channels), frames.dtype)
    vmem = pl.BlockSpec(memory_space=pltpu.VMEM)
    return pl.pallas_call(
        prologue_kernel,
        out_shape=(
            jax.ShapeDtypeStruct(frames.shape, frames.dtype),
            jax.ShapeDtypeStruct((groups,) + conv_shard.shape, conv_shard.dtype),
            jax.ShapeDtypeStruct((groups,) + mix_shard.shape, mix_shard.dtype),
            edge,
            edge,
        ),
        in_specs=[vmem] * 5,
        out_specs=(vmem,) * 5,
        scratch_shapes=[
            pltpu.SemaphoreType.DMA((4,)),
            pltpu.SemaphoreType.DMA((4,)),
            pltpu.SemaphoreType.DMA((groups,)),
            pltpu.SemaphoreType.DMA((groups,)),
            pltpu.SemaphoreType.DMA((groups,)),
            pltpu.SemaphoreType.DMA((groups,)),
            pltpu.SemaphoreType.DMA((2,)),
            pltpu.SemaphoreType.DMA((4,)),
            pltpu.SemaphoreType.DMA((4,)),
        ],
        compiler_params=pltpu.CompilerParams(collective_id=2, has_side_effects=True),
    )(frames, conv_shard, mix_shard, lcol, rcol)


def local(frames, conv_weight, mix_weight, cotangent):
    t = lax.axis_index("tm")
    count_frames, height, width, channels = frames.shape
    part = conv_weight.shape[-1]
    conv_shard = jnp.swapaxes(conv_weight, 3, 4).reshape(-1, part, channels)
    mix_shard = jnp.swapaxes(mix_weight, 1, 2)
    previous, wall, mall, left, right = prologue(frames, conv_shard, mix_shard)
    full_conv = jnp.transpose(wall, (1, 3, 0, 2)).reshape(conv_weight.shape[:-1] + (-1,))
    full_mix = jnp.transpose(mall, (1, 3, 0, 2)).reshape(mix_weight.shape[:-1] + (-1,))
    weights = jnp.transpose(full_conv, (1, 2, 0, 3, 4)).reshape(9, 3 * channels, -1)
    pooled = conv_pool(previous, frames, left, right, weights)
    branch = pooled.astype(jnp.float32).reshape(-1, channels)
    flat_cot = cotangent.reshape(-1, channels)
    grad_terms = []
    for offset in range(3):
        lagged = delayed(pooled, offset).reshape(-1, channels)
        branch = branch + jnp.dot(lagged, full_mix[offset], preferred_element_type=jnp.float32)
        grad_terms.append(
            lax.dot_general(
                lagged, flat_cot, (((0,), (0,)), ((), ())), preferred_element_type=jnp.float32
            )
        )
    encoded = branch.astype(jnp.bfloat16).reshape(pooled.shape)
    mix_grad = scatter_sum(jnp.stack(grad_terms).reshape(-1))
    return (encoded, mix_grad)


def solution(mesh):
    return jax.shard_map(
        local,
        mesh=mesh,
        in_specs=(
            P("tm", None, "fsdp", None),
            P(None, None, None, None, "fsdp"),
            P(None, None, "fsdp"),
            P(None, "tm", "fsdp", None),
        ),
        out_specs=(P(None, "tm", "fsdp", None), P(("tm", "fsdp"))),
        check_vma=False,
    )
```

```python
import jax
import jax.numpy as jnp
from jax import lax
from jax.experimental import pallas as pl
from jax.experimental.pallas import tpu as pltpu
from jax.sharding import PartitionSpec as P

MESH = pl.DeviceIdType.MESH


def from_behind(block, axis, distance):
    devices = range(lax.axis_size(axis))
    route = [(i - distance, i) for i in devices if i - distance in devices]
    return lax.ppermute(block, axis, route)


def with_halo(cells, sides, width):
    for axis, dim in sides:
        count = lax.axis_size(axis)
        ends = count - 1
        head = lax.slice_in_dim(cells, 0, width, axis=dim)
        tail = lax.slice_in_dim(cells, cells.shape[dim] - width, cells.shape[dim], axis=dim)
        cells = jnp.concatenate(
            [
                lax.ppermute(tail, axis, [(i, (i + 1) % count) for i in range(ends)]),
                cells,
                lax.ppermute(head, axis, [((i + 1) % count, i) for i in range(ends)]),
            ],
            axis=dim,
        )
    return cells


def pool_pairs(hidden):
    shaped = hidden.reshape((hidden.shape[0] // 2, 2) + hidden.shape[1:]).astype(jnp.float32)
    return ((shaped[:, 0] + shaped[:, 1]) * 0.5).astype(jnp.bfloat16)


def delayed(block, offset):
    return jnp.pad(block, ((offset, 0), (0, 0), (0, 0), (0, 0)))[: block.shape[0]]


def scatter_kernel(p_ref, o_ref, first, second, summed, s1, r1, s2, r2, l1, l2):
    groups, count = first.shape[0], second.shape[0]
    f, t = lax.axis_index("fsdp"), lax.axis_index("tm")
    barrier = pltpu.get_barrier_semaphore()
    for k in range(1, groups):
        pl.semaphore_signal(
            barrier, inc=1, device_id={"fsdp": lax.rem(f + k, groups)}, device_id_type=MESH
        )
    for k in range(1, count):
        pl.semaphore_signal(
            barrier, inc=1, device_id={"tm": lax.rem(t + k, count)}, device_id_type=MESH
        )
    pl.semaphore_wait(barrier, groups - 1 + count - 1)
    local = pltpu.make_async_copy(p_ref.at[f], first.at[f], l1)
    local.start()
    copies = []
    for k in range(1, groups):
        peer = lax.rem(f + k, groups)
        copy = pltpu.make_async_remote_copy(
            src_ref=p_ref.at[peer],
            dst_ref=first.at[f],
            send_sem=s1.at[k],
            recv_sem=r1.at[k],
            device_id={"fsdp": peer},
            device_id_type=MESH,
        )
        copy.start()
        copies.append(copy)
    local.wait()
    for copy in copies:
        copy.wait()
    summed[...] = jnp.sum(first[...], axis=0)
    local = pltpu.make_async_copy(summed.at[t], second.at[t], l2)
    local.start()
    copies = []
    for k in range(1, count):
        peer = lax.rem(t + k, count)
        copy = pltpu.make_async_remote_copy(
            src_ref=summed.at[peer],
            dst_ref=second.at[t],
            send_sem=s2.at[k],
            recv_sem=r2.at[k],
            device_id={"tm": peer},
            device_id_type=MESH,
        )
        copy.start()
        copies.append(copy)
    local.wait()
    for copy in copies:
        copy.wait()
    o_ref[...] = jnp.sum(second[...], axis=0)


def scatter_sum(partial):
    groups, count = lax.axis_size("fsdp"), lax.axis_size("tm")
    piece = partial.size // (groups * count)
    arranged = jnp.transpose(partial.reshape(count, groups, 1, piece), (1, 0, 2, 3))
    out = pl.pallas_call(
        scatter_kernel,
        out_shape=jax.ShapeDtypeStruct((1, piece), jnp.float32),
        in_specs=[pl.BlockSpec(memory_space=pltpu.VMEM)],
        out_specs=pl.BlockSpec(memory_space=pltpu.VMEM),
        scratch_shapes=[
            pltpu.VMEM((groups, count, 1, piece), jnp.float32),
            pltpu.VMEM((count, 1, piece), jnp.float32),
            pltpu.VMEM((count, 1, piece), jnp.float32),
            pltpu.SemaphoreType.DMA((groups,)),
            pltpu.SemaphoreType.DMA((groups,)),
            pltpu.SemaphoreType.DMA((count,)),
            pltpu.SemaphoreType.DMA((count,)),
            pltpu.SemaphoreType.DMA,
            pltpu.SemaphoreType.DMA,
        ],
        compiler_params=pltpu.CompilerParams(collective_id=1, has_side_effects=True),
    )(arranged)
    return out.reshape(piece)


def conv_pool_kernel(h_ref, x_ref, l_ref, r_ref, w_ref, o_ref, xs_ref, pooled_ref, sends, recvs, local_sem):
    height, width, channels = pooled_ref.shape
    count, per_dev = o_ref.shape[0], o_ref.shape[1]
    me = lax.axis_index("tm")
    barrier = pltpu.get_barrier_semaphore()
    for k in range(1, count):
        pl.semaphore_signal(
            barrier, inc=1, device_id={"tm": lax.rem(me + k, count)}, device_id_type=MESH
        )
    depth = x_ref.shape[0]
    groups = lax.axis_size("fsdp")
    t, f = lax.axis_index("tm"), lax.axis_index("fsdp")
    rows = 8
    zero_rows = jnp.zeros((3, 2 * depth, 1, width, channels), xs_ref.dtype)
    xs_ref[:, :, pl.ds(0, 1)] = zero_rows
    xs_ref[:, :, pl.ds(height + 1, 1)] = zero_rows
    col = lax.broadcasted_iota(jnp.int32, (rows, width, channels), 1)

    def shift(r, carry):
        top = pl.multiple_of(r * rows, rows)
        for q in range(2 * depth):
            earlier = q < depth
            src = h_ref if earlier else x_ref
            block = src[q % depth, pl.ds(top, rows)].astype(jnp.float32)
            lft = l_ref[q, pl.ds(top, rows)].astype(jnp.float32)[:, None, :]
            rgt = r_ref[q, pl.ds(top, rows)].astype(jnp.float32)[:, None, :]
            lok, rok = f > 0, f < groups - 1
            if earlier:
                block = jnp.where(t > 0, block, 0.0)
                lok, rok = lok & (t > 0), rok & (t > 0)
            lft = jnp.where(lok, lft, 0.0)
            rgt = jnp.where(rok, rgt, 0.0)
            moved = [
                jnp.where(col == 0, lft, pltpu.roll(block, 1, 1)),
                block,
                jnp.where(col == width - 1, rgt, pltpu.roll(block, width - 1, 1)),
            ]
            for c in range(3):
                xs_ref[c, q, pl.ds(top + 1, rows)] = moved[c].astype(xs_ref.dtype)
        return carry

    lax.fori_loop(0, height // rows, shift, 0)
    pl.semaphore_wait(barrier, count - 1)

    def body(r, carry):
        top = pl.multiple_of(r * rows, rows)
        span = rows * width
        acc = jnp.zeros((2 * span, channels), jnp.float32)
        for b in range(3):
            for c in range(3):
                lhs = jnp.concatenate(
                    [
                        jnp.concatenate(
                            [xs_ref[c, j + a, pl.ds(top + b, rows)] for a in range(3)], axis=-1
                        ).reshape(span, 3 * channels)
                        for j in range(2)
                    ],
                    axis=0,
                )
                acc = acc + lax.dot_general(
                    lhs, w_ref[b * 3 + c], (((1,), (1,)), ((), ())),
                    preferred_element_type=jnp.float32,
                )
        silu = (acc / (1.0 + jnp.exp(-acc))).astype(jnp.bfloat16).astype(jnp.float32)
        pooled = ((silu[:span] + silu[span:]) * 0.5).astype(o_ref.dtype)
        pooled_ref[pl.ds(top, rows)] = pooled.reshape(rows, width, channels)
        for i in range(rows // per_dev):
            dest = r * (rows // per_dev) + i
            src = pooled_ref.at[pl.ds(top + i * per_dev, per_dev)]

            @pl.when(dest != me)
            def _():
                pltpu.make_async_remote_copy(
                    src_ref=src, dst_ref=o_ref.at[me], send_sem=sends.at[dest],
                    recv_sem=recvs.at[me], device_id={"tm": dest}, device_id_type=MESH,
                ).start()

            @pl.when(dest == me)
            def _():
                local = pltpu.make_async_copy(src, o_ref.at[me], local_sem)
                local.start()
                local.wait()

        return carry

    lax.fori_loop(0, height // rows, body, 0)

    @pl.loop(1, count)
    def _(k):
        peer = lax.rem(me + k, count)
        copy = pltpu.make_async_remote_copy(
            src_ref=pooled_ref.at[pl.ds(0, per_dev)], dst_ref=o_ref.at[peer],
            send_sem=sends.at[peer], recv_sem=recvs.at[peer],
            device_id={"tm": peer}, device_id_type=MESH,
        )
        copy.wait_send()
        copy.wait_recv()


def conv_pool(halo, frames, left, right, weights):
    depth, height, width, channels = frames.shape
    count = lax.axis_size("tm")
    vmem = pl.BlockSpec(memory_space=pltpu.VMEM)
    flops = 2 * 2 * height * width * weights.shape[0] * weights.shape[2] * channels
    return pl.pallas_call(
        conv_pool_kernel,
        out_shape=jax.ShapeDtypeStruct((count, height // count, width, channels), jnp.bfloat16),
        in_specs=[vmem] * 5,
        out_specs=vmem,
        scratch_shapes=[
            pltpu.VMEM((3, 2 * depth, height + 8, width, channels), frames.dtype),
            pltpu.VMEM((height, width, channels), jnp.bfloat16),
            pltpu.SemaphoreType.DMA((count,)),
            pltpu.SemaphoreType.DMA((count,)),
            pltpu.SemaphoreType.DMA,
        ],
        cost_estimate=pl.CostEstimate(
            flops=flops,
            transcendentals=2 * height * width * channels,
            bytes_accessed=4 * frames.size + weights.size * 2 + height * width * channels * 2,
        ),
        compiler_params=pltpu.CompilerParams(collective_id=3, has_side_effects=True),
    )(halo, frames, left, right, weights)


def prologue_kernel(x_ref, w_ref, m_ref, lcol_ref, rcol_ref, halo_ref, wall_ref, mall_ref, left_ref, right_ref, sends, recvs, wsends, wrecvs, msends, mrecvs, lsems, esends, erecvs):
    count, groups = lax.axis_size("tm"), lax.axis_size("fsdp")
    t, f = lax.axis_index("tm"), lax.axis_index("fsdp")
    t_next, t_prev = lax.rem(t + 1, count), lax.rem(t + count - 1, count)
    f_next, f_prev = lax.rem(f + 1, groups), lax.rem(f + groups - 1, groups)
    peers = [(t_next, f), (t_prev, f)] + [(t, lax.rem(f + k, groups)) for k in range(1, groups)]
    peers += [(a, b) for a in (t_next, t_prev) for b in (f_next, f_prev)]
    barrier = pltpu.get_barrier_semaphore()
    for dev in peers:
        pl.semaphore_signal(barrier, inc=1, device_id=dev, device_id_type=MESH)
    pl.semaphore_wait(barrier, len(peers))
    pieces = sends.shape[0]
    rows = x_ref.shape[1] // pieces
    halo = [
        pltpu.make_async_remote_copy(
            src_ref=x_ref.at[:, pl.ds(i * rows, rows)],
            dst_ref=halo_ref.at[:, pl.ds(i * rows, rows)],
            send_sem=sends.at[i], recv_sem=recvs.at[i],
            device_id=(t_next, f), device_id_type=MESH,
        )
        for i in range(pieces)
    ]

    depth = x_ref.shape[0]
    edges = [
        (rcol_ref, left_ref.at[pl.ds(depth, depth)], (t, f_next)),
        (lcol_ref, right_ref.at[pl.ds(depth, depth)], (t, f_prev)),
        (rcol_ref, left_ref.at[pl.ds(0, depth)], (t_next, f_next)),
        (lcol_ref, right_ref.at[pl.ds(0, depth)], (t_next, f_prev)),
    ]
    edges = [
        pltpu.make_async_remote_copy(
            src_ref=src, dst_ref=dst, send_sem=esends.at[i], recv_sem=erecvs.at[i],
            device_id=dev, device_id_type=MESH,
        )
        for i, (src, dst, dev) in enumerate(edges)
    ]
    for copy in edges[:2]:
        copy.start()
    halo = halo + edges[2:]

    @pl.when(t < count - 1)
    def _():
        for copy in halo:
            copy.start()

    copies = []
    locals_ = [
        pltpu.make_async_copy(w_ref, wall_ref.at[f], lsems.at[0]),
        pltpu.make_async_copy(m_ref, mall_ref.at[f], lsems.at[1]),
    ]
    for copy in locals_:
        copy.start()
    for k in range(1, groups):
        dev = (t, lax.rem(f + k, groups))
        for src, dst, ss, rs in ((w_ref, wall_ref, wsends, wrecvs), (m_ref, mall_ref, msends, mrecvs)):
            copy = pltpu.make_async_remote_copy(
                src_ref=src, dst_ref=dst.at[f], send_sem=ss.at[k], recv_sem=rs.at[k],
                device_id=dev, device_id_type=MESH,
            )
            copy.start()
            copies.append(copy)
    for copy in locals_:
        copy.wait()
    for copy in copies + edges[:2]:
        copy.wait()

    @pl.when(t < count - 1)
    def _():
        for copy in halo:
            copy.wait_send()

    @pl.when(t > 0)
    def _():
        for copy in halo:
            copy.wait_recv()


def prologue(frames, conv_shard, mix_shard):
    groups = lax.axis_size("fsdp")
    depth, height, width, channels = frames.shape
    lcol = frames[:, :, 0, :]
    rcol = frames[:, :, width - 1, :]
    edge = jax.ShapeDtypeStruct((2 * depth, height, channels), frames.dtype)
    vmem = pl.BlockSpec(memory_space=pltpu.VMEM)
    return pl.pallas_call(
        prologue_kernel,
        out_shape=(
            jax.ShapeDtypeStruct(frames.shape, frames.dtype),
            jax.ShapeDtypeStruct((groups,) + conv_shard.shape, conv_shard.dtype),
            jax.ShapeDtypeStruct((groups,) + mix_shard.shape, mix_shard.dtype),
            edge,
            edge,
        ),
        in_specs=[vmem] * 5,
        out_specs=(vmem,) * 5,
        scratch_shapes=[
            pltpu.SemaphoreType.DMA((4,)),
            pltpu.SemaphoreType.DMA((4,)),
            pltpu.SemaphoreType.DMA((groups,)),
            pltpu.SemaphoreType.DMA((groups,)),
            pltpu.SemaphoreType.DMA((groups,)),
            pltpu.SemaphoreType.DMA((groups,)),
            pltpu.SemaphoreType.DMA((2,)),
            pltpu.SemaphoreType.DMA((4,)),
            pltpu.SemaphoreType.DMA((4,)),
        ],
        compiler_params=pltpu.CompilerParams(collective_id=2, has_side_effects=True),
    )(frames, conv_shard, mix_shard, lcol, rcol)


def local(frames, conv_weight, mix_weight, cotangent):
    t = lax.axis_index("tm")
    count_frames, height, width, channels = frames.shape
    part = conv_weight.shape[-1]
    conv_shard = jnp.swapaxes(conv_weight, 3, 4).reshape(-1, part, channels)
    mix_shard = jnp.swapaxes(mix_weight, 1, 2)
    previous, wall, mall, left, right = prologue(frames, conv_shard, mix_shard)
    full_mix = jnp.transpose(mall, (1, 3, 0, 2)).reshape(mix_weight.shape[:-1] + (-1,))
    groups = wall.shape[0]
    weights = wall.reshape(groups, 3, 9, part, channels)
    weights = jnp.transpose(weights, (2, 0, 3, 1, 4)).reshape(9, groups * part, 3 * channels)
    pooled = conv_pool(previous, frames, left, right, weights)
    branch = pooled.astype(jnp.float32).reshape(-1, channels)
    flat_cot = cotangent.reshape(-1, channels)
    grad_terms = []
    for offset in range(3):
        lagged = delayed(pooled, offset).reshape(-1, channels)
        branch = branch + jnp.dot(lagged, full_mix[offset], preferred_element_type=jnp.float32)
        grad_terms.append(
            lax.dot_general(
                lagged, flat_cot, (((0,), (0,)), ((), ())), preferred_element_type=jnp.float32
            )
        )
    encoded = branch.astype(jnp.bfloat16).reshape(pooled.shape)
    mix_grad = scatter_sum(jnp.stack(grad_terms).reshape(-1))
    return (encoded, mix_grad)


def solution(mesh):
    return jax.shard_map(
        local,
        mesh=mesh,
        in_specs=(
            P("tm", None, "fsdp", None),
            P(None, None, None, None, "fsdp"),
            P(None, None, "fsdp"),
            P(None, "tm", "fsdp", None),
        ),
        out_specs=(P(None, "tm", "fsdp", None), P(("tm", "fsdp"))),
        check_vma=False,
    )
```

```python
import jax
import jax.numpy as jnp
from jax import lax
from jax.experimental import pallas as pl
from jax.experimental.pallas import tpu as pltpu
from jax.sharding import PartitionSpec as P

MESH = pl.DeviceIdType.MESH


def from_behind(block, axis, distance):
    devices = range(lax.axis_size(axis))
    route = [(i - distance, i) for i in devices if i - distance in devices]
    return lax.ppermute(block, axis, route)


def with_halo(cells, sides, width):
    for axis, dim in sides:
        count = lax.axis_size(axis)
        ends = count - 1
        head = lax.slice_in_dim(cells, 0, width, axis=dim)
        tail = lax.slice_in_dim(cells, cells.shape[dim] - width, cells.shape[dim], axis=dim)
        cells = jnp.concatenate(
            [
                lax.ppermute(tail, axis, [(i, (i + 1) % count) for i in range(ends)]),
                cells,
                lax.ppermute(head, axis, [((i + 1) % count, i) for i in range(ends)]),
            ],
            axis=dim,
        )
    return cells


def pool_pairs(hidden):
    shaped = hidden.reshape((hidden.shape[0] // 2, 2) + hidden.shape[1:]).astype(jnp.float32)
    return ((shaped[:, 0] + shaped[:, 1]) * 0.5).astype(jnp.bfloat16)


def delayed(block, offset):
    return jnp.pad(block, ((offset, 0), (0, 0), (0, 0), (0, 0)))[: block.shape[0]]


def scatter_kernel(p_ref, o_ref, first, second, summed, s1, r1, s2, r2, l1, l2):
    count, groups = first.shape[0], second.shape[0]
    t, f = lax.axis_index("tm"), lax.axis_index("fsdp")
    barrier = pltpu.get_barrier_semaphore()
    for k in range(1, count):
        pl.semaphore_signal(
            barrier, inc=1, device_id={"tm": lax.rem(t + k, count)}, device_id_type=MESH
        )
    for k in range(1, groups):
        pl.semaphore_signal(
            barrier, inc=1, device_id={"fsdp": lax.rem(f + k, groups)}, device_id_type=MESH
        )
    pl.semaphore_wait(barrier, groups - 1 + count - 1)
    local = pltpu.make_async_copy(p_ref.at[t], first.at[t], l1)
    local.start()
    copies = []
    for k in range(1, count):
        peer = lax.rem(t + k, count)
        copy = pltpu.make_async_remote_copy(
            src_ref=p_ref.at[peer], dst_ref=first.at[t], send_sem=s1.at[k], recv_sem=r1.at[k],
            device_id={"tm": peer}, device_id_type=MESH,
        )
        copy.start()
        copies.append(copy)
    local.wait()
    for copy in copies:
        copy.wait()
    summed[...] = jnp.sum(first[...], axis=0)
    local = pltpu.make_async_copy(summed, second.at[f], l2)
    local.start()
    copies = []
    for k in range(1, groups):
        peer = lax.rem(f + k, groups)
        copy = pltpu.make_async_remote_copy(
            src_ref=summed, dst_ref=second.at[f], send_sem=s2.at[k], recv_sem=r2.at[k],
            device_id={"fsdp": peer}, device_id_type=MESH,
        )
        copy.start()
        copies.append(copy)
    local.wait()
    for copy in copies:
        copy.wait()
    o_ref[...] = jnp.sum(second[...], axis=0)


def scatter_sum(partial):
    groups, count = lax.axis_size("fsdp"), lax.axis_size("tm")
    rows = partial.size // (count * 128)
    out = pl.pallas_call(
        scatter_kernel,
        out_shape=jax.ShapeDtypeStruct((rows, 128), jnp.float32),
        in_specs=[pl.BlockSpec(memory_space=pltpu.VMEM)],
        out_specs=pl.BlockSpec(memory_space=pltpu.VMEM),
        scratch_shapes=[
            pltpu.VMEM((count, rows, 128), jnp.float32),
            pltpu.VMEM((groups, rows, 128), jnp.float32),
            pltpu.VMEM((rows, 128), jnp.float32),
            pltpu.SemaphoreType.DMA((count,)),
            pltpu.SemaphoreType.DMA((count,)),
            pltpu.SemaphoreType.DMA((groups,)),
            pltpu.SemaphoreType.DMA((groups,)),
            pltpu.SemaphoreType.DMA,
            pltpu.SemaphoreType.DMA,
        ],
        compiler_params=pltpu.CompilerParams(collective_id=1, has_side_effects=True),
    )(partial.reshape(count, rows, 128))
    piece = partial.size // (count * groups)
    return lax.dynamic_slice_in_dim(out.reshape(-1), lax.axis_index("fsdp") * piece, piece)


def conv_pool_kernel(h_ref, x_ref, l_ref, r_ref, w_ref, o_ref, xs_ref, pooled_ref, sends, recvs, local_sem):
    height, width, channels = pooled_ref.shape
    count, per_dev = o_ref.shape[0], o_ref.shape[1]
    me = lax.axis_index("tm")
    barrier = pltpu.get_barrier_semaphore()
    for k in range(1, count):
        pl.semaphore_signal(
            barrier, inc=1, device_id={"tm": lax.rem(me + k, count)}, device_id_type=MESH
        )
    depth = x_ref.shape[0]
    groups = lax.axis_size("fsdp")
    t, f = lax.axis_index("tm"), lax.axis_index("fsdp")
    rows = 8
    zero_rows = jnp.zeros((3, 2 * depth, 1, width, channels), xs_ref.dtype)
    xs_ref[:, :, pl.ds(0, 1)] = zero_rows
    xs_ref[:, :, pl.ds(height + 1, 1)] = zero_rows
    col = lax.broadcasted_iota(jnp.int32, (rows, width, channels), 1)

    def shift(r, carry):
        top = pl.multiple_of(r * rows, rows)
        for q in range(2 * depth):
            earlier = q < depth
            src = h_ref if earlier else x_ref
            block = src[q % depth, pl.ds(top, rows)].astype(jnp.float32)
            lft = l_ref[q, pl.ds(top, rows)].astype(jnp.float32)[:, None, :]
            rgt = r_ref[q, pl.ds(top, rows)].astype(jnp.float32)[:, None, :]
            lok, rok = f > 0, f < groups - 1
            if earlier:
                block = jnp.where(t > 0, block, 0.0)
                lok, rok = lok & (t > 0), rok & (t > 0)
            lft = jnp.where(lok, lft, 0.0)
            rgt = jnp.where(rok, rgt, 0.0)
            moved = [
                jnp.where(col == 0, lft, pltpu.roll(block, 1, 1)),
                block,
                jnp.where(col == width - 1, rgt, pltpu.roll(block, width - 1, 1)),
            ]
            for c in range(3):
                xs_ref[c, q, pl.ds(top + 1, rows)] = moved[c].astype(xs_ref.dtype)
        return carry

    lax.fori_loop(0, height // rows, shift, 0)
    pl.semaphore_wait(barrier, count - 1)

    def body(r, carry):
        top = pl.multiple_of(r * rows, rows)
        span = rows * width
        acc = jnp.zeros((2 * span, channels), jnp.float32)
        for b in range(3):
            for c in range(3):
                lhs = jnp.concatenate(
                    [
                        jnp.concatenate(
                            [xs_ref[c, j + a, pl.ds(top + b, rows)] for a in range(3)], axis=-1
                        ).reshape(span, 3 * channels)
                        for j in range(2)
                    ],
                    axis=0,
                )
                acc = acc + jnp.dot(lhs, w_ref[b * 3 + c], preferred_element_type=jnp.float32)
        silu = (acc / (1.0 + jnp.exp(-acc))).astype(jnp.bfloat16).astype(jnp.float32)
        pooled = ((silu[:span] + silu[span:]) * 0.5).astype(o_ref.dtype)
        pooled_ref[pl.ds(top, rows)] = pooled.reshape(rows, width, channels)
        for i in range(rows // per_dev):
            dest = r * (rows // per_dev) + i
            src = pooled_ref.at[pl.ds(top + i * per_dev, per_dev)]

            @pl.when(dest != me)
            def _():
                pltpu.make_async_remote_copy(
                    src_ref=src, dst_ref=o_ref.at[me], send_sem=sends.at[dest],
                    recv_sem=recvs.at[me], device_id={"tm": dest}, device_id_type=MESH,
                ).start()

            @pl.when(dest == me)
            def _():
                local = pltpu.make_async_copy(src, o_ref.at[me], local_sem)
                local.start()
                local.wait()

        return carry

    lax.fori_loop(0, height // rows, body, 0)

    @pl.loop(1, count)
    def _(k):
        peer = lax.rem(me + k, count)
        copy = pltpu.make_async_remote_copy(
            src_ref=pooled_ref.at[pl.ds(0, per_dev)], dst_ref=o_ref.at[peer],
            send_sem=sends.at[peer], recv_sem=recvs.at[peer],
            device_id={"tm": peer}, device_id_type=MESH,
        )
        copy.wait_send()
        copy.wait_recv()


def conv_pool(halo, frames, left, right, weights):
    depth, height, width, channels = frames.shape
    count = lax.axis_size("tm")
    vmem = pl.BlockSpec(memory_space=pltpu.VMEM)
    flops = 2 * 2 * height * width * weights.shape[0] * weights.shape[1] * channels
    return pl.pallas_call(
        conv_pool_kernel,
        out_shape=jax.ShapeDtypeStruct((count, height // count, width, channels), jnp.bfloat16),
        in_specs=[vmem] * 5,
        out_specs=vmem,
        scratch_shapes=[
            pltpu.VMEM((3, 2 * depth, height + 8, width, channels), frames.dtype),
            pltpu.VMEM((height, width, channels), jnp.bfloat16),
            pltpu.SemaphoreType.DMA((count,)),
            pltpu.SemaphoreType.DMA((count,)),
            pltpu.SemaphoreType.DMA,
        ],
        cost_estimate=pl.CostEstimate(
            flops=flops,
            transcendentals=2 * height * width * channels,
            bytes_accessed=4 * frames.size + weights.size * 2 + height * width * channels * 2,
        ),
        compiler_params=pltpu.CompilerParams(collective_id=3, has_side_effects=True),
    )(halo, frames, left, right, weights)


def prologue_kernel(x_ref, w_ref, m_ref, lcol_ref, rcol_ref, halo_ref, wall_ref, mall_ref, left_ref, right_ref, sends, recvs, wsends, wrecvs, msends, mrecvs, lsems, esends, erecvs):
    count, groups = lax.axis_size("tm"), lax.axis_size("fsdp")
    t, f = lax.axis_index("tm"), lax.axis_index("fsdp")
    t_next, t_prev = lax.rem(t + 1, count), lax.rem(t + count - 1, count)
    f_next, f_prev = lax.rem(f + 1, groups), lax.rem(f + groups - 1, groups)
    peers = [(t_next, f), (t_prev, f)] + [(t, lax.rem(f + k, groups)) for k in range(1, groups)]
    peers += [(a, b) for a in (t_next, t_prev) for b in (f_next, f_prev)]
    barrier = pltpu.get_barrier_semaphore()
    for dev in peers:
        pl.semaphore_signal(barrier, inc=1, device_id=dev, device_id_type=MESH)
    pl.semaphore_wait(barrier, len(peers))
    pieces = sends.shape[0]
    rows = x_ref.shape[1] // pieces
    halo = [
        pltpu.make_async_remote_copy(
            src_ref=x_ref.at[:, pl.ds(i * rows, rows)],
            dst_ref=halo_ref.at[:, pl.ds(i * rows, rows)],
            send_sem=sends.at[i], recv_sem=recvs.at[i],
            device_id=(t_next, f), device_id_type=MESH,
        )
        for i in range(pieces)
    ]

    depth = x_ref.shape[0]
    edges = [
        (rcol_ref, left_ref.at[pl.ds(depth, depth)], (t, f_next)),
        (lcol_ref, right_ref.at[pl.ds(depth, depth)], (t, f_prev)),
        (rcol_ref, left_ref.at[pl.ds(0, depth)], (t_next, f_next)),
        (lcol_ref, right_ref.at[pl.ds(0, depth)], (t_next, f_prev)),
    ]
    edges = [
        pltpu.make_async_remote_copy(
            src_ref=src, dst_ref=dst, send_sem=esends.at[i], recv_sem=erecvs.at[i],
            device_id=dev, device_id_type=MESH,
        )
        for i, (src, dst, dev) in enumerate(edges)
    ]
    for copy in edges[:2]:
        copy.start()
    halo = halo + edges[2:]

    @pl.when(t < count - 1)
    def _():
        for copy in halo:
            copy.start()

    copies = []
    locals_ = [
        pltpu.make_async_copy(w_ref, wall_ref.at[f], lsems.at[0]),
        pltpu.make_async_copy(m_ref, mall_ref.at[f], lsems.at[1]),
    ]
    for copy in locals_:
        copy.start()
    for k in range(1, groups):
        dev = (t, lax.rem(f + k, groups))
        for src, dst, ss, rs in ((w_ref, wall_ref, wsends, wrecvs), (m_ref, mall_ref, msends, mrecvs)):
            copy = pltpu.make_async_remote_copy(
                src_ref=src, dst_ref=dst.at[f], send_sem=ss.at[k], recv_sem=rs.at[k],
                device_id=dev, device_id_type=MESH,
            )
            copy.start()
            copies.append(copy)
    for copy in locals_:
        copy.wait()
    for copy in copies + edges[:2]:
        copy.wait()

    @pl.when(t < count - 1)
    def _():
        for copy in halo:
            copy.wait_send()

    @pl.when(t > 0)
    def _():
        for copy in halo:
            copy.wait_recv()


def prologue(frames, conv_shard, mix_shard):
    groups = lax.axis_size("fsdp")
    depth, height, width, channels = frames.shape
    lcol = frames[:, :, 0, :]
    rcol = frames[:, :, width - 1, :]
    edge = jax.ShapeDtypeStruct((2 * depth, height, channels), frames.dtype)
    vmem = pl.BlockSpec(memory_space=pltpu.VMEM)
    return pl.pallas_call(
        prologue_kernel,
        out_shape=(
            jax.ShapeDtypeStruct(frames.shape, frames.dtype),
            jax.ShapeDtypeStruct((groups,) + conv_shard.shape, conv_shard.dtype),
            jax.ShapeDtypeStruct((groups,) + mix_shard.shape, mix_shard.dtype),
            edge,
            edge,
        ),
        in_specs=[vmem] * 5,
        out_specs=(vmem,) * 5,
        scratch_shapes=[
            pltpu.SemaphoreType.DMA((4,)),
            pltpu.SemaphoreType.DMA((4,)),
            pltpu.SemaphoreType.DMA((groups,)),
            pltpu.SemaphoreType.DMA((groups,)),
            pltpu.SemaphoreType.DMA((groups,)),
            pltpu.SemaphoreType.DMA((groups,)),
            pltpu.SemaphoreType.DMA((2,)),
            pltpu.SemaphoreType.DMA((4,)),
            pltpu.SemaphoreType.DMA((4,)),
        ],
        compiler_params=pltpu.CompilerParams(collective_id=2, has_side_effects=True),
    )(frames, conv_shard, mix_shard, lcol, rcol)


def local(frames, conv_weight, mix_weight, cotangent):
    t = lax.axis_index("tm")
    count_frames, height, width, channels = frames.shape
    part = conv_weight.shape[-1]
    conv_shard = jnp.swapaxes(conv_weight, 3, 4).reshape(-1, part, channels)
    mix_shard = jnp.swapaxes(mix_weight, 1, 2)
    previous, wall, mall, left, right = prologue(frames, conv_shard, mix_shard)
    full_conv = jnp.transpose(wall, (1, 3, 0, 2)).reshape(conv_weight.shape[:-1] + (-1,))
    full_mix = jnp.transpose(mall, (1, 3, 0, 2)).reshape(mix_weight.shape[:-1] + (-1,))
    weights = jnp.transpose(full_conv, (1, 2, 0, 3, 4)).reshape(9, 3 * channels, -1)
    pooled = conv_pool(previous, frames, left, right, weights)
    branch = pooled.astype(jnp.float32).reshape(-1, channels)
    flat_cot = cotangent.reshape(-1, channels)
    grad_terms = []
    for offset in range(3):
        lagged = delayed(pooled, offset).reshape(-1, channels)
        branch = branch + jnp.dot(lagged, full_mix[offset], preferred_element_type=jnp.float32)
        grad_terms.append(
            lax.dot_general(
                lagged, flat_cot, (((0,), (0,)), ((), ())), preferred_element_type=jnp.float32
            )
        )
    encoded = branch.astype(jnp.bfloat16).reshape(pooled.shape)
    mix_grad = scatter_sum(jnp.stack(grad_terms).reshape(-1))
    return (encoded, mix_grad)


def solution(mesh):
    return jax.shard_map(
        local,
        mesh=mesh,
        in_specs=(
            P("tm", None, "fsdp", None),
            P(None, None, None, None, "fsdp"),
            P(None, None, "fsdp"),
            P(None, "tm", "fsdp", None),
        ),
        out_specs=(P(None, "tm", "fsdp", None), P(("tm", "fsdp"))),
        check_vma=False,
    )
```

```python
import jax
import jax.numpy as jnp
from jax import lax
from jax.experimental import pallas as pl
from jax.experimental.pallas import tpu as pltpu
from jax.sharding import PartitionSpec as P

MESH = pl.DeviceIdType.MESH


def from_behind(block, axis, distance):
    devices = range(lax.axis_size(axis))
    route = [(i - distance, i) for i in devices if i - distance in devices]
    return lax.ppermute(block, axis, route)


def with_halo(cells, sides, width):
    for axis, dim in sides:
        count = lax.axis_size(axis)
        ends = count - 1
        head = lax.slice_in_dim(cells, 0, width, axis=dim)
        tail = lax.slice_in_dim(cells, cells.shape[dim] - width, cells.shape[dim], axis=dim)
        cells = jnp.concatenate(
            [
                lax.ppermute(tail, axis, [(i, (i + 1) % count) for i in range(ends)]),
                cells,
                lax.ppermute(head, axis, [((i + 1) % count, i) for i in range(ends)]),
            ],
            axis=dim,
        )
    return cells


def pool_pairs(hidden):
    shaped = hidden.reshape((hidden.shape[0] // 2, 2) + hidden.shape[1:]).astype(jnp.float32)
    return ((shaped[:, 0] + shaped[:, 1]) * 0.5).astype(jnp.bfloat16)


def delayed(block, offset):
    return jnp.pad(block, ((offset, 0), (0, 0), (0, 0), (0, 0)))[: block.shape[0]]


def scatter_kernel(p_ref, o_ref, first, second, summed, s1, r1, s2, r2, l1, l2):
    count, groups = first.shape[0], second.shape[0]
    t, f = lax.axis_index("tm"), lax.axis_index("fsdp")
    barrier = pltpu.get_barrier_semaphore()
    for k in range(1, count):
        pl.semaphore_signal(
            barrier, inc=1, device_id={"tm": lax.rem(t + k, count)}, device_id_type=MESH
        )
    for k in range(1, groups):
        pl.semaphore_signal(
            barrier, inc=1, device_id={"fsdp": lax.rem(f + k, groups)}, device_id_type=MESH
        )
    pl.semaphore_wait(barrier, groups - 1 + count - 1)
    local = pltpu.make_async_copy(p_ref.at[t], first.at[t], l1)
    local.start()
    copies = []
    for k in range(1, count):
        peer = lax.rem(t + k, count)
        copy = pltpu.make_async_remote_copy(
            src_ref=p_ref.at[peer], dst_ref=first.at[t], send_sem=s1.at[k], recv_sem=r1.at[k],
            device_id={"tm": peer}, device_id_type=MESH,
        )
        copy.start()
        copies.append(copy)
    local.wait()
    for copy in copies:
        copy.wait()
    summed[...] = jnp.sum(first[...], axis=0)
    local = pltpu.make_async_copy(summed, second.at[f], l2)
    local.start()
    copies = []
    for k in range(1, groups):
        peer = lax.rem(f + k, groups)
        copy = pltpu.make_async_remote_copy(
            src_ref=summed, dst_ref=second.at[f], send_sem=s2.at[k], recv_sem=r2.at[k],
            device_id={"fsdp": peer}, device_id_type=MESH,
        )
        copy.start()
        copies.append(copy)
    local.wait()
    for copy in copies:
        copy.wait()
    o_ref[...] = jnp.sum(second[...], axis=0)


def scatter_sum(partial):
    groups, count = lax.axis_size("fsdp"), lax.axis_size("tm")
    rows = partial.size // (count * 128)
    out = pl.pallas_call(
        scatter_kernel,
        out_shape=jax.ShapeDtypeStruct((rows, 128), jnp.float32),
        in_specs=[pl.BlockSpec(memory_space=pltpu.VMEM)],
        out_specs=pl.BlockSpec(memory_space=pltpu.VMEM),
        scratch_shapes=[
            pltpu.VMEM((count, rows, 128), jnp.float32),
            pltpu.VMEM((groups, rows, 128), jnp.float32),
            pltpu.VMEM((rows, 128), jnp.float32),
            pltpu.SemaphoreType.DMA((count,)),
            pltpu.SemaphoreType.DMA((count,)),
            pltpu.SemaphoreType.DMA((groups,)),
            pltpu.SemaphoreType.DMA((groups,)),
            pltpu.SemaphoreType.DMA,
            pltpu.SemaphoreType.DMA,
        ],
        compiler_params=pltpu.CompilerParams(collective_id=1, has_side_effects=True),
    )(partial.reshape(count, rows, 128))
    piece = partial.size // (count * groups)
    return lax.dynamic_slice_in_dim(out.reshape(-1), lax.axis_index("fsdp") * piece, piece)


def conv_pool_kernel(h_ref, x_ref, l_ref, r_ref, w_ref, o_ref, xs_ref, pooled_ref, sends, recvs, local_sem):
    height, width, channels = pooled_ref.shape
    count, per_dev = o_ref.shape[0], o_ref.shape[1]
    me = lax.axis_index("tm")
    barrier = pltpu.get_barrier_semaphore()
    for k in range(1, count):
        pl.semaphore_signal(
            barrier, inc=1, device_id={"tm": lax.rem(me + k, count)}, device_id_type=MESH
        )
    depth = x_ref.shape[0]
    groups = lax.axis_size("fsdp")
    t, f = lax.axis_index("tm"), lax.axis_index("fsdp")
    rows = 8
    zero_rows = jnp.zeros((3, 2 * depth, 1, width, channels), xs_ref.dtype)
    xs_ref[:, :, pl.ds(0, 1)] = zero_rows
    xs_ref[:, :, pl.ds(height + 1, 1)] = zero_rows
    col = lax.broadcasted_iota(jnp.int32, (rows, width, channels), 1)

    def shift(r, carry):
        top = pl.multiple_of(r * rows, rows)
        for q in range(2 * depth):
            earlier = q < depth
            src = h_ref if earlier else x_ref
            block = src[q % depth, pl.ds(top, rows)].astype(jnp.float32)
            lft = l_ref[q, pl.ds(top, rows)].astype(jnp.float32)[:, None, :]
            rgt = r_ref[q, pl.ds(top, rows)].astype(jnp.float32)[:, None, :]
            lok, rok = f > 0, f < groups - 1
            if earlier:
                block = jnp.where(t > 0, block, 0.0)
                lok, rok = lok & (t > 0), rok & (t > 0)
            lft = jnp.where(lok, lft, 0.0)
            rgt = jnp.where(rok, rgt, 0.0)
            moved = [
                jnp.where(col == 0, lft, pltpu.roll(block, 1, 1)),
                block,
                jnp.where(col == width - 1, rgt, pltpu.roll(block, width - 1, 1)),
            ]
            for c in range(3):
                xs_ref[c, q, pl.ds(top + 1, rows)] = moved[c].astype(xs_ref.dtype)
        return carry

    lax.fori_loop(0, height // rows, shift, 0)
    pl.semaphore_wait(barrier, count - 1)

    chunks, spread = height // rows, rows // per_dev

    def body(step, carry):
        r = lax.rem(step + me // spread + 1, chunks)
        top = pl.multiple_of(r * rows, rows)
        span = rows * width
        acc = jnp.zeros((2 * span, channels), jnp.float32)
        for b in range(3):
            for c in range(3):
                lhs = jnp.concatenate(
                    [
                        jnp.concatenate(
                            [xs_ref[c, j + a, pl.ds(top + b, rows)] for a in range(3)], axis=-1
                        ).reshape(span, 3 * channels)
                        for j in range(2)
                    ],
                    axis=0,
                )
                acc = acc + jnp.dot(lhs, w_ref[b * 3 + c], preferred_element_type=jnp.float32)
        silu = (acc / (1.0 + jnp.exp(-acc))).astype(jnp.bfloat16).astype(jnp.float32)
        pooled = ((silu[:span] + silu[span:]) * 0.5).astype(o_ref.dtype)
        pooled_ref[pl.ds(top, rows)] = pooled.reshape(rows, width, channels)
        for i in range(rows // per_dev):
            dest = r * (rows // per_dev) + i
            src = pooled_ref.at[pl.ds(top + i * per_dev, per_dev)]

            @pl.when(dest != me)
            def _():
                pltpu.make_async_remote_copy(
                    src_ref=src, dst_ref=o_ref.at[me], send_sem=sends.at[dest],
                    recv_sem=recvs.at[me], device_id={"tm": dest}, device_id_type=MESH,
                ).start()

            @pl.when(dest == me)
            def _():
                local = pltpu.make_async_copy(src, o_ref.at[me], local_sem)
                local.start()
                local.wait()

        return carry

    lax.fori_loop(0, height // rows, body, 0)

    @pl.loop(1, count)
    def _(k):
        peer = lax.rem(me + k, count)
        copy = pltpu.make_async_remote_copy(
            src_ref=pooled_ref.at[pl.ds(0, per_dev)], dst_ref=o_ref.at[peer],
            send_sem=sends.at[peer], recv_sem=recvs.at[peer],
            device_id={"tm": peer}, device_id_type=MESH,
        )
        copy.wait_send()
        copy.wait_recv()


def conv_pool(halo, frames, left, right, weights):
    depth, height, width, channels = frames.shape
    count = lax.axis_size("tm")
    vmem = pl.BlockSpec(memory_space=pltpu.VMEM)
    flops = 2 * 2 * height * width * weights.shape[0] * weights.shape[1] * channels
    return pl.pallas_call(
        conv_pool_kernel,
        out_shape=jax.ShapeDtypeStruct((count, height // count, width, channels), jnp.bfloat16),
        in_specs=[vmem] * 5,
        out_specs=vmem,
        scratch_shapes=[
            pltpu.VMEM((3, 2 * depth, height + 8, width, channels), frames.dtype),
            pltpu.VMEM((height, width, channels), jnp.bfloat16),
            pltpu.SemaphoreType.DMA((count,)),
            pltpu.SemaphoreType.DMA((count,)),
            pltpu.SemaphoreType.DMA,
        ],
        cost_estimate=pl.CostEstimate(
            flops=flops,
            transcendentals=2 * height * width * channels,
            bytes_accessed=4 * frames.size + weights.size * 2 + height * width * channels * 2,
        ),
        compiler_params=pltpu.CompilerParams(collective_id=3, has_side_effects=True),
    )(halo, frames, left, right, weights)


def prologue_kernel(x_ref, w_ref, m_ref, lcol_ref, rcol_ref, halo_ref, wall_ref, mall_ref, left_ref, right_ref, sends, recvs, wsends, wrecvs, msends, mrecvs, lsems, esends, erecvs):
    count, groups = lax.axis_size("tm"), lax.axis_size("fsdp")
    t, f = lax.axis_index("tm"), lax.axis_index("fsdp")
    t_next, t_prev = lax.rem(t + 1, count), lax.rem(t + count - 1, count)
    f_next, f_prev = lax.rem(f + 1, groups), lax.rem(f + groups - 1, groups)
    peers = [(t_next, f), (t_prev, f)] + [(t, lax.rem(f + k, groups)) for k in range(1, groups)]
    peers += [(a, b) for a in (t_next, t_prev) for b in (f_next, f_prev)]
    barrier = pltpu.get_barrier_semaphore()
    for dev in peers:
        pl.semaphore_signal(barrier, inc=1, device_id=dev, device_id_type=MESH)
    pl.semaphore_wait(barrier, len(peers))
    pieces = sends.shape[0]
    rows = x_ref.shape[1] // pieces
    halo = [
        pltpu.make_async_remote_copy(
            src_ref=x_ref.at[:, pl.ds(i * rows, rows)],
            dst_ref=halo_ref.at[:, pl.ds(i * rows, rows)],
            send_sem=sends.at[i], recv_sem=recvs.at[i],
            device_id=(t_next, f), device_id_type=MESH,
        )
        for i in range(pieces)
    ]

    depth = x_ref.shape[0]
    edges = [
        (rcol_ref, left_ref.at[pl.ds(depth, depth)], (t, f_next)),
        (lcol_ref, right_ref.at[pl.ds(depth, depth)], (t, f_prev)),
        (rcol_ref, left_ref.at[pl.ds(0, depth)], (t_next, f_next)),
        (lcol_ref, right_ref.at[pl.ds(0, depth)], (t_next, f_prev)),
    ]
    edges = [
        pltpu.make_async_remote_copy(
            src_ref=src, dst_ref=dst, send_sem=esends.at[i], recv_sem=erecvs.at[i],
            device_id=dev, device_id_type=MESH,
        )
        for i, (src, dst, dev) in enumerate(edges)
    ]
    for copy in edges[:2]:
        copy.start()
    halo = halo + edges[2:]

    @pl.when(t < count - 1)
    def _():
        for copy in halo:
            copy.start()

    copies = []
    locals_ = [
        pltpu.make_async_copy(w_ref, wall_ref.at[f], lsems.at[0]),
        pltpu.make_async_copy(m_ref, mall_ref.at[f], lsems.at[1]),
    ]
    for copy in locals_:
        copy.start()
    for k in range(1, groups):
        dev = (t, lax.rem(f + k, groups))
        for src, dst, ss, rs in ((w_ref, wall_ref, wsends, wrecvs), (m_ref, mall_ref, msends, mrecvs)):
            copy = pltpu.make_async_remote_copy(
                src_ref=src, dst_ref=dst.at[f], send_sem=ss.at[k], recv_sem=rs.at[k],
                device_id=dev, device_id_type=MESH,
            )
            copy.start()
            copies.append(copy)
    for copy in locals_:
        copy.wait()
    for copy in copies + edges[:2]:
        copy.wait()

    @pl.when(t < count - 1)
    def _():
        for copy in halo:
            copy.wait_send()

    @pl.when(t > 0)
    def _():
        for copy in halo:
            copy.wait_recv()


def prologue(frames, conv_shard, mix_shard):
    groups = lax.axis_size("fsdp")
    depth, height, width, channels = frames.shape
    lcol = frames[:, :, 0, :]
    rcol = frames[:, :, width - 1, :]
    edge = jax.ShapeDtypeStruct((2 * depth, height, channels), frames.dtype)
    vmem = pl.BlockSpec(memory_space=pltpu.VMEM)
    return pl.pallas_call(
        prologue_kernel,
        out_shape=(
            jax.ShapeDtypeStruct(frames.shape, frames.dtype),
            jax.ShapeDtypeStruct((groups,) + conv_shard.shape, conv_shard.dtype),
            jax.ShapeDtypeStruct((groups,) + mix_shard.shape, mix_shard.dtype),
            edge,
            edge,
        ),
        in_specs=[vmem] * 5,
        out_specs=(vmem,) * 5,
        scratch_shapes=[
            pltpu.SemaphoreType.DMA((4,)),
            pltpu.SemaphoreType.DMA((4,)),
            pltpu.SemaphoreType.DMA((groups,)),
            pltpu.SemaphoreType.DMA((groups,)),
            pltpu.SemaphoreType.DMA((groups,)),
            pltpu.SemaphoreType.DMA((groups,)),
            pltpu.SemaphoreType.DMA((2,)),
            pltpu.SemaphoreType.DMA((4,)),
            pltpu.SemaphoreType.DMA((4,)),
        ],
        compiler_params=pltpu.CompilerParams(collective_id=2, has_side_effects=True),
    )(frames, conv_shard, mix_shard, lcol, rcol)


def local(frames, conv_weight, mix_weight, cotangent):
    t = lax.axis_index("tm")
    count_frames, height, width, channels = frames.shape
    part = conv_weight.shape[-1]
    conv_shard = jnp.swapaxes(conv_weight, 3, 4).reshape(-1, part, channels)
    mix_shard = jnp.swapaxes(mix_weight, 1, 2)
    previous, wall, mall, left, right = prologue(frames, conv_shard, mix_shard)
    full_conv = jnp.transpose(wall, (1, 3, 0, 2)).reshape(conv_weight.shape[:-1] + (-1,))
    full_mix = jnp.transpose(mall, (1, 3, 0, 2)).reshape(mix_weight.shape[:-1] + (-1,))
    weights = jnp.transpose(full_conv, (1, 2, 0, 3, 4)).reshape(9, 3 * channels, -1)
    pooled = conv_pool(previous, frames, left, right, weights)
    branch = pooled.astype(jnp.float32).reshape(-1, channels)
    flat_cot = cotangent.reshape(-1, channels)
    grad_terms = []
    for offset in range(3):
        lagged = delayed(pooled, offset).reshape(-1, channels)
        branch = branch + jnp.dot(lagged, full_mix[offset], preferred_element_type=jnp.float32)
        grad_terms.append(
            lax.dot_general(
                lagged, flat_cot, (((0,), (0,)), ((), ())), preferred_element_type=jnp.float32
            )
        )
    encoded = branch.astype(jnp.bfloat16).reshape(pooled.shape)
    mix_grad = scatter_sum(jnp.stack(grad_terms).reshape(-1))
    return (encoded, mix_grad)


def solution(mesh):
    return jax.shard_map(
        local,
        mesh=mesh,
        in_specs=(
            P("tm", None, "fsdp", None),
            P(None, None, None, None, "fsdp"),
            P(None, None, "fsdp"),
            P(None, "tm", "fsdp", None),
        ),
        out_specs=(P(None, "tm", "fsdp", None), P(("tm", "fsdp"))),
        check_vma=False,
    )
```

```python
import jax
import jax.numpy as jnp
from jax import lax
from jax.experimental import pallas as pl
from jax.experimental.pallas import tpu as pltpu
from jax.sharding import PartitionSpec as P

MESH = pl.DeviceIdType.MESH


def from_behind(block, axis, distance):
    devices = range(lax.axis_size(axis))
    route = [(i - distance, i) for i in devices if i - distance in devices]
    return lax.ppermute(block, axis, route)


def with_halo(cells, sides, width):
    for axis, dim in sides:
        count = lax.axis_size(axis)
        ends = count - 1
        head = lax.slice_in_dim(cells, 0, width, axis=dim)
        tail = lax.slice_in_dim(cells, cells.shape[dim] - width, cells.shape[dim], axis=dim)
        cells = jnp.concatenate(
            [
                lax.ppermute(tail, axis, [(i, (i + 1) % count) for i in range(ends)]),
                cells,
                lax.ppermute(head, axis, [((i + 1) % count, i) for i in range(ends)]),
            ],
            axis=dim,
        )
    return cells


def pool_pairs(hidden):
    shaped = hidden.reshape((hidden.shape[0] // 2, 2) + hidden.shape[1:]).astype(jnp.float32)
    return ((shaped[:, 0] + shaped[:, 1]) * 0.5).astype(jnp.bfloat16)


def delayed(block, offset):
    return jnp.pad(block, ((offset, 0), (0, 0), (0, 0), (0, 0)))[: block.shape[0]]


def scatter_kernel(p_ref, o_ref, first, second, summed, s1, r1, s2, r2, l1, l2):
    count, groups = first.shape[0], second.shape[0]
    t, f = lax.axis_index("tm"), lax.axis_index("fsdp")
    barrier = pltpu.get_barrier_semaphore()
    for k in range(1, count):
        pl.semaphore_signal(
            barrier, inc=1, device_id={"tm": lax.rem(t + k, count)}, device_id_type=MESH
        )
    for k in range(1, groups):
        pl.semaphore_signal(
            barrier, inc=1, device_id={"fsdp": lax.rem(f + k, groups)}, device_id_type=MESH
        )
    pl.semaphore_wait(barrier, groups - 1 + count - 1)
    local = pltpu.make_async_copy(p_ref.at[t], first.at[t], l1)
    local.start()
    copies = []
    for k in range(1, count):
        peer = lax.rem(t + k, count)
        copy = pltpu.make_async_remote_copy(
            src_ref=p_ref.at[peer], dst_ref=first.at[t], send_sem=s1.at[k], recv_sem=r1.at[k],
            device_id={"tm": peer}, device_id_type=MESH,
        )
        copy.start()
        copies.append(copy)
    local.wait()
    for copy in copies:
        copy.wait()
    summed[...] = jnp.sum(first[...], axis=0)
    local = pltpu.make_async_copy(summed, second.at[f], l2)
    local.start()
    copies = []
    for k in range(1, groups):
        peer = lax.rem(f + k, groups)
        copy = pltpu.make_async_remote_copy(
            src_ref=summed, dst_ref=second.at[f], send_sem=s2.at[k], recv_sem=r2.at[k],
            device_id={"fsdp": peer}, device_id_type=MESH,
        )
        copy.start()
        copies.append(copy)
    local.wait()
    for copy in copies:
        copy.wait()
    o_ref[...] = jnp.sum(second[...], axis=0)


def scatter_sum(partial):
    groups, count = lax.axis_size("fsdp"), lax.axis_size("tm")
    rows = partial.size // (count * 128)
    out = pl.pallas_call(
        scatter_kernel,
        out_shape=jax.ShapeDtypeStruct((rows, 128), jnp.float32),
        in_specs=[pl.BlockSpec(memory_space=pltpu.VMEM)],
        out_specs=pl.BlockSpec(memory_space=pltpu.VMEM),
        scratch_shapes=[
            pltpu.VMEM((count, rows, 128), jnp.float32),
            pltpu.VMEM((groups, rows, 128), jnp.float32),
            pltpu.VMEM((rows, 128), jnp.float32),
            pltpu.SemaphoreType.DMA((count,)),
            pltpu.SemaphoreType.DMA((count,)),
            pltpu.SemaphoreType.DMA((groups,)),
            pltpu.SemaphoreType.DMA((groups,)),
            pltpu.SemaphoreType.DMA,
            pltpu.SemaphoreType.DMA,
        ],
        compiler_params=pltpu.CompilerParams(collective_id=1, has_side_effects=True),
    )(partial.reshape(count, rows, 128))
    piece = partial.size // (count * groups)
    return lax.dynamic_slice_in_dim(out.reshape(-1), lax.axis_index("fsdp") * piece, piece)


def conv_pool_kernel(h_ref, x_ref, l_ref, r_ref, wall_ref, o_ref, xs_ref, pooled_ref, w_ref, sends, recvs, local_sem):
    height, width, channels = pooled_ref.shape
    count, per_dev = o_ref.shape[0], o_ref.shape[1]
    me = lax.axis_index("tm")
    barrier = pltpu.get_barrier_semaphore()
    for k in range(1, count):
        pl.semaphore_signal(
            barrier, inc=1, device_id={"tm": lax.rem(me + k, count)}, device_id_type=MESH
        )
    depth = x_ref.shape[0]
    groups = lax.axis_size("fsdp")
    for tap in range(9):
        w_ref[tap] = jnp.concatenate(
            [wall_ref[:, a * 9 + tap].reshape(w_ref.shape[1], channels) for a in range(3)], axis=-1
        )
    t, f = lax.axis_index("tm"), lax.axis_index("fsdp")
    rows = 8
    zero_rows = jnp.zeros((3, 2 * depth, 1, width, channels), xs_ref.dtype)
    xs_ref[:, :, pl.ds(0, 1)] = zero_rows
    xs_ref[:, :, pl.ds(height + 1, 1)] = zero_rows
    col = lax.broadcasted_iota(jnp.int32, (rows, width, channels), 1)

    def shift(r, carry):
        top = pl.multiple_of(r * rows, rows)
        for q in range(2 * depth):
            earlier = q < depth
            src = h_ref if earlier else x_ref
            block = src[q % depth, pl.ds(top, rows)].astype(jnp.float32)
            lft = l_ref[q, pl.ds(top, rows)].astype(jnp.float32)[:, None, :]
            rgt = r_ref[q, pl.ds(top, rows)].astype(jnp.float32)[:, None, :]
            lok, rok = f > 0, f < groups - 1
            if earlier:
                block = jnp.where(t > 0, block, 0.0)
                lok, rok = lok & (t > 0), rok & (t > 0)
            lft = jnp.where(lok, lft, 0.0)
            rgt = jnp.where(rok, rgt, 0.0)
            moved = [
                jnp.where(col == 0, lft, pltpu.roll(block, 1, 1)),
                block,
                jnp.where(col == width - 1, rgt, pltpu.roll(block, width - 1, 1)),
            ]
            for c in range(3):
                xs_ref[c, q, pl.ds(top + 1, rows)] = moved[c].astype(xs_ref.dtype)
        return carry

    lax.fori_loop(0, height // rows, shift, 0)
    pl.semaphore_wait(barrier, count - 1)

    chunks, spread = height // rows, rows // per_dev

    def body(step, carry):
        r = lax.rem(step + me // spread + 1, chunks)
        top = pl.multiple_of(r * rows, rows)
        span = rows * width
        acc = jnp.zeros((2 * span, channels), jnp.float32)
        for b in range(3):
            for c in range(3):
                lhs = jnp.concatenate(
                    [
                        jnp.concatenate(
                            [xs_ref[c, j + a, pl.ds(top + b, rows)] for a in range(3)], axis=-1
                        ).reshape(span, 3 * channels)
                        for j in range(2)
                    ],
                    axis=0,
                )
                acc = acc + lax.dot_general(
                    lhs, w_ref[b * 3 + c], (((1,), (1,)), ((), ())),
                    preferred_element_type=jnp.float32,
                )
        silu = (acc / (1.0 + jnp.exp(-acc))).astype(jnp.bfloat16).astype(jnp.float32)
        pooled = ((silu[:span] + silu[span:]) * 0.5).astype(o_ref.dtype)
        pooled_ref[pl.ds(top, rows)] = pooled.reshape(rows, width, channels)
        for i in range(rows // per_dev):
            dest = r * (rows // per_dev) + i
            src = pooled_ref.at[pl.ds(top + i * per_dev, per_dev)]

            @pl.when(dest != me)
            def _():
                pltpu.make_async_remote_copy(
                    src_ref=src, dst_ref=o_ref.at[me], send_sem=sends.at[dest],
                    recv_sem=recvs.at[me], device_id={"tm": dest}, device_id_type=MESH,
                ).start()

            @pl.when(dest == me)
            def _():
                local = pltpu.make_async_copy(src, o_ref.at[me], local_sem)
                local.start()
                local.wait()

        return carry

    lax.fori_loop(0, height // rows, body, 0)

    @pl.loop(1, count)
    def _(k):
        peer = lax.rem(me + k, count)
        copy = pltpu.make_async_remote_copy(
            src_ref=pooled_ref.at[pl.ds(0, per_dev)], dst_ref=o_ref.at[peer],
            send_sem=sends.at[peer], recv_sem=recvs.at[peer],
            device_id={"tm": peer}, device_id_type=MESH,
        )
        copy.wait_send()
        copy.wait_recv()


def conv_pool(halo, frames, left, right, wall):
    depth, height, width, channels = frames.shape
    count = lax.axis_size("tm")
    vmem = pl.BlockSpec(memory_space=pltpu.VMEM)
    cout = wall.shape[0] * wall.shape[2]
    flops = 2 * 2 * height * width * 27 * channels * cout
    return pl.pallas_call(
        conv_pool_kernel,
        out_shape=jax.ShapeDtypeStruct((count, height // count, width, channels), jnp.bfloat16),
        in_specs=[vmem] * 5,
        out_specs=vmem,
        scratch_shapes=[
            pltpu.VMEM((3, 2 * depth, height + 8, width, channels), frames.dtype),
            pltpu.VMEM((height, width, channels), jnp.bfloat16),
            pltpu.VMEM((9, cout, 3 * channels), wall.dtype),
            pltpu.SemaphoreType.DMA((count,)),
            pltpu.SemaphoreType.DMA((count,)),
            pltpu.SemaphoreType.DMA,
        ],
        cost_estimate=pl.CostEstimate(
            flops=flops,
            transcendentals=2 * height * width * channels,
            bytes_accessed=4 * frames.size + wall.size * 2 + height * width * channels * 2,
        ),
        compiler_params=pltpu.CompilerParams(collective_id=3, has_side_effects=True),
    )(halo, frames, left, right, wall)


def prologue_kernel(x_ref, w_ref, m_ref, lcol_ref, rcol_ref, halo_ref, wall_ref, mall_ref, left_ref, right_ref, sends, recvs, wsends, wrecvs, msends, mrecvs, lsems, esends, erecvs):
    count, groups = lax.axis_size("tm"), lax.axis_size("fsdp")
    t, f = lax.axis_index("tm"), lax.axis_index("fsdp")
    t_next, t_prev = lax.rem(t + 1, count), lax.rem(t + count - 1, count)
    f_next, f_prev = lax.rem(f + 1, groups), lax.rem(f + groups - 1, groups)
    peers = [(t_next, f), (t_prev, f)] + [(t, lax.rem(f + k, groups)) for k in range(1, groups)]
    peers += [(a, b) for a in (t_next, t_prev) for b in (f_next, f_prev)]
    barrier = pltpu.get_barrier_semaphore()
    for dev in peers:
        pl.semaphore_signal(barrier, inc=1, device_id=dev, device_id_type=MESH)
    pl.semaphore_wait(barrier, len(peers))
    pieces = sends.shape[0]
    rows = x_ref.shape[1] // pieces
    halo = [
        pltpu.make_async_remote_copy(
            src_ref=x_ref.at[:, pl.ds(i * rows, rows)],
            dst_ref=halo_ref.at[:, pl.ds(i * rows, rows)],
            send_sem=sends.at[i], recv_sem=recvs.at[i],
            device_id=(t_next, f), device_id_type=MESH,
        )
        for i in range(pieces)
    ]

    depth = x_ref.shape[0]
    edges = [
        (rcol_ref, left_ref.at[pl.ds(depth, depth)], (t, f_next)),
        (lcol_ref, right_ref.at[pl.ds(depth, depth)], (t, f_prev)),
        (rcol_ref, left_ref.at[pl.ds(0, depth)], (t_next, f_next)),
        (lcol_ref, right_ref.at[pl.ds(0, depth)], (t_next, f_prev)),
    ]
    edges = [
        pltpu.make_async_remote_copy(
            src_ref=src, dst_ref=dst, send_sem=esends.at[i], recv_sem=erecvs.at[i],
            device_id=dev, device_id_type=MESH,
        )
        for i, (src, dst, dev) in enumerate(edges)
    ]
    for copy in edges[:2]:
        copy.start()
    halo = halo + edges[2:]

    @pl.when(t < count - 1)
    def _():
        for copy in halo:
            copy.start()

    copies = []
    locals_ = [
        pltpu.make_async_copy(w_ref, wall_ref.at[f], lsems.at[0]),
        pltpu.make_async_copy(m_ref, mall_ref.at[f], lsems.at[1]),
    ]
    for copy in locals_:
        copy.start()
    for k in range(1, groups):
        dev = (t, lax.rem(f + k, groups))
        for src, dst, ss, rs in ((w_ref, wall_ref, wsends, wrecvs), (m_ref, mall_ref, msends, mrecvs)):
            copy = pltpu.make_async_remote_copy(
                src_ref=src, dst_ref=dst.at[f], send_sem=ss.at[k], recv_sem=rs.at[k],
                device_id=dev, device_id_type=MESH,
            )
            copy.start()
            copies.append(copy)
    for copy in locals_:
        copy.wait()
    for copy in copies + edges[:2]:
        copy.wait()

    @pl.when(t < count - 1)
    def _():
        for copy in halo:
            copy.wait_send()

    @pl.when(t > 0)
    def _():
        for copy in halo:
            copy.wait_recv()


def prologue(frames, conv_shard, mix_shard):
    groups = lax.axis_size("fsdp")
    depth, height, width, channels = frames.shape
    lcol = frames[:, :, 0, :]
    rcol = frames[:, :, width - 1, :]
    edge = jax.ShapeDtypeStruct((2 * depth, height, channels), frames.dtype)
    vmem = pl.BlockSpec(memory_space=pltpu.VMEM)
    return pl.pallas_call(
        prologue_kernel,
        out_shape=(
            jax.ShapeDtypeStruct(frames.shape, frames.dtype),
            jax.ShapeDtypeStruct((groups,) + conv_shard.shape, conv_shard.dtype),
            jax.ShapeDtypeStruct((groups,) + mix_shard.shape, mix_shard.dtype),
            edge,
            edge,
        ),
        in_specs=[vmem] * 5,
        out_specs=(vmem,) * 5,
        scratch_shapes=[
            pltpu.SemaphoreType.DMA((4,)),
            pltpu.SemaphoreType.DMA((4,)),
            pltpu.SemaphoreType.DMA((groups,)),
            pltpu.SemaphoreType.DMA((groups,)),
            pltpu.SemaphoreType.DMA((groups,)),
            pltpu.SemaphoreType.DMA((groups,)),
            pltpu.SemaphoreType.DMA((2,)),
            pltpu.SemaphoreType.DMA((4,)),
            pltpu.SemaphoreType.DMA((4,)),
        ],
        compiler_params=pltpu.CompilerParams(collective_id=2, has_side_effects=True),
    )(frames, conv_shard, mix_shard, lcol, rcol)


def local(frames, conv_weight, mix_weight, cotangent):
    t = lax.axis_index("tm")
    count_frames, height, width, channels = frames.shape
    part = conv_weight.shape[-1]
    conv_shard = jnp.swapaxes(conv_weight, 3, 4).reshape(-1, part, channels)
    mix_shard = jnp.swapaxes(mix_weight, 1, 2)
    previous, wall, mall, left, right = prologue(frames, conv_shard, mix_shard)
    full_mix = jnp.transpose(mall, (1, 3, 0, 2)).reshape(mix_weight.shape[:-1] + (-1,))
    pooled = conv_pool(previous, frames, left, right, wall)
    branch = pooled.astype(jnp.float32).reshape(-1, channels)
    flat_cot = cotangent.reshape(-1, channels)
    grad_terms = []
    for offset in range(3):
        lagged = delayed(pooled, offset).reshape(-1, channels)
        branch = branch + jnp.dot(lagged, full_mix[offset], preferred_element_type=jnp.float32)
        grad_terms.append(
            lax.dot_general(
                lagged, flat_cot, (((0,), (0,)), ((), ())), preferred_element_type=jnp.float32
            )
        )
    encoded = branch.astype(jnp.bfloat16).reshape(pooled.shape)
    mix_grad = scatter_sum(jnp.stack(grad_terms).reshape(-1))
    return (encoded, mix_grad)


def solution(mesh):
    return jax.shard_map(
        local,
        mesh=mesh,
        in_specs=(
            P("tm", None, "fsdp", None),
            P(None, None, None, None, "fsdp"),
            P(None, None, "fsdp"),
            P(None, "tm", "fsdp", None),
        ),
        out_specs=(P(None, "tm", "fsdp", None), P(("tm", "fsdp"))),
        check_vma=False,
    )
```

```python
import jax
import jax.numpy as jnp
from jax import lax
from jax.experimental import pallas as pl
from jax.experimental.pallas import tpu as pltpu
from jax.sharding import PartitionSpec as P

MESH = pl.DeviceIdType.MESH


def from_behind(block, axis, distance):
    devices = range(lax.axis_size(axis))
    route = [(i - distance, i) for i in devices if i - distance in devices]
    return lax.ppermute(block, axis, route)


def with_halo(cells, sides, width):
    for axis, dim in sides:
        count = lax.axis_size(axis)
        ends = count - 1
        head = lax.slice_in_dim(cells, 0, width, axis=dim)
        tail = lax.slice_in_dim(cells, cells.shape[dim] - width, cells.shape[dim], axis=dim)
        cells = jnp.concatenate(
            [
                lax.ppermute(tail, axis, [(i, (i + 1) % count) for i in range(ends)]),
                cells,
                lax.ppermute(head, axis, [((i + 1) % count, i) for i in range(ends)]),
            ],
            axis=dim,
        )
    return cells


def pool_pairs(hidden):
    shaped = hidden.reshape((hidden.shape[0] // 2, 2) + hidden.shape[1:]).astype(jnp.float32)
    return ((shaped[:, 0] + shaped[:, 1]) * 0.5).astype(jnp.bfloat16)


def delayed(block, offset):
    return jnp.pad(block, ((offset, 0), (0, 0), (0, 0), (0, 0)))[: block.shape[0]]


def scatter_kernel(p_ref, x_ref, m_ref, o_ref, e_ref, first, second, summed, branch, s1, r1, s2, r2, l1, l2):
    count, groups = first.shape[0], second.shape[0]
    t, f = lax.axis_index("tm"), lax.axis_index("fsdp")
    barrier = pltpu.get_barrier_semaphore()
    for k in range(1, count):
        pl.semaphore_signal(
            barrier, inc=1, device_id={"tm": lax.rem(t + k, count)}, device_id_type=MESH
        )
    for k in range(1, groups):
        pl.semaphore_signal(
            barrier, inc=1, device_id={"fsdp": lax.rem(f + k, groups)}, device_id_type=MESH
        )
    total = x_ref.shape[0]
    lag = total // count
    branch[...] = x_ref[...].astype(jnp.float32) + jnp.dot(
        x_ref[...], m_ref[0], preferred_element_type=jnp.float32
    )
    for k in (1, 2):
        branch[pl.ds(k * lag, total - k * lag)] += jnp.dot(
            x_ref[pl.ds(0, total - k * lag)], m_ref[k], preferred_element_type=jnp.float32
        )
    e_ref[...] = branch[...].astype(e_ref.dtype)
    pl.semaphore_wait(barrier, groups - 1 + count - 1)
    local = pltpu.make_async_copy(p_ref.at[t], first.at[t], l1)
    local.start()
    copies = []
    for k in range(1, count):
        peer = lax.rem(t + k, count)
        copy = pltpu.make_async_remote_copy(
            src_ref=p_ref.at[peer], dst_ref=first.at[t], send_sem=s1.at[k], recv_sem=r1.at[k],
            device_id={"tm": peer}, device_id_type=MESH,
        )
        copy.start()
        copies.append(copy)
    local.wait()
    for copy in copies:
        copy.wait()
    summed[...] = jnp.sum(first[...], axis=0)
    local = pltpu.make_async_copy(summed, second.at[f], l2)
    local.start()
    copies = []
    for k in range(1, groups):
        peer = lax.rem(f + k, groups)
        copy = pltpu.make_async_remote_copy(
            src_ref=summed, dst_ref=second.at[f], send_sem=s2.at[k], recv_sem=r2.at[k],
            device_id={"fsdp": peer}, device_id_type=MESH,
        )
        copy.start()
        copies.append(copy)
    local.wait()
    for copy in copies:
        copy.wait()
    o_ref[...] = jnp.sum(second[...], axis=0)


def scatter_sum(partial, pooled, mix):
    groups, count = lax.axis_size("fsdp"), lax.axis_size("tm")
    rows = partial.size // (count * 128)
    vmem = pl.BlockSpec(memory_space=pltpu.VMEM)
    out, encoded = pl.pallas_call(
        scatter_kernel,
        out_shape=(
            jax.ShapeDtypeStruct((rows, 128), jnp.float32),
            jax.ShapeDtypeStruct(pooled.shape, pooled.dtype),
        ),
        in_specs=[vmem] * 3,
        out_specs=(vmem, vmem),
        scratch_shapes=[
            pltpu.VMEM((count, rows, 128), jnp.float32),
            pltpu.VMEM((groups, rows, 128), jnp.float32),
            pltpu.VMEM((rows, 128), jnp.float32),
            pltpu.VMEM(pooled.shape, jnp.float32),
            pltpu.SemaphoreType.DMA((count,)),
            pltpu.SemaphoreType.DMA((count,)),
            pltpu.SemaphoreType.DMA((groups,)),
            pltpu.SemaphoreType.DMA((groups,)),
            pltpu.SemaphoreType.DMA,
            pltpu.SemaphoreType.DMA,
        ],
        compiler_params=pltpu.CompilerParams(collective_id=1, has_side_effects=True),
    )(partial.reshape(count, rows, 128), pooled, mix)
    piece = partial.size // (count * groups)
    return lax.dynamic_slice_in_dim(out.reshape(-1), lax.axis_index("fsdp") * piece, piece), encoded


def conv_pool_kernel(h_ref, x_ref, l_ref, r_ref, wall_ref, o_ref, xs_ref, pooled_ref, w_ref, sends, recvs, local_sem):
    height, width, channels = pooled_ref.shape
    count, per_dev = o_ref.shape[0], o_ref.shape[1]
    me = lax.axis_index("tm")
    barrier = pltpu.get_barrier_semaphore()
    for k in range(1, count):
        pl.semaphore_signal(
            barrier, inc=1, device_id={"tm": lax.rem(me + k, count)}, device_id_type=MESH
        )
    depth = x_ref.shape[0]
    groups = lax.axis_size("fsdp")
    for tap in range(9):
        w_ref[tap] = jnp.concatenate(
            [wall_ref[:, a * 9 + tap].reshape(w_ref.shape[1], channels) for a in range(3)], axis=-1
        )
    t, f = lax.axis_index("tm"), lax.axis_index("fsdp")
    rows = 8
    zero_rows = jnp.zeros((3, 2 * depth, 1, width, channels), xs_ref.dtype)
    xs_ref[:, :, pl.ds(0, 1)] = zero_rows
    xs_ref[:, :, pl.ds(height + 1, 1)] = zero_rows
    col = lax.broadcasted_iota(jnp.int32, (rows, width, channels), 1)

    def shift(r, carry):
        top = pl.multiple_of(r * rows, rows)
        for q in range(2 * depth):
            earlier = q < depth
            src = h_ref if earlier else x_ref
            block = src[q % depth, pl.ds(top, rows)].astype(jnp.float32)
            lft = l_ref[q, pl.ds(top, rows)].astype(jnp.float32)[:, None, :]
            rgt = r_ref[q, pl.ds(top, rows)].astype(jnp.float32)[:, None, :]
            lok, rok = f > 0, f < groups - 1
            if earlier:
                block = jnp.where(t > 0, block, 0.0)
                lok, rok = lok & (t > 0), rok & (t > 0)
            lft = jnp.where(lok, lft, 0.0)
            rgt = jnp.where(rok, rgt, 0.0)
            moved = [
                jnp.where(col == 0, lft, pltpu.roll(block, 1, 1)),
                block,
                jnp.where(col == width - 1, rgt, pltpu.roll(block, width - 1, 1)),
            ]
            for c in range(3):
                xs_ref[c, q, pl.ds(top + 1, rows)] = moved[c].astype(xs_ref.dtype)
        return carry

    lax.fori_loop(0, height // rows, shift, 0)
    pl.semaphore_wait(barrier, count - 1)

    chunks, spread = height // rows, rows // per_dev

    def body(step, carry):
        r = lax.rem(step + me // spread + 1, chunks)
        top = pl.multiple_of(r * rows, rows)
        span = rows * width
        acc = jnp.zeros((2 * span, channels), jnp.float32)
        for b in range(3):
            for c in range(3):
                lhs = jnp.concatenate(
                    [
                        jnp.concatenate(
                            [xs_ref[c, j + a, pl.ds(top + b, rows)] for a in range(3)], axis=-1
                        ).reshape(span, 3 * channels)
                        for j in range(2)
                    ],
                    axis=0,
                )
                acc = acc + lax.dot_general(
                    lhs, w_ref[b * 3 + c], (((1,), (1,)), ((), ())),
                    preferred_element_type=jnp.float32,
                )
        silu = (acc / (1.0 + jnp.exp(-acc))).astype(jnp.bfloat16).astype(jnp.float32)
        pooled = ((silu[:span] + silu[span:]) * 0.5).astype(o_ref.dtype)
        pooled_ref[pl.ds(top, rows)] = pooled.reshape(rows, width, channels)
        for i in range(rows // per_dev):
            dest = r * (rows // per_dev) + i
            src = pooled_ref.at[pl.ds(top + i * per_dev, per_dev)]

            @pl.when(dest != me)
            def _():
                pltpu.make_async_remote_copy(
                    src_ref=src, dst_ref=o_ref.at[me], send_sem=sends.at[dest],
                    recv_sem=recvs.at[me], device_id={"tm": dest}, device_id_type=MESH,
                ).start()

            @pl.when(dest == me)
            def _():
                local = pltpu.make_async_copy(src, o_ref.at[me], local_sem)
                local.start()
                local.wait()

        return carry

    lax.fori_loop(0, height // rows, body, 0)

    @pl.loop(1, count)
    def _(k):
        peer = lax.rem(me + k, count)
        copy = pltpu.make_async_remote_copy(
            src_ref=pooled_ref.at[pl.ds(0, per_dev)], dst_ref=o_ref.at[peer],
            send_sem=sends.at[peer], recv_sem=recvs.at[peer],
            device_id={"tm": peer}, device_id_type=MESH,
        )
        copy.wait_send()
        copy.wait_recv()


def conv_pool(halo, frames, left, right, wall):
    depth, height, width, channels = frames.shape
    count = lax.axis_size("tm")
    vmem = pl.BlockSpec(memory_space=pltpu.VMEM)
    cout = wall.shape[0] * wall.shape[2]
    flops = 2 * 2 * height * width * 27 * channels * cout
    return pl.pallas_call(
        conv_pool_kernel,
        out_shape=jax.ShapeDtypeStruct((count, height // count, width, channels), jnp.bfloat16),
        in_specs=[vmem] * 5,
        out_specs=vmem,
        scratch_shapes=[
            pltpu.VMEM((3, 2 * depth, height + 8, width, channels), frames.dtype),
            pltpu.VMEM((height, width, channels), jnp.bfloat16),
            pltpu.VMEM((9, cout, 3 * channels), wall.dtype),
            pltpu.SemaphoreType.DMA((count,)),
            pltpu.SemaphoreType.DMA((count,)),
            pltpu.SemaphoreType.DMA,
        ],
        cost_estimate=pl.CostEstimate(
            flops=flops,
            transcendentals=2 * height * width * channels,
            bytes_accessed=4 * frames.size + wall.size * 2 + height * width * channels * 2,
        ),
        compiler_params=pltpu.CompilerParams(collective_id=3, has_side_effects=True),
    )(halo, frames, left, right, wall)


def prologue_kernel(x_ref, w_ref, m_ref, lcol_ref, rcol_ref, halo_ref, wall_ref, mall_ref, left_ref, right_ref, sends, recvs, wsends, wrecvs, msends, mrecvs, lsems, esends, erecvs):
    count, groups = lax.axis_size("tm"), lax.axis_size("fsdp")
    t, f = lax.axis_index("tm"), lax.axis_index("fsdp")
    t_next, t_prev = lax.rem(t + 1, count), lax.rem(t + count - 1, count)
    f_next, f_prev = lax.rem(f + 1, groups), lax.rem(f + groups - 1, groups)
    peers = [(t_next, f), (t_prev, f)] + [(t, lax.rem(f + k, groups)) for k in range(1, groups)]
    peers += [(a, b) for a in (t_next, t_prev) for b in (f_next, f_prev)]
    barrier = pltpu.get_barrier_semaphore()
    for dev in peers:
        pl.semaphore_signal(barrier, inc=1, device_id=dev, device_id_type=MESH)
    pl.semaphore_wait(barrier, len(peers))
    pieces = sends.shape[0]
    rows = x_ref.shape[1] // pieces
    halo = [
        pltpu.make_async_remote_copy(
            src_ref=x_ref.at[:, pl.ds(i * rows, rows)],
            dst_ref=halo_ref.at[:, pl.ds(i * rows, rows)],
            send_sem=sends.at[i], recv_sem=recvs.at[i],
            device_id=(t_next, f), device_id_type=MESH,
        )
        for i in range(pieces)
    ]

    depth = x_ref.shape[0]
    edges = [
        (rcol_ref, left_ref.at[pl.ds(depth, depth)], (t, f_next)),
        (lcol_ref, right_ref.at[pl.ds(depth, depth)], (t, f_prev)),
        (rcol_ref, left_ref.at[pl.ds(0, depth)], (t_next, f_next)),
        (lcol_ref, right_ref.at[pl.ds(0, depth)], (t_next, f_prev)),
    ]
    edges = [
        pltpu.make_async_remote_copy(
            src_ref=src, dst_ref=dst, send_sem=esends.at[i], recv_sem=erecvs.at[i],
            device_id=dev, device_id_type=MESH,
        )
        for i, (src, dst, dev) in enumerate(edges)
    ]
    for copy in edges[:2]:
        copy.start()
    halo = halo + edges[2:]

    @pl.when(t < count - 1)
    def _():
        for copy in halo:
            copy.start()

    copies = []
    locals_ = [
        pltpu.make_async_copy(w_ref, wall_ref.at[f], lsems.at[0]),
        pltpu.make_async_copy(m_ref, mall_ref.at[f], lsems.at[1]),
    ]
    for copy in locals_:
        copy.start()
    for k in range(1, groups):
        dev = (t, lax.rem(f + k, groups))
        for src, dst, ss, rs in ((w_ref, wall_ref, wsends, wrecvs), (m_ref, mall_ref, msends, mrecvs)):
            copy = pltpu.make_async_remote_copy(
                src_ref=src, dst_ref=dst.at[f], send_sem=ss.at[k], recv_sem=rs.at[k],
                device_id=dev, device_id_type=MESH,
            )
            copy.start()
            copies.append(copy)
    for copy in locals_:
        copy.wait()
    for copy in copies + edges[:2]:
        copy.wait()

    @pl.when(t < count - 1)
    def _():
        for copy in halo:
            copy.wait_send()

    @pl.when(t > 0)
    def _():
        for copy in halo:
            copy.wait_recv()


def prologue(frames, conv_shard, mix_shard):
    groups = lax.axis_size("fsdp")
    depth, height, width, channels = frames.shape
    lcol = frames[:, :, 0, :]
    rcol = frames[:, :, width - 1, :]
    edge = jax.ShapeDtypeStruct((2 * depth, height, channels), frames.dtype)
    vmem = pl.BlockSpec(memory_space=pltpu.VMEM)
    return pl.pallas_call(
        prologue_kernel,
        out_shape=(
            jax.ShapeDtypeStruct(frames.shape, frames.dtype),
            jax.ShapeDtypeStruct((groups,) + conv_shard.shape, conv_shard.dtype),
            jax.ShapeDtypeStruct((groups,) + mix_shard.shape, mix_shard.dtype),
            edge,
            edge,
        ),
        in_specs=[vmem] * 5,
        out_specs=(vmem,) * 5,
        scratch_shapes=[
            pltpu.SemaphoreType.DMA((4,)),
            pltpu.SemaphoreType.DMA((4,)),
            pltpu.SemaphoreType.DMA((groups,)),
            pltpu.SemaphoreType.DMA((groups,)),
            pltpu.SemaphoreType.DMA((groups,)),
            pltpu.SemaphoreType.DMA((groups,)),
            pltpu.SemaphoreType.DMA((2,)),
            pltpu.SemaphoreType.DMA((4,)),
            pltpu.SemaphoreType.DMA((4,)),
        ],
        compiler_params=pltpu.CompilerParams(collective_id=2, has_side_effects=True),
    )(frames, conv_shard, mix_shard, lcol, rcol)


def local(frames, conv_weight, mix_weight, cotangent):
    t = lax.axis_index("tm")
    count_frames, height, width, channels = frames.shape
    part = conv_weight.shape[-1]
    conv_shard = jnp.swapaxes(conv_weight, 3, 4).reshape(-1, part, channels)
    mix_shard = jnp.swapaxes(mix_weight, 1, 2)
    previous, wall, mall, left, right = prologue(frames, conv_shard, mix_shard)
    full_mix = jnp.transpose(mall, (1, 3, 0, 2)).reshape(mix_weight.shape[:-1] + (-1,))
    pooled = conv_pool(previous, frames, left, right, wall)
    flat_cot = cotangent.reshape(-1, channels)
    grad_terms = []
    for offset in range(3):
        lagged = delayed(pooled, offset).reshape(-1, channels)
        grad_terms.append(
            lax.dot_general(
                lagged, flat_cot, (((0,), (0,)), ((), ())), preferred_element_type=jnp.float32
            )
        )
    mix_grad, encoded = scatter_sum(
        jnp.stack(grad_terms).reshape(-1), pooled.reshape(-1, channels), full_mix
    )
    encoded = encoded.reshape(pooled.shape)
    return (encoded, mix_grad)


def solution(mesh):
    return jax.shard_map(
        local,
        mesh=mesh,
        in_specs=(
            P("tm", None, "fsdp", None),
            P(None, None, None, None, "fsdp"),
            P(None, None, "fsdp"),
            P(None, "tm", "fsdp", None),
        ),
        out_specs=(P(None, "tm", "fsdp", None), P(("tm", "fsdp"))),
        check_vma=False,
    )
```

```python
import jax
import jax.numpy as jnp
from jax import lax
from jax.experimental import pallas as pl
from jax.experimental.pallas import tpu as pltpu
from jax.sharding import PartitionSpec as P

MESH = pl.DeviceIdType.MESH


def from_behind(block, axis, distance):
    devices = range(lax.axis_size(axis))
    route = [(i - distance, i) for i in devices if i - distance in devices]
    return lax.ppermute(block, axis, route)


def with_halo(cells, sides, width):
    for axis, dim in sides:
        count = lax.axis_size(axis)
        ends = count - 1
        head = lax.slice_in_dim(cells, 0, width, axis=dim)
        tail = lax.slice_in_dim(cells, cells.shape[dim] - width, cells.shape[dim], axis=dim)
        cells = jnp.concatenate(
            [
                lax.ppermute(tail, axis, [(i, (i + 1) % count) for i in range(ends)]),
                cells,
                lax.ppermute(head, axis, [((i + 1) % count, i) for i in range(ends)]),
            ],
            axis=dim,
        )
    return cells


def pool_pairs(hidden):
    shaped = hidden.reshape((hidden.shape[0] // 2, 2) + hidden.shape[1:]).astype(jnp.float32)
    return ((shaped[:, 0] + shaped[:, 1]) * 0.5).astype(jnp.bfloat16)


def delayed(block, offset):
    return jnp.pad(block, ((offset, 0), (0, 0), (0, 0), (0, 0)))[: block.shape[0]]


def scatter_kernel(p_ref, o_ref, first, second, summed, s1, r1, s2, r2, l1, l2):
    count, groups = first.shape[0], second.shape[0]
    t, f = lax.axis_index("tm"), lax.axis_index("fsdp")
    barrier = pltpu.get_barrier_semaphore()
    for k in range(1, count):
        pl.semaphore_signal(
            barrier, inc=1, device_id={"tm": lax.rem(t + k, count)}, device_id_type=MESH
        )
    for k in range(1, groups):
        pl.semaphore_signal(
            barrier, inc=1, device_id={"fsdp": lax.rem(f + k, groups)}, device_id_type=MESH
        )
    pl.semaphore_wait(barrier, groups - 1 + count - 1)
    local = pltpu.make_async_copy(p_ref.at[t], first.at[t], l1)
    local.start()
    copies = []
    for k in range(1, count):
        peer = lax.rem(t + k, count)
        copy = pltpu.make_async_remote_copy(
            src_ref=p_ref.at[peer], dst_ref=first.at[t], send_sem=s1.at[k], recv_sem=r1.at[k],
            device_id={"tm": peer}, device_id_type=MESH,
        )
        copy.start()
        copies.append(copy)
    local.wait()
    for copy in copies:
        copy.wait()
    summed[...] = jnp.sum(first[...], axis=0)
    local = pltpu.make_async_copy(summed, second.at[f], l2)
    local.start()
    copies = []
    for k in range(1, groups):
        peer = lax.rem(f + k, groups)
        copy = pltpu.make_async_remote_copy(
            src_ref=summed, dst_ref=second.at[f], send_sem=s2.at[k], recv_sem=r2.at[k],
            device_id={"fsdp": peer}, device_id_type=MESH,
        )
        copy.start()
        copies.append(copy)
    local.wait()
    for copy in copies:
        copy.wait()
    summed[...] = jnp.sum(second[...], axis=0)
    per = o_ref.shape[0]
    o_ref[...] = summed[pl.ds(pl.multiple_of(f * per, per), per)]


def scatter_sum(partial):
    groups, count = lax.axis_size("fsdp"), lax.axis_size("tm")
    piece = partial.size // (count * groups)
    wide = -(-piece // 128) * 128
    arranged = jnp.pad(partial.reshape(count, groups, piece), ((0, 0), (0, 0), (0, wide - piece)))
    rows = groups * wide // 128
    out = pl.pallas_call(
        scatter_kernel,
        out_shape=jax.ShapeDtypeStruct((wide // 128, 128), jnp.float32),
        in_specs=[pl.BlockSpec(memory_space=pltpu.VMEM)],
        out_specs=pl.BlockSpec(memory_space=pltpu.VMEM),
        scratch_shapes=[
            pltpu.VMEM((count, rows, 128), jnp.float32),
            pltpu.VMEM((groups, rows, 128), jnp.float32),
            pltpu.VMEM((rows, 128), jnp.float32),
            pltpu.SemaphoreType.DMA((count,)),
            pltpu.SemaphoreType.DMA((count,)),
            pltpu.SemaphoreType.DMA((groups,)),
            pltpu.SemaphoreType.DMA((groups,)),
            pltpu.SemaphoreType.DMA,
            pltpu.SemaphoreType.DMA,
        ],
        compiler_params=pltpu.CompilerParams(collective_id=1, has_side_effects=True),
    )(arranged.reshape(count, rows, 128))
    return out.reshape(-1)[:piece]


def conv_pool_kernel(h_ref, x_ref, l_ref, r_ref, wall_ref, o_ref, xs_ref, pooled_ref, w_ref, sends, recvs, local_sem):
    height, width, channels = pooled_ref.shape
    count, per_dev = o_ref.shape[0], o_ref.shape[1]
    me = lax.axis_index("tm")
    barrier = pltpu.get_barrier_semaphore()
    for k in range(1, count):
        pl.semaphore_signal(
            barrier, inc=1, device_id={"tm": lax.rem(me + k, count)}, device_id_type=MESH
        )
    depth = x_ref.shape[0]
    groups = lax.axis_size("fsdp")
    for tap in range(9):
        w_ref[tap] = jnp.concatenate(
            [wall_ref[:, a * 9 + tap].reshape(w_ref.shape[1], channels) for a in range(3)], axis=-1
        )
    t, f = lax.axis_index("tm"), lax.axis_index("fsdp")
    rows = 8
    zero_rows = jnp.zeros((3, 2 * depth, 1, width, channels), xs_ref.dtype)
    xs_ref[:, :, pl.ds(0, 1)] = zero_rows
    xs_ref[:, :, pl.ds(height + 1, 1)] = zero_rows
    col = lax.broadcasted_iota(jnp.int32, (rows, width, channels), 1)

    def shift(r, carry):
        top = pl.multiple_of(r * rows, rows)
        for q in range(2 * depth):
            earlier = q < depth
            src = h_ref if earlier else x_ref
            block = src[q % depth, pl.ds(top, rows)].astype(jnp.float32)
            lft = l_ref[q, pl.ds(top, rows)].astype(jnp.float32)[:, None, :]
            rgt = r_ref[q, pl.ds(top, rows)].astype(jnp.float32)[:, None, :]
            lok, rok = f > 0, f < groups - 1
            if earlier:
                block = jnp.where(t > 0, block, 0.0)
                lok, rok = lok & (t > 0), rok & (t > 0)
            lft = jnp.where(lok, lft, 0.0)
            rgt = jnp.where(rok, rgt, 0.0)
            moved = [
                jnp.where(col == 0, lft, pltpu.roll(block, 1, 1)),
                block,
                jnp.where(col == width - 1, rgt, pltpu.roll(block, width - 1, 1)),
            ]
            for c in range(3):
                xs_ref[c, q, pl.ds(top + 1, rows)] = moved[c].astype(xs_ref.dtype)
        return carry

    lax.fori_loop(0, height // rows, shift, 0)
    pl.semaphore_wait(barrier, count - 1)

    chunks, spread = height // rows, rows // per_dev

    def body(step, carry):
        r = lax.rem(step + me // spread + 1, chunks)
        top = pl.multiple_of(r * rows, rows)
        span = rows * width
        acc = jnp.zeros((2 * span, channels), jnp.float32)
        for b in range(3):
            for c in range(3):
                lhs = jnp.concatenate(
                    [
                        jnp.concatenate(
                            [xs_ref[c, j + a, pl.ds(top + b, rows)] for a in range(3)], axis=-1
                        ).reshape(span, 3 * channels)
                        for j in range(2)
                    ],
                    axis=0,
                )
                acc = acc + lax.dot_general(
                    lhs, w_ref[b * 3 + c], (((1,), (1,)), ((), ())),
                    preferred_element_type=jnp.float32,
                )
        silu = (acc / (1.0 + jnp.exp(-acc))).astype(jnp.bfloat16).astype(jnp.float32)
        pooled = ((silu[:span] + silu[span:]) * 0.5).astype(o_ref.dtype)
        pooled_ref[pl.ds(top, rows)] = pooled.reshape(rows, width, channels)
        for i in range(rows // per_dev):
            dest = r * (rows // per_dev) + i
            src = pooled_ref.at[pl.ds(top + i * per_dev, per_dev)]

            @pl.when(dest != me)
            def _():
                pltpu.make_async_remote_copy(
                    src_ref=src, dst_ref=o_ref.at[me], send_sem=sends.at[dest],
                    recv_sem=recvs.at[me], device_id={"tm": dest}, device_id_type=MESH,
                ).start()

            @pl.when(dest == me)
            def _():
                local = pltpu.make_async_copy(src, o_ref.at[me], local_sem)
                local.start()
                local.wait()

        return carry

    lax.fori_loop(0, height // rows, body, 0)

    @pl.loop(1, count)
    def _(k):
        peer = lax.rem(me + k, count)
        copy = pltpu.make_async_remote_copy(
            src_ref=pooled_ref.at[pl.ds(0, per_dev)], dst_ref=o_ref.at[peer],
            send_sem=sends.at[peer], recv_sem=recvs.at[peer],
            device_id={"tm": peer}, device_id_type=MESH,
        )
        copy.wait_send()
        copy.wait_recv()


def conv_pool(halo, frames, left, right, wall):
    depth, height, width, channels = frames.shape
    count = lax.axis_size("tm")
    vmem = pl.BlockSpec(memory_space=pltpu.VMEM)
    cout = wall.shape[0] * wall.shape[2]
    flops = 2 * 2 * height * width * 27 * channels * cout
    return pl.pallas_call(
        conv_pool_kernel,
        out_shape=jax.ShapeDtypeStruct((count, height // count, width, channels), jnp.bfloat16),
        in_specs=[vmem] * 5,
        out_specs=vmem,
        scratch_shapes=[
            pltpu.VMEM((3, 2 * depth, height + 8, width, channels), frames.dtype),
            pltpu.VMEM((height, width, channels), jnp.bfloat16),
            pltpu.VMEM((9, cout, 3 * channels), wall.dtype),
            pltpu.SemaphoreType.DMA((count,)),
            pltpu.SemaphoreType.DMA((count,)),
            pltpu.SemaphoreType.DMA,
        ],
        cost_estimate=pl.CostEstimate(
            flops=flops,
            transcendentals=2 * height * width * channels,
            bytes_accessed=4 * frames.size + wall.size * 2 + height * width * channels * 2,
        ),
        compiler_params=pltpu.CompilerParams(collective_id=3, has_side_effects=True),
    )(halo, frames, left, right, wall)


def prologue_kernel(x_ref, w_ref, m_ref, lcol_ref, rcol_ref, halo_ref, wall_ref, mall_ref, left_ref, right_ref, sends, recvs, wsends, wrecvs, msends, mrecvs, lsems, esends, erecvs):
    count, groups = lax.axis_size("tm"), lax.axis_size("fsdp")
    t, f = lax.axis_index("tm"), lax.axis_index("fsdp")
    t_next, t_prev = lax.rem(t + 1, count), lax.rem(t + count - 1, count)
    f_next, f_prev = lax.rem(f + 1, groups), lax.rem(f + groups - 1, groups)
    peers = [(t_next, f), (t_prev, f)] + [(t, lax.rem(f + k, groups)) for k in range(1, groups)]
    peers += [(a, b) for a in (t_next, t_prev) for b in (f_next, f_prev)]
    barrier = pltpu.get_barrier_semaphore()
    for dev in peers:
        pl.semaphore_signal(barrier, inc=1, device_id=dev, device_id_type=MESH)
    pl.semaphore_wait(barrier, len(peers))
    pieces = sends.shape[0]
    rows = x_ref.shape[1] // pieces
    halo = [
        pltpu.make_async_remote_copy(
            src_ref=x_ref.at[:, pl.ds(i * rows, rows)],
            dst_ref=halo_ref.at[:, pl.ds(i * rows, rows)],
            send_sem=sends.at[i], recv_sem=recvs.at[i],
            device_id=(t_next, f), device_id_type=MESH,
        )
        for i in range(pieces)
    ]

    depth = x_ref.shape[0]
    edges = [
        (rcol_ref, left_ref.at[pl.ds(depth, depth)], (t, f_next)),
        (lcol_ref, right_ref.at[pl.ds(depth, depth)], (t, f_prev)),
        (rcol_ref, left_ref.at[pl.ds(0, depth)], (t_next, f_next)),
        (lcol_ref, right_ref.at[pl.ds(0, depth)], (t_next, f_prev)),
    ]
    edges = [
        pltpu.make_async_remote_copy(
            src_ref=src, dst_ref=dst, send_sem=esends.at[i], recv_sem=erecvs.at[i],
            device_id=dev, device_id_type=MESH,
        )
        for i, (src, dst, dev) in enumerate(edges)
    ]
    for copy in edges[:2]:
        copy.start()
    halo = halo + edges[2:]

    @pl.when(t < count - 1)
    def _():
        for copy in halo:
            copy.start()

    copies = []
    locals_ = [
        pltpu.make_async_copy(w_ref, wall_ref.at[f], lsems.at[0]),
        pltpu.make_async_copy(m_ref, mall_ref.at[f], lsems.at[1]),
    ]
    for copy in locals_:
        copy.start()
    for k in range(1, groups):
        dev = (t, lax.rem(f + k, groups))
        for src, dst, ss, rs in ((w_ref, wall_ref, wsends, wrecvs), (m_ref, mall_ref, msends, mrecvs)):
            copy = pltpu.make_async_remote_copy(
                src_ref=src, dst_ref=dst.at[f], send_sem=ss.at[k], recv_sem=rs.at[k],
                device_id=dev, device_id_type=MESH,
            )
            copy.start()
            copies.append(copy)
    for copy in locals_:
        copy.wait()
    for copy in copies + edges[:2]:
        copy.wait()

    @pl.when(t < count - 1)
    def _():
        for copy in halo:
            copy.wait_send()

    @pl.when(t > 0)
    def _():
        for copy in halo:
            copy.wait_recv()


def prologue(frames, conv_shard, mix_shard):
    groups = lax.axis_size("fsdp")
    depth, height, width, channels = frames.shape
    lcol = frames[:, :, 0, :]
    rcol = frames[:, :, width - 1, :]
    edge = jax.ShapeDtypeStruct((2 * depth, height, channels), frames.dtype)
    vmem = pl.BlockSpec(memory_space=pltpu.VMEM)
    return pl.pallas_call(
        prologue_kernel,
        out_shape=(
            jax.ShapeDtypeStruct(frames.shape, frames.dtype),
            jax.ShapeDtypeStruct((groups,) + conv_shard.shape, conv_shard.dtype),
            jax.ShapeDtypeStruct((groups,) + mix_shard.shape, mix_shard.dtype),
            edge,
            edge,
        ),
        in_specs=[vmem] * 5,
        out_specs=(vmem,) * 5,
        scratch_shapes=[
            pltpu.SemaphoreType.DMA((4,)),
            pltpu.SemaphoreType.DMA((4,)),
            pltpu.SemaphoreType.DMA((groups,)),
            pltpu.SemaphoreType.DMA((groups,)),
            pltpu.SemaphoreType.DMA((groups,)),
            pltpu.SemaphoreType.DMA((groups,)),
            pltpu.SemaphoreType.DMA((2,)),
            pltpu.SemaphoreType.DMA((4,)),
            pltpu.SemaphoreType.DMA((4,)),
        ],
        compiler_params=pltpu.CompilerParams(collective_id=2, has_side_effects=True),
    )(frames, conv_shard, mix_shard, lcol, rcol)


def local(frames, conv_weight, mix_weight, cotangent):
    t = lax.axis_index("tm")
    count_frames, height, width, channels = frames.shape
    part = conv_weight.shape[-1]
    conv_shard = jnp.swapaxes(conv_weight, 3, 4).reshape(-1, part, channels)
    mix_shard = jnp.swapaxes(mix_weight, 1, 2)
    previous, wall, mall, left, right = prologue(frames, conv_shard, mix_shard)
    full_mix = jnp.transpose(mall, (1, 3, 0, 2)).reshape(mix_weight.shape[:-1] + (-1,))
    pooled = conv_pool(previous, frames, left, right, wall)
    branch = pooled.astype(jnp.float32).reshape(-1, channels)
    flat_cot = cotangent.reshape(-1, channels)
    grad_terms = []
    for offset in range(3):
        lagged = delayed(pooled, offset).reshape(-1, channels)
        branch = branch + jnp.dot(lagged, full_mix[offset], preferred_element_type=jnp.float32)
        grad_terms.append(
            lax.dot_general(
                lagged, flat_cot, (((0,), (0,)), ((), ())), preferred_element_type=jnp.float32
            )
        )
    encoded = branch.astype(jnp.bfloat16).reshape(pooled.shape)
    mix_grad = scatter_sum(jnp.stack(grad_terms).reshape(-1))
    return (encoded, mix_grad)


def solution(mesh):
    return jax.shard_map(
        local,
        mesh=mesh,
        in_specs=(
            P("tm", None, "fsdp", None),
            P(None, None, None, None, "fsdp"),
            P(None, None, "fsdp"),
            P(None, "tm", "fsdp", None),
        ),
        out_specs=(P(None, "tm", "fsdp", None), P(("tm", "fsdp"))),
        check_vma=False,
    )
```

```python
import jax
import jax.numpy as jnp
from jax import lax
from jax.experimental import pallas as pl
from jax.experimental.pallas import tpu as pltpu
from jax.sharding import PartitionSpec as P

MESH = pl.DeviceIdType.MESH


def from_behind(block, axis, distance):
    devices = range(lax.axis_size(axis))
    route = [(i - distance, i) for i in devices if i - distance in devices]
    return lax.ppermute(block, axis, route)


def with_halo(cells, sides, width):
    for axis, dim in sides:
        count = lax.axis_size(axis)
        ends = count - 1
        head = lax.slice_in_dim(cells, 0, width, axis=dim)
        tail = lax.slice_in_dim(cells, cells.shape[dim] - width, cells.shape[dim], axis=dim)
        cells = jnp.concatenate(
            [
                lax.ppermute(tail, axis, [(i, (i + 1) % count) for i in range(ends)]),
                cells,
                lax.ppermute(head, axis, [((i + 1) % count, i) for i in range(ends)]),
            ],
            axis=dim,
        )
    return cells


def pool_pairs(hidden):
    shaped = hidden.reshape((hidden.shape[0] // 2, 2) + hidden.shape[1:]).astype(jnp.float32)
    return ((shaped[:, 0] + shaped[:, 1]) * 0.5).astype(jnp.bfloat16)


def delayed(block, offset):
    return jnp.pad(block, ((offset, 0), (0, 0), (0, 0), (0, 0)))[: block.shape[0]]


def scatter_kernel(p_ref, o_ref, first, second, summed, s1, r1, s2, r2, l1, l2):
    count, groups = first.shape[0], second.shape[0]
    t, f = lax.axis_index("tm"), lax.axis_index("fsdp")
    barrier = pltpu.get_barrier_semaphore()
    for k in range(1, count):
        pl.semaphore_signal(
            barrier, inc=1, device_id={"tm": lax.rem(t + k, count)}, device_id_type=MESH
        )
    for k in range(1, groups):
        pl.semaphore_signal(
            barrier, inc=1, device_id={"fsdp": lax.rem(f + k, groups)}, device_id_type=MESH
        )
    pl.semaphore_wait(barrier, groups - 1 + count - 1)
    local = pltpu.make_async_copy(p_ref.at[t], first.at[t], l1)
    local.start()
    copies = []
    for k in range(1, count):
        peer = lax.rem(t + k, count)
        copy = pltpu.make_async_remote_copy(
            src_ref=p_ref.at[peer], dst_ref=first.at[t], send_sem=s1.at[k], recv_sem=r1.at[k],
            device_id={"tm": peer}, device_id_type=MESH,
        )
        copy.start()
        copies.append(copy)
    local.wait()
    for copy in copies:
        copy.wait()
    summed[...] = jnp.sum(first[...], axis=0)
    local = pltpu.make_async_copy(summed, second.at[f], l2)
    local.start()
    copies = []
    for k in range(1, groups):
        peer = lax.rem(f + k, groups)
        copy = pltpu.make_async_remote_copy(
            src_ref=summed, dst_ref=second.at[f], send_sem=s2.at[k], recv_sem=r2.at[k],
            device_id={"fsdp": peer}, device_id_type=MESH,
        )
        copy.start()
        copies.append(copy)
    local.wait()
    for copy in copies:
        copy.wait()
    o_ref[...] = jnp.sum(second[...], axis=0)


def scatter_sum(partial):
    groups, count = lax.axis_size("fsdp"), lax.axis_size("tm")
    rows = partial.size // (count * 128)
    out = pl.pallas_call(
        scatter_kernel,
        out_shape=jax.ShapeDtypeStruct((rows, 128), jnp.float32),
        in_specs=[pl.BlockSpec(memory_space=pltpu.VMEM)],
        out_specs=pl.BlockSpec(memory_space=pltpu.VMEM),
        scratch_shapes=[
            pltpu.VMEM((count, rows, 128), jnp.float32),
            pltpu.VMEM((groups, rows, 128), jnp.float32),
            pltpu.VMEM((rows, 128), jnp.float32),
            pltpu.SemaphoreType.DMA((count,)),
            pltpu.SemaphoreType.DMA((count,)),
            pltpu.SemaphoreType.DMA((groups,)),
            pltpu.SemaphoreType.DMA((groups,)),
            pltpu.SemaphoreType.DMA,
            pltpu.SemaphoreType.DMA,
        ],
        compiler_params=pltpu.CompilerParams(collective_id=1, has_side_effects=True),
    )(partial.reshape(count, rows, 128))
    piece = partial.size // (count * groups)
    return lax.dynamic_slice_in_dim(out.reshape(-1), lax.axis_index("fsdp") * piece, piece)


def conv_pool_kernel(h_ref, x_ref, l_ref, r_ref, wall_ref, o_ref, xs_ref, pooled_ref, w_ref, sends, recvs, local_sem):
    height, width, channels = pooled_ref.shape
    count, per_dev = o_ref.shape[0], o_ref.shape[1]
    me = lax.axis_index("tm")
    barrier = pltpu.get_barrier_semaphore()
    for k in range(1, count):
        pl.semaphore_signal(
            barrier, inc=1, device_id={"tm": lax.rem(me + k, count)}, device_id_type=MESH
        )
    depth = x_ref.shape[0]
    groups = lax.axis_size("fsdp")
    for tap in range(9):
        w_ref[tap] = jnp.concatenate(
            [wall_ref[:, a * 9 + tap].reshape(w_ref.shape[1], channels) for a in range(3)], axis=-1
        )
    t, f = lax.axis_index("tm"), lax.axis_index("fsdp")
    rows = 8
    zero_rows = jnp.zeros((3, 2 * depth, 1, width, channels), xs_ref.dtype)
    xs_ref[:, :, pl.ds(0, 1)] = zero_rows
    xs_ref[:, :, pl.ds(height + 1, 1)] = zero_rows
    col = lax.broadcasted_iota(jnp.int32, (rows, width, channels), 1)

    def shift(r, carry):
        top = pl.multiple_of(r * rows, rows)
        for q in range(2 * depth):
            earlier = q < depth
            src = h_ref if earlier else x_ref
            block = src[q % depth, pl.ds(top, rows)].astype(jnp.float32)
            lft = l_ref[q, pl.ds(top, rows)].astype(jnp.float32)[:, None, :]
            rgt = r_ref[q, pl.ds(top, rows)].astype(jnp.float32)[:, None, :]
            lok, rok = f > 0, f < groups - 1
            if earlier:
                block = jnp.where(t > 0, block, 0.0)
                lok, rok = lok & (t > 0), rok & (t > 0)
            lft = jnp.where(lok, lft, 0.0)
            rgt = jnp.where(rok, rgt, 0.0)
            moved = [
                jnp.where(col == 0, lft, pltpu.roll(block, 1, 1)),
                block,
                jnp.where(col == width - 1, rgt, pltpu.roll(block, width - 1, 1)),
            ]
            for c in range(3):
                xs_ref[c, q, pl.ds(top + 1, rows)] = moved[c].astype(xs_ref.dtype)
        return carry

    lax.fori_loop(0, height // rows, shift, 0)
    pl.semaphore_wait(barrier, count - 1)

    chunks, spread = height // rows, rows // per_dev

    def body(step, carry):
        r = lax.rem(step + me // spread + 1, chunks)
        top = pl.multiple_of(r * rows, rows)
        span = rows * width
        acc = jnp.zeros((2 * span, channels), jnp.float32)
        for b in range(3):
            for c in range(3):
                lhs = jnp.concatenate(
                    [
                        jnp.concatenate(
                            [xs_ref[c, j + a, pl.ds(top + b, rows)] for a in range(3)], axis=-1
                        ).reshape(span, 3 * channels)
                        for j in range(2)
                    ],
                    axis=0,
                )
                acc = acc + lax.dot_general(
                    lhs, w_ref[b * 3 + c], (((1,), (1,)), ((), ())),
                    preferred_element_type=jnp.float32,
                )
        silu = (acc / (1.0 + jnp.exp(-acc))).astype(jnp.bfloat16).astype(jnp.float32)
        pooled = ((silu[:span] + silu[span:]) * 0.5).astype(o_ref.dtype)
        pooled_ref[pl.ds(top, rows)] = pooled.reshape(rows, width, channels)
        for i in range(rows // per_dev):
            dest = r * (rows // per_dev) + i
            src = pooled_ref.at[pl.ds(top + i * per_dev, per_dev)]

            @pl.when(dest != me)
            def _():
                pltpu.make_async_remote_copy(
                    src_ref=src, dst_ref=o_ref.at[me], send_sem=sends.at[dest],
                    recv_sem=recvs.at[me], device_id={"tm": dest}, device_id_type=MESH,
                ).start()

            @pl.when(dest == me)
            def _():
                local = pltpu.make_async_copy(src, o_ref.at[me], local_sem)
                local.start()
                local.wait()

        return carry

    lax.fori_loop(0, height // rows, body, 0)

    @pl.loop(1, count)
    def _(k):
        peer = lax.rem(me + k, count)
        copy = pltpu.make_async_remote_copy(
            src_ref=pooled_ref.at[pl.ds(0, per_dev)], dst_ref=o_ref.at[peer],
            send_sem=sends.at[peer], recv_sem=recvs.at[peer],
            device_id={"tm": peer}, device_id_type=MESH,
        )
        copy.wait_send()
        copy.wait_recv()


def conv_pool(halo, frames, left, right, wall):
    depth, height, width, channels = frames.shape
    count = lax.axis_size("tm")
    vmem = pl.BlockSpec(memory_space=pltpu.VMEM)
    cout = wall.shape[0] * wall.shape[2]
    flops = 2 * 2 * height * width * 27 * channels * cout
    return pl.pallas_call(
        conv_pool_kernel,
        out_shape=jax.ShapeDtypeStruct((count, height // count, width, channels), jnp.bfloat16),
        in_specs=[vmem] * 5,
        out_specs=vmem,
        scratch_shapes=[
            pltpu.VMEM((3, 2 * depth, height + 8, width, channels), frames.dtype),
            pltpu.VMEM((height, width, channels), jnp.bfloat16),
            pltpu.VMEM((9, cout, 3 * channels), wall.dtype),
            pltpu.SemaphoreType.DMA((count,)),
            pltpu.SemaphoreType.DMA((count,)),
            pltpu.SemaphoreType.DMA,
        ],
        cost_estimate=pl.CostEstimate(
            flops=flops,
            transcendentals=2 * height * width * channels,
            bytes_accessed=4 * frames.size + wall.size * 2 + height * width * channels * 2,
        ),
        compiler_params=pltpu.CompilerParams(collective_id=3, has_side_effects=True),
    )(halo, frames, left, right, wall)


def prologue_kernel(x_ref, w_ref, m_ref, halo_ref, wall_ref, mall_ref, left_ref, right_ref, lcol_ref, rcol_ref, sends, recvs, wsends, wrecvs, msends, mrecvs, lsems, esends, erecvs):
    lcol_ref[...] = x_ref[:, :, 0, :]
    rcol_ref[...] = x_ref[:, :, x_ref.shape[2] - 1, :]
    count, groups = lax.axis_size("tm"), lax.axis_size("fsdp")
    t, f = lax.axis_index("tm"), lax.axis_index("fsdp")
    t_next, t_prev = lax.rem(t + 1, count), lax.rem(t + count - 1, count)
    f_next, f_prev = lax.rem(f + 1, groups), lax.rem(f + groups - 1, groups)
    peers = [(t_next, f), (t_prev, f)] + [(t, lax.rem(f + k, groups)) for k in range(1, groups)]
    peers += [(a, b) for a in (t_next, t_prev) for b in (f_next, f_prev)]
    barrier = pltpu.get_barrier_semaphore()
    for dev in peers:
        pl.semaphore_signal(barrier, inc=1, device_id=dev, device_id_type=MESH)
    pl.semaphore_wait(barrier, len(peers))
    pieces = sends.shape[0]
    rows = x_ref.shape[1] // pieces
    halo = [
        pltpu.make_async_remote_copy(
            src_ref=x_ref.at[:, pl.ds(i * rows, rows)],
            dst_ref=halo_ref.at[:, pl.ds(i * rows, rows)],
            send_sem=sends.at[i], recv_sem=recvs.at[i],
            device_id=(t_next, f), device_id_type=MESH,
        )
        for i in range(pieces)
    ]

    depth = x_ref.shape[0]
    edges = [
        (rcol_ref, left_ref.at[pl.ds(depth, depth)], (t, f_next)),
        (lcol_ref, right_ref.at[pl.ds(depth, depth)], (t, f_prev)),
        (rcol_ref, left_ref.at[pl.ds(0, depth)], (t_next, f_next)),
        (lcol_ref, right_ref.at[pl.ds(0, depth)], (t_next, f_prev)),
    ]
    edges = [
        pltpu.make_async_remote_copy(
            src_ref=src, dst_ref=dst, send_sem=esends.at[i], recv_sem=erecvs.at[i],
            device_id=dev, device_id_type=MESH,
        )
        for i, (src, dst, dev) in enumerate(edges)
    ]
    for copy in edges[:2]:
        copy.start()
    halo = halo + edges[2:]

    @pl.when(t < count - 1)
    def _():
        for copy in halo:
            copy.start()

    copies = []
    locals_ = [
        pltpu.make_async_copy(w_ref, wall_ref.at[f], lsems.at[0]),
        pltpu.make_async_copy(m_ref, mall_ref.at[f], lsems.at[1]),
    ]
    for copy in locals_:
        copy.start()
    for k in range(1, groups):
        dev = (t, lax.rem(f + k, groups))
        for src, dst, ss, rs in ((w_ref, wall_ref, wsends, wrecvs), (m_ref, mall_ref, msends, mrecvs)):
            copy = pltpu.make_async_remote_copy(
                src_ref=src, dst_ref=dst.at[f], send_sem=ss.at[k], recv_sem=rs.at[k],
                device_id=dev, device_id_type=MESH,
            )
            copy.start()
            copies.append(copy)
    for copy in locals_:
        copy.wait()
    for copy in copies + edges[:2]:
        copy.wait()

    @pl.when(t < count - 1)
    def _():
        for copy in halo:
            copy.wait_send()

    @pl.when(t > 0)
    def _():
        for copy in halo:
            copy.wait_recv()


def prologue(frames, conv_shard, mix_shard):
    groups = lax.axis_size("fsdp")
    depth, height, width, channels = frames.shape
    edge = jax.ShapeDtypeStruct((2 * depth, height, channels), frames.dtype)
    vmem = pl.BlockSpec(memory_space=pltpu.VMEM)
    return pl.pallas_call(
        prologue_kernel,
        out_shape=(
            jax.ShapeDtypeStruct(frames.shape, frames.dtype),
            jax.ShapeDtypeStruct((groups,) + conv_shard.shape, conv_shard.dtype),
            jax.ShapeDtypeStruct((groups,) + mix_shard.shape, mix_shard.dtype),
            edge,
            edge,
        ),
        in_specs=[vmem] * 3,
        out_specs=(vmem,) * 5,
        scratch_shapes=[
            pltpu.VMEM((depth, height, channels), frames.dtype),
            pltpu.VMEM((depth, height, channels), frames.dtype),
            pltpu.SemaphoreType.DMA((4,)),
            pltpu.SemaphoreType.DMA((4,)),
            pltpu.SemaphoreType.DMA((groups,)),
            pltpu.SemaphoreType.DMA((groups,)),
            pltpu.SemaphoreType.DMA((groups,)),
            pltpu.SemaphoreType.DMA((groups,)),
            pltpu.SemaphoreType.DMA((2,)),
            pltpu.SemaphoreType.DMA((4,)),
            pltpu.SemaphoreType.DMA((4,)),
        ],
        compiler_params=pltpu.CompilerParams(collective_id=2, has_side_effects=True),
    )(frames, conv_shard, mix_shard)


def local(frames, conv_weight, mix_weight, cotangent):
    t = lax.axis_index("tm")
    count_frames, height, width, channels = frames.shape
    part = conv_weight.shape[-1]
    conv_shard = jnp.swapaxes(conv_weight, 3, 4).reshape(-1, part, channels)
    mix_shard = jnp.swapaxes(mix_weight, 1, 2)
    previous, wall, mall, left, right = prologue(frames, conv_shard, mix_shard)
    full_mix = jnp.transpose(mall, (1, 3, 0, 2)).reshape(mix_weight.shape[:-1] + (-1,))
    pooled = conv_pool(previous, frames, left, right, wall)
    branch = pooled.astype(jnp.float32).reshape(-1, channels)
    flat_cot = cotangent.reshape(-1, channels)
    grad_terms = []
    for offset in range(3):
        lagged = delayed(pooled, offset).reshape(-1, channels)
        branch = branch + jnp.dot(lagged, full_mix[offset], preferred_element_type=jnp.float32)
        grad_terms.append(
            lax.dot_general(
                lagged, flat_cot, (((0,), (0,)), ((), ())), preferred_element_type=jnp.float32
            )
        )
    encoded = branch.astype(jnp.bfloat16).reshape(pooled.shape)
    mix_grad = scatter_sum(jnp.stack(grad_terms).reshape(-1))
    return (encoded, mix_grad)


def solution(mesh):
    return jax.shard_map(
        local,
        mesh=mesh,
        in_specs=(
            P("tm", None, "fsdp", None),
            P(None, None, None, None, "fsdp"),
            P(None, None, "fsdp"),
            P(None, "tm", "fsdp", None),
        ),
        out_specs=(P(None, "tm", "fsdp", None), P(("tm", "fsdp"))),
        check_vma=False,
    )
```

```python
import jax
import jax.numpy as jnp
from jax import lax
from jax.experimental import pallas as pl
from jax.experimental.pallas import tpu as pltpu
from jax.sharding import PartitionSpec as P

MESH = pl.DeviceIdType.MESH


def from_behind(block, axis, distance):
    devices = range(lax.axis_size(axis))
    route = [(i - distance, i) for i in devices if i - distance in devices]
    return lax.ppermute(block, axis, route)


def with_halo(cells, sides, width):
    for axis, dim in sides:
        count = lax.axis_size(axis)
        ends = count - 1
        head = lax.slice_in_dim(cells, 0, width, axis=dim)
        tail = lax.slice_in_dim(cells, cells.shape[dim] - width, cells.shape[dim], axis=dim)
        cells = jnp.concatenate(
            [
                lax.ppermute(tail, axis, [(i, (i + 1) % count) for i in range(ends)]),
                cells,
                lax.ppermute(head, axis, [((i + 1) % count, i) for i in range(ends)]),
            ],
            axis=dim,
        )
    return cells


def pool_pairs(hidden):
    shaped = hidden.reshape((hidden.shape[0] // 2, 2) + hidden.shape[1:]).astype(jnp.float32)
    return ((shaped[:, 0] + shaped[:, 1]) * 0.5).astype(jnp.bfloat16)


def delayed(block, offset):
    return jnp.pad(block, ((offset, 0), (0, 0), (0, 0), (0, 0)))[: block.shape[0]]


def scatter_kernel(p_ref, o_ref, first, second, summed, s1, r1, s2, r2, l1, l2):
    count, groups = first.shape[0], second.shape[0]
    t, f = lax.axis_index("tm"), lax.axis_index("fsdp")
    barrier = pltpu.get_barrier_semaphore()
    for k in range(1, count):
        pl.semaphore_signal(
            barrier, inc=1, device_id={"tm": lax.rem(t + k, count)}, device_id_type=MESH
        )
    for k in range(1, groups):
        pl.semaphore_signal(
            barrier, inc=1, device_id={"fsdp": lax.rem(f + k, groups)}, device_id_type=MESH
        )
    pl.semaphore_wait(barrier, groups - 1 + count - 1)
    local = pltpu.make_async_copy(p_ref.at[t], first.at[t], l1)
    local.start()
    copies = []
    for k in range(1, count):
        peer = lax.rem(t + k, count)
        copy = pltpu.make_async_remote_copy(
            src_ref=p_ref.at[peer], dst_ref=first.at[t], send_sem=s1.at[k], recv_sem=r1.at[k],
            device_id={"tm": peer}, device_id_type=MESH,
        )
        copy.start()
        copies.append(copy)
    local.wait()
    for copy in copies:
        copy.wait()
    summed[...] = jnp.sum(first[...], axis=0)
    local = pltpu.make_async_copy(summed, second.at[f], l2)
    local.start()
    copies = []
    for k in range(1, groups):
        peer = lax.rem(f + k, groups)
        copy = pltpu.make_async_remote_copy(
            src_ref=summed, dst_ref=second.at[f], send_sem=s2.at[k], recv_sem=r2.at[k],
            device_id={"fsdp": peer}, device_id_type=MESH,
        )
        copy.start()
        copies.append(copy)
    local.wait()
    for copy in copies:
        copy.wait()
    summed[...] = jnp.sum(second[...], axis=0)
    per = o_ref.shape[0]
    o_ref[...] = summed[pl.ds(pl.multiple_of(f * per, per), per)]


def scatter_sum(partial):
    groups, count = lax.axis_size("fsdp"), lax.axis_size("tm")
    piece = partial.size // (count * groups)
    wide = -(-piece // 128) * 128
    arranged = jnp.pad(partial.reshape(count, groups, piece), ((0, 0), (0, 0), (0, wide - piece)))
    rows = groups * wide // 128
    out = pl.pallas_call(
        scatter_kernel,
        out_shape=jax.ShapeDtypeStruct((wide // 128, 128), jnp.float32),
        in_specs=[pl.BlockSpec(memory_space=pltpu.VMEM)],
        out_specs=pl.BlockSpec(memory_space=pltpu.VMEM),
        scratch_shapes=[
            pltpu.VMEM((count, rows, 128), jnp.float32),
            pltpu.VMEM((groups, rows, 128), jnp.float32),
            pltpu.VMEM((rows, 128), jnp.float32),
            pltpu.SemaphoreType.DMA((count,)),
            pltpu.SemaphoreType.DMA((count,)),
            pltpu.SemaphoreType.DMA((groups,)),
            pltpu.SemaphoreType.DMA((groups,)),
            pltpu.SemaphoreType.DMA,
            pltpu.SemaphoreType.DMA,
        ],
        compiler_params=pltpu.CompilerParams(collective_id=1, has_side_effects=True),
    )(arranged.reshape(count, rows, 128))
    return out.reshape(-1)[:piece]


def conv_pool_kernel(h_ref, x_ref, l_ref, r_ref, wall_ref, o_ref, xs_ref, pooled_ref, w_ref, sends, recvs, local_sem):
    height, width, channels = pooled_ref.shape
    count, per_dev = o_ref.shape[0], o_ref.shape[1]
    me = lax.axis_index("tm")
    barrier = pltpu.get_barrier_semaphore()
    for k in range(1, count):
        pl.semaphore_signal(
            barrier, inc=1, device_id={"tm": lax.rem(me + k, count)}, device_id_type=MESH
        )
    depth = x_ref.shape[0]
    groups = lax.axis_size("fsdp")
    for tap in range(9):
        w_ref[tap] = jnp.concatenate(
            [wall_ref[:, a * 9 + tap].reshape(w_ref.shape[1], channels) for a in range(3)], axis=-1
        )
    t, f = lax.axis_index("tm"), lax.axis_index("fsdp")
    rows = 8
    zero_rows = jnp.zeros((3, 2 * depth, 1, width, channels), xs_ref.dtype)
    xs_ref[:, :, pl.ds(0, 1)] = zero_rows
    xs_ref[:, :, pl.ds(height + 1, 1)] = zero_rows
    col = lax.broadcasted_iota(jnp.int32, (rows, width, channels), 1)

    def shift(r, carry):
        top = pl.multiple_of(r * rows, rows)
        for q in range(2 * depth):
            earlier = q < depth
            src = h_ref if earlier else x_ref
            block = src[q % depth, pl.ds(top, rows)].astype(jnp.float32)
            lft = l_ref[q, pl.ds(top, rows)].astype(jnp.float32)[:, None, :]
            rgt = r_ref[q, pl.ds(top, rows)].astype(jnp.float32)[:, None, :]
            lok, rok = f > 0, f < groups - 1
            if earlier:
                block = jnp.where(t > 0, block, 0.0)
                lok, rok = lok & (t > 0), rok & (t > 0)
            lft = jnp.where(lok, lft, 0.0)
            rgt = jnp.where(rok, rgt, 0.0)
            moved = [
                jnp.where(col == 0, lft, pltpu.roll(block, 1, 1)),
                block,
                jnp.where(col == width - 1, rgt, pltpu.roll(block, width - 1, 1)),
            ]
            for c in range(3):
                xs_ref[c, q, pl.ds(top + 1, rows)] = moved[c].astype(xs_ref.dtype)
        return carry

    lax.fori_loop(0, height // rows, shift, 0)
    pl.semaphore_wait(barrier, count - 1)

    chunks, spread = height // rows, rows // per_dev

    def body(step, carry):
        r = lax.rem(step + me // spread + 1, chunks)
        top = pl.multiple_of(r * rows, rows)
        span = rows * width
        acc = jnp.zeros((2 * span, channels), jnp.float32)
        for b in range(3):
            for c in range(3):
                lhs = jnp.concatenate(
                    [
                        jnp.concatenate(
                            [xs_ref[c, j + a, pl.ds(top + b, rows)] for a in range(3)], axis=-1
                        ).reshape(span, 3 * channels)
                        for j in range(2)
                    ],
                    axis=0,
                )
                acc = acc + lax.dot_general(
                    lhs, w_ref[b * 3 + c], (((1,), (1,)), ((), ())),
                    preferred_element_type=jnp.float32,
                )
        silu = (acc / (1.0 + jnp.exp(-acc))).astype(jnp.bfloat16).astype(jnp.float32)
        pooled = ((silu[:span] + silu[span:]) * 0.5).astype(o_ref.dtype)
        pooled_ref[pl.ds(top, rows)] = pooled.reshape(rows, width, channels)
        for i in range(rows // per_dev):
            dest = r * (rows // per_dev) + i
            src = pooled_ref.at[pl.ds(top + i * per_dev, per_dev)]

            @pl.when(dest != me)
            def _():
                pltpu.make_async_remote_copy(
                    src_ref=src, dst_ref=o_ref.at[me], send_sem=sends.at[dest],
                    recv_sem=recvs.at[me], device_id={"tm": dest}, device_id_type=MESH,
                ).start()

            @pl.when(dest == me)
            def _():
                local = pltpu.make_async_copy(src, o_ref.at[me], local_sem)
                local.start()
                local.wait()

        return carry

    lax.fori_loop(0, height // rows, body, 0)

    @pl.loop(1, count)
    def _(k):
        peer = lax.rem(me + k, count)
        copy = pltpu.make_async_remote_copy(
            src_ref=pooled_ref.at[pl.ds(0, per_dev)], dst_ref=o_ref.at[peer],
            send_sem=sends.at[peer], recv_sem=recvs.at[peer],
            device_id={"tm": peer}, device_id_type=MESH,
        )
        copy.wait_send()
        copy.wait_recv()


def conv_pool(halo, frames, left, right, wall):
    depth, height, width, channels = frames.shape
    count = lax.axis_size("tm")
    vmem = pl.BlockSpec(memory_space=pltpu.VMEM)
    cout = wall.shape[0] * wall.shape[2]
    flops = 2 * 2 * height * width * 27 * channels * cout
    return pl.pallas_call(
        conv_pool_kernel,
        out_shape=jax.ShapeDtypeStruct((count, height // count, width, channels), jnp.bfloat16),
        in_specs=[vmem] * 5,
        out_specs=vmem,
        scratch_shapes=[
            pltpu.VMEM((3, 2 * depth, height + 8, width, channels), frames.dtype),
            pltpu.VMEM((height, width, channels), jnp.bfloat16),
            pltpu.VMEM((9, cout, 3 * channels), wall.dtype),
            pltpu.SemaphoreType.DMA((count,)),
            pltpu.SemaphoreType.DMA((count,)),
            pltpu.SemaphoreType.DMA,
        ],
        cost_estimate=pl.CostEstimate(
            flops=flops,
            transcendentals=2 * height * width * channels,
            bytes_accessed=4 * frames.size + wall.size * 2 + height * width * channels * 2,
        ),
        compiler_params=pltpu.CompilerParams(collective_id=3, has_side_effects=True),
    )(halo, frames, left, right, wall)


def prologue_kernel(x_ref, w_ref, m_ref, halo_ref, wall_ref, mall_ref, left_ref, right_ref, lcol_ref, rcol_ref, sends, recvs, wsends, wrecvs, msends, mrecvs, lsems, esends, erecvs):
    lcol_ref[...] = x_ref[:, :, 0, :]
    rcol_ref[...] = x_ref[:, :, x_ref.shape[2] - 1, :]
    count, groups = lax.axis_size("tm"), lax.axis_size("fsdp")
    t, f = lax.axis_index("tm"), lax.axis_index("fsdp")
    t_next, t_prev = lax.rem(t + 1, count), lax.rem(t + count - 1, count)
    f_next, f_prev = lax.rem(f + 1, groups), lax.rem(f + groups - 1, groups)
    peers = [(t_next, f), (t_prev, f)] + [(t, lax.rem(f + k, groups)) for k in range(1, groups)]
    peers += [(a, b) for a in (t_next, t_prev) for b in (f_next, f_prev)]
    barrier = pltpu.get_barrier_semaphore()
    for dev in peers:
        pl.semaphore_signal(barrier, inc=1, device_id=dev, device_id_type=MESH)
    pl.semaphore_wait(barrier, len(peers))
    pieces = sends.shape[0]
    rows = x_ref.shape[1] // pieces
    halo = [
        pltpu.make_async_remote_copy(
            src_ref=x_ref.at[:, pl.ds(i * rows, rows)],
            dst_ref=halo_ref.at[:, pl.ds(i * rows, rows)],
            send_sem=sends.at[i], recv_sem=recvs.at[i],
            device_id=(t_next, f), device_id_type=MESH,
        )
        for i in range(pieces)
    ]

    depth = x_ref.shape[0]
    edges = [
        (rcol_ref, left_ref.at[pl.ds(depth, depth)], (t, f_next)),
        (lcol_ref, right_ref.at[pl.ds(depth, depth)], (t, f_prev)),
        (rcol_ref, left_ref.at[pl.ds(0, depth)], (t_next, f_next)),
        (lcol_ref, right_ref.at[pl.ds(0, depth)], (t_next, f_prev)),
    ]
    edges = [
        pltpu.make_async_remote_copy(
            src_ref=src, dst_ref=dst, send_sem=esends.at[i], recv_sem=erecvs.at[i],
            device_id=dev, device_id_type=MESH,
        )
        for i, (src, dst, dev) in enumerate(edges)
    ]
    for copy in edges[:2]:
        copy.start()
    halo = halo + edges[2:]

    @pl.when(t < count - 1)
    def _():
        for copy in halo:
            copy.start()

    copies = []
    locals_ = [
        pltpu.make_async_copy(w_ref, wall_ref.at[f], lsems.at[0]),
        pltpu.make_async_copy(m_ref, mall_ref.at[f], lsems.at[1]),
    ]
    for copy in locals_:
        copy.start()
    for k in range(1, groups):
        dev = (t, lax.rem(f + k, groups))
        for src, dst, ss, rs in ((w_ref, wall_ref, wsends, wrecvs), (m_ref, mall_ref, msends, mrecvs)):
            copy = pltpu.make_async_remote_copy(
                src_ref=src, dst_ref=dst.at[f], send_sem=ss.at[k], recv_sem=rs.at[k],
                device_id=dev, device_id_type=MESH,
            )
            copy.start()
            copies.append(copy)
    for copy in locals_:
        copy.wait()
    for copy in copies + edges[:2]:
        copy.wait()

    @pl.when(t < count - 1)
    def _():
        for copy in halo:
            copy.wait_send()

    @pl.when(t > 0)
    def _():
        for copy in halo:
            copy.wait_recv()


def prologue(frames, conv_shard, mix_shard):
    groups = lax.axis_size("fsdp")
    depth, height, width, channels = frames.shape
    edge = jax.ShapeDtypeStruct((2 * depth, height, channels), frames.dtype)
    vmem = pl.BlockSpec(memory_space=pltpu.VMEM)
    return pl.pallas_call(
        prologue_kernel,
        out_shape=(
            jax.ShapeDtypeStruct(frames.shape, frames.dtype),
            jax.ShapeDtypeStruct((groups,) + conv_shard.shape, conv_shard.dtype),
            jax.ShapeDtypeStruct((groups,) + mix_shard.shape, mix_shard.dtype),
            edge,
            edge,
        ),
        in_specs=[vmem] * 3,
        out_specs=(vmem,) * 5,
        scratch_shapes=[
            pltpu.VMEM((depth, height, channels), frames.dtype),
            pltpu.VMEM((depth, height, channels), frames.dtype),
            pltpu.SemaphoreType.DMA((4,)),
            pltpu.SemaphoreType.DMA((4,)),
            pltpu.SemaphoreType.DMA((groups,)),
            pltpu.SemaphoreType.DMA((groups,)),
            pltpu.SemaphoreType.DMA((groups,)),
            pltpu.SemaphoreType.DMA((groups,)),
            pltpu.SemaphoreType.DMA((2,)),
            pltpu.SemaphoreType.DMA((4,)),
            pltpu.SemaphoreType.DMA((4,)),
        ],
        compiler_params=pltpu.CompilerParams(collective_id=2, has_side_effects=True),
    )(frames, conv_shard, mix_shard)


def local(frames, conv_weight, mix_weight, cotangent):
    t = lax.axis_index("tm")
    count_frames, height, width, channels = frames.shape
    part = conv_weight.shape[-1]
    conv_shard = jnp.swapaxes(conv_weight, 3, 4).reshape(-1, part, channels)
    mix_shard = jnp.swapaxes(mix_weight, 1, 2)
    previous, wall, mall, left, right = prologue(frames, conv_shard, mix_shard)
    full_mix = jnp.transpose(mall, (1, 3, 0, 2)).reshape(mix_weight.shape[:-1] + (-1,))
    pooled = conv_pool(previous, frames, left, right, wall)
    branch = pooled.astype(jnp.float32).reshape(-1, channels)
    flat_cot = cotangent.reshape(-1, channels)
    grad_terms = []
    for offset in range(3):
        lagged = delayed(pooled, offset).reshape(-1, channels)
        branch = branch + jnp.dot(lagged, full_mix[offset], preferred_element_type=jnp.float32)
        grad_terms.append(
            lax.dot_general(
                lagged, flat_cot, (((0,), (0,)), ((), ())), preferred_element_type=jnp.float32
            )
        )
    encoded = branch.astype(jnp.bfloat16).reshape(pooled.shape)
    mix_grad = scatter_sum(jnp.stack(grad_terms).reshape(-1))
    return (encoded, mix_grad)


def solution(mesh):
    return jax.shard_map(
        local,
        mesh=mesh,
        in_specs=(
            P("tm", None, "fsdp", None),
            P(None, None, None, None, "fsdp"),
            P(None, None, "fsdp"),
            P(None, "tm", "fsdp", None),
        ),
        out_specs=(P(None, "tm", "fsdp", None), P(("tm", "fsdp"))),
        check_vma=False,
    )
```

```python
import jax
import jax.numpy as jnp
from jax import lax
from jax.experimental import pallas as pl
from jax.experimental.pallas import tpu as pltpu
from jax.sharding import PartitionSpec as P

MESH = pl.DeviceIdType.MESH


def from_behind(block, axis, distance):
    devices = range(lax.axis_size(axis))
    route = [(i - distance, i) for i in devices if i - distance in devices]
    return lax.ppermute(block, axis, route)


def with_halo(cells, sides, width):
    for axis, dim in sides:
        count = lax.axis_size(axis)
        ends = count - 1
        head = lax.slice_in_dim(cells, 0, width, axis=dim)
        tail = lax.slice_in_dim(cells, cells.shape[dim] - width, cells.shape[dim], axis=dim)
        cells = jnp.concatenate(
            [
                lax.ppermute(tail, axis, [(i, (i + 1) % count) for i in range(ends)]),
                cells,
                lax.ppermute(head, axis, [((i + 1) % count, i) for i in range(ends)]),
            ],
            axis=dim,
        )
    return cells


def pool_pairs(hidden):
    shaped = hidden.reshape((hidden.shape[0] // 2, 2) + hidden.shape[1:]).astype(jnp.float32)
    return ((shaped[:, 0] + shaped[:, 1]) * 0.5).astype(jnp.bfloat16)


def delayed(block, offset):
    return jnp.pad(block, ((offset, 0), (0, 0), (0, 0), (0, 0)))[: block.shape[0]]


def scatter_kernel(p_ref, o_ref, first, second, summed, s1, r1, s2, r2, l1, l2):
    count, groups = first.shape[0], second.shape[0]
    t, f = lax.axis_index("tm"), lax.axis_index("fsdp")
    barrier = pltpu.get_barrier_semaphore()
    for k in range(1, count):
        pl.semaphore_signal(
            barrier, inc=1, device_id={"tm": lax.rem(t + k, count)}, device_id_type=MESH
        )
    for k in range(1, groups):
        pl.semaphore_signal(
            barrier, inc=1, device_id={"fsdp": lax.rem(f + k, groups)}, device_id_type=MESH
        )
    pl.semaphore_wait(barrier, groups - 1 + count - 1)
    local = pltpu.make_async_copy(p_ref.at[t], first.at[t], l1)
    local.start()
    copies = []
    for k in range(1, count):
        peer = lax.rem(t + k, count)
        copy = pltpu.make_async_remote_copy(
            src_ref=p_ref.at[peer], dst_ref=first.at[t], send_sem=s1.at[k], recv_sem=r1.at[k],
            device_id={"tm": peer}, device_id_type=MESH,
        )
        copy.start()
        copies.append(copy)
    local.wait()
    for copy in copies:
        copy.wait()
    summed[...] = jnp.sum(first[...], axis=0)
    local = pltpu.make_async_copy(summed, second.at[f], l2)
    local.start()
    copies = []
    for k in range(1, groups):
        peer = lax.rem(f + k, groups)
        copy = pltpu.make_async_remote_copy(
            src_ref=summed, dst_ref=second.at[f], send_sem=s2.at[k], recv_sem=r2.at[k],
            device_id={"fsdp": peer}, device_id_type=MESH,
        )
        copy.start()
        copies.append(copy)
    local.wait()
    for copy in copies:
        copy.wait()
    o_ref[...] = jnp.sum(second[...], axis=0)


def scatter_sum(partial):
    groups, count = lax.axis_size("fsdp"), lax.axis_size("tm")
    rows = partial.size // (count * 128)
    out = pl.pallas_call(
        scatter_kernel,
        out_shape=jax.ShapeDtypeStruct((rows, 128), jnp.float32),
        in_specs=[pl.BlockSpec(memory_space=pltpu.VMEM)],
        out_specs=pl.BlockSpec(memory_space=pltpu.VMEM),
        scratch_shapes=[
            pltpu.VMEM((count, rows, 128), jnp.float32),
            pltpu.VMEM((groups, rows, 128), jnp.float32),
            pltpu.VMEM((rows, 128), jnp.float32),
            pltpu.SemaphoreType.DMA((count,)),
            pltpu.SemaphoreType.DMA((count,)),
            pltpu.SemaphoreType.DMA((groups,)),
            pltpu.SemaphoreType.DMA((groups,)),
            pltpu.SemaphoreType.DMA,
            pltpu.SemaphoreType.DMA,
        ],
        compiler_params=pltpu.CompilerParams(collective_id=1, has_side_effects=True),
    )(partial.reshape(count, rows, 128))
    piece = partial.size // (count * groups)
    return lax.dynamic_slice_in_dim(out.reshape(-1), lax.axis_index("fsdp") * piece, piece)


def conv_pool_kernel(h_ref, x_ref, l_ref, r_ref, wall_ref, o_ref, xs_ref, pooled_ref, w_ref, sends, recvs, local_sem):
    height, width, channels = pooled_ref.shape
    count, per_dev = o_ref.shape[0], o_ref.shape[1]
    me = lax.axis_index("tm")
    barrier = pltpu.get_barrier_semaphore()
    for k in range(1, count):
        pl.semaphore_signal(
            barrier, inc=1, device_id={"tm": lax.rem(me + k, count)}, device_id_type=MESH
        )
    depth = x_ref.shape[0]
    groups = lax.axis_size("fsdp")
    for tap in range(9):
        w_ref[tap] = jnp.concatenate(
            [wall_ref[:, a * 9 + tap].reshape(w_ref.shape[1], channels) for a in range(3)], axis=-1
        )
    t, f = lax.axis_index("tm"), lax.axis_index("fsdp")
    rows = 8
    zero_rows = jnp.zeros((3, 2 * depth, 1, width, channels), xs_ref.dtype)
    xs_ref[:, :, pl.ds(0, 1)] = zero_rows
    xs_ref[:, :, pl.ds(height + 1, 1)] = zero_rows
    col = lax.broadcasted_iota(jnp.int32, (rows, width, channels), 1)

    def shift(r, carry):
        top = pl.multiple_of(r * rows, rows)
        for q in range(2 * depth):
            earlier = q < depth
            src = h_ref if earlier else x_ref
            block = src[q % depth, pl.ds(top, rows)].astype(jnp.float32)
            lft = l_ref[q, pl.ds(top, rows)].astype(jnp.float32)[:, None, :]
            rgt = r_ref[q, pl.ds(top, rows)].astype(jnp.float32)[:, None, :]
            lok, rok = f > 0, f < groups - 1
            if earlier:
                block = jnp.where(t > 0, block, 0.0)
                lok, rok = lok & (t > 0), rok & (t > 0)
            lft = jnp.where(lok, lft, 0.0)
            rgt = jnp.where(rok, rgt, 0.0)
            moved = [
                jnp.where(col == 0, lft, pltpu.roll(block, 1, 1)),
                block,
                jnp.where(col == width - 1, rgt, pltpu.roll(block, width - 1, 1)),
            ]
            for c in range(3):
                xs_ref[c, q, pl.ds(top + 1, rows)] = moved[c].astype(xs_ref.dtype)
        return carry

    lax.fori_loop(0, height // rows, shift, 0)
    pl.semaphore_wait(barrier, count - 1)

    chunks, spread = height // rows, rows // per_dev

    def body(step, carry):
        r = lax.rem(step + me // spread + 1, chunks)
        top = pl.multiple_of(r * rows, rows)
        span = rows * width
        acc = jnp.zeros((2 * span, channels), jnp.float32)
        for b in range(3):
            for c in range(3):
                lhs = jnp.concatenate(
                    [
                        jnp.concatenate(
                            [xs_ref[c, j + a, pl.ds(top + b, rows)] for a in range(3)], axis=-1
                        ).reshape(span, 3 * channels)
                        for j in range(2)
                    ],
                    axis=0,
                )
                acc = acc + lax.dot_general(
                    lhs, w_ref[b * 3 + c], (((1,), (1,)), ((), ())),
                    preferred_element_type=jnp.float32,
                )
        silu = (acc / (1.0 + jnp.exp(-acc))).astype(jnp.bfloat16).astype(jnp.float32)
        pooled = ((silu[:span] + silu[span:]) * 0.5).astype(o_ref.dtype)
        pooled_ref[pl.ds(top, rows)] = pooled.reshape(rows, width, channels)
        for i in range(rows // per_dev):
            dest = r * (rows // per_dev) + i
            src = pooled_ref.at[pl.ds(top + i * per_dev, per_dev)]

            @pl.when(dest != me)
            def _():
                pltpu.make_async_remote_copy(
                    src_ref=src, dst_ref=o_ref.at[me], send_sem=sends.at[dest],
                    recv_sem=recvs.at[me], device_id={"tm": dest}, device_id_type=MESH,
                ).start()

            @pl.when(dest == me)
            def _():
                local = pltpu.make_async_copy(src, o_ref.at[me], local_sem)
                local.start()
                local.wait()

        return carry

    lax.fori_loop(0, height // rows, body, 0)

    @pl.loop(1, count)
    def _(k):
        peer = lax.rem(me + k, count)
        copy = pltpu.make_async_remote_copy(
            src_ref=pooled_ref.at[pl.ds(0, per_dev)], dst_ref=o_ref.at[peer],
            send_sem=sends.at[peer], recv_sem=recvs.at[peer],
            device_id={"tm": peer}, device_id_type=MESH,
        )
        copy.wait_send()
        copy.wait_recv()


def conv_pool(halo, frames, left, right, wall):
    depth, height, width, channels = frames.shape
    count = lax.axis_size("tm")
    vmem = pl.BlockSpec(memory_space=pltpu.VMEM)
    cout = wall.shape[0] * wall.shape[2]
    flops = 2 * 2 * height * width * 27 * channels * cout
    return pl.pallas_call(
        conv_pool_kernel,
        out_shape=jax.ShapeDtypeStruct((count, height // count, width, channels), jnp.bfloat16),
        in_specs=[vmem] * 5,
        out_specs=vmem,
        scratch_shapes=[
            pltpu.VMEM((3, 2 * depth, height + 8, width, channels), frames.dtype),
            pltpu.VMEM((height, width, channels), jnp.bfloat16),
            pltpu.VMEM((9, cout, 3 * channels), wall.dtype),
            pltpu.SemaphoreType.DMA((count,)),
            pltpu.SemaphoreType.DMA((count,)),
            pltpu.SemaphoreType.DMA,
        ],
        cost_estimate=pl.CostEstimate(
            flops=flops,
            transcendentals=2 * height * width * channels,
            bytes_accessed=4 * frames.size + wall.size * 2 + height * width * channels * 2,
        ),
        compiler_params=pltpu.CompilerParams(collective_id=3, has_side_effects=True),
    )(halo, frames, left, right, wall)


def prologue_kernel(x_ref, w_ref, m_ref, halo_ref, wall_ref, mall_ref, left_ref, right_ref, lcol_ref, rcol_ref, sends, recvs, wsends, wrecvs, msends, mrecvs, lsems, esends, erecvs):
    lcol_ref[...] = x_ref[:, :, 0, :]
    rcol_ref[...] = x_ref[:, :, x_ref.shape[2] - 1, :]
    count, groups = lax.axis_size("tm"), lax.axis_size("fsdp")
    t, f = lax.axis_index("tm"), lax.axis_index("fsdp")
    t_next, t_prev = lax.rem(t + 1, count), lax.rem(t + count - 1, count)
    f_next, f_prev = lax.rem(f + 1, groups), lax.rem(f + groups - 1, groups)
    peers = [(t_next, f), (t_prev, f)] + [(t, lax.rem(f + k, groups)) for k in range(1, groups)]
    peers += [(a, b) for a in (t_next, t_prev) for b in (f_next, f_prev)]
    barrier = pltpu.get_barrier_semaphore()
    for dev in peers:
        pl.semaphore_signal(barrier, inc=1, device_id=dev, device_id_type=MESH)
    pl.semaphore_wait(barrier, len(peers))
    pieces = sends.shape[0]
    rows = x_ref.shape[1] // pieces
    halo = [
        pltpu.make_async_remote_copy(
            src_ref=x_ref.at[:, pl.ds(i * rows, rows)],
            dst_ref=halo_ref.at[:, pl.ds(i * rows, rows)],
            send_sem=sends.at[i], recv_sem=recvs.at[i],
            device_id=(t_next, f), device_id_type=MESH,
        )
        for i in range(pieces)
    ]

    depth = x_ref.shape[0]
    edges = [
        (rcol_ref, left_ref.at[pl.ds(depth, depth)], (t, f_next)),
        (lcol_ref, right_ref.at[pl.ds(depth, depth)], (t, f_prev)),
        (rcol_ref, left_ref.at[pl.ds(0, depth)], (t_next, f_next)),
        (lcol_ref, right_ref.at[pl.ds(0, depth)], (t_next, f_prev)),
    ]
    edges = [
        pltpu.make_async_remote_copy(
            src_ref=src, dst_ref=dst, send_sem=esends.at[i], recv_sem=erecvs.at[i],
            device_id=dev, device_id_type=MESH,
        )
        for i, (src, dst, dev) in enumerate(edges)
    ]
    halo = halo + edges[2:]

    @pl.when(t < count - 1)
    def _():
        for copy in halo:
            copy.start()

    for copy in edges[:2]:
        copy.start()

    copies = []
    locals_ = [
        pltpu.make_async_copy(w_ref, wall_ref.at[f], lsems.at[0]),
        pltpu.make_async_copy(m_ref, mall_ref.at[f], lsems.at[1]),
    ]
    for copy in locals_:
        copy.start()
    for k in range(1, groups):
        dev = (t, lax.rem(f + k, groups))
        for src, dst, ss, rs in ((w_ref, wall_ref, wsends, wrecvs), (m_ref, mall_ref, msends, mrecvs)):
            copy = pltpu.make_async_remote_copy(
                src_ref=src, dst_ref=dst.at[f], send_sem=ss.at[k], recv_sem=rs.at[k],
                device_id=dev, device_id_type=MESH,
            )
            copy.start()
            copies.append(copy)
    for copy in locals_:
        copy.wait()
    for copy in copies + edges[:2]:
        copy.wait()

    @pl.when(t < count - 1)
    def _():
        for copy in halo:
            copy.wait_send()

    @pl.when(t > 0)
    def _():
        for copy in halo:
            copy.wait_recv()


def prologue(frames, conv_shard, mix_shard):
    groups = lax.axis_size("fsdp")
    depth, height, width, channels = frames.shape
    edge = jax.ShapeDtypeStruct((2 * depth, height, channels), frames.dtype)
    vmem = pl.BlockSpec(memory_space=pltpu.VMEM)
    return pl.pallas_call(
        prologue_kernel,
        out_shape=(
            jax.ShapeDtypeStruct(frames.shape, frames.dtype),
            jax.ShapeDtypeStruct((groups,) + conv_shard.shape, conv_shard.dtype),
            jax.ShapeDtypeStruct((groups,) + mix_shard.shape, mix_shard.dtype),
            edge,
            edge,
        ),
        in_specs=[vmem] * 3,
        out_specs=(vmem,) * 5,
        scratch_shapes=[
            pltpu.VMEM((depth, height, channels), frames.dtype),
            pltpu.VMEM((depth, height, channels), frames.dtype),
            pltpu.SemaphoreType.DMA((4,)),
            pltpu.SemaphoreType.DMA((4,)),
            pltpu.SemaphoreType.DMA((groups,)),
            pltpu.SemaphoreType.DMA((groups,)),
            pltpu.SemaphoreType.DMA((groups,)),
            pltpu.SemaphoreType.DMA((groups,)),
            pltpu.SemaphoreType.DMA((2,)),
            pltpu.SemaphoreType.DMA((4,)),
            pltpu.SemaphoreType.DMA((4,)),
        ],
        compiler_params=pltpu.CompilerParams(collective_id=2, has_side_effects=True),
    )(frames, conv_shard, mix_shard)


def local(frames, conv_weight, mix_weight, cotangent):
    t = lax.axis_index("tm")
    count_frames, height, width, channels = frames.shape
    part = conv_weight.shape[-1]
    conv_shard = jnp.swapaxes(conv_weight, 3, 4).reshape(-1, part, channels)
    mix_shard = jnp.swapaxes(mix_weight, 1, 2)
    previous, wall, mall, left, right = prologue(frames, conv_shard, mix_shard)
    full_mix = jnp.transpose(mall, (1, 3, 0, 2)).reshape(mix_weight.shape[:-1] + (-1,))
    pooled = conv_pool(previous, frames, left, right, wall)
    branch = pooled.astype(jnp.float32).reshape(-1, channels)
    flat_cot = cotangent.reshape(-1, channels)
    grad_terms = []
    for offset in range(3):
        lagged = delayed(pooled, offset).reshape(-1, channels)
        branch = branch + jnp.dot(lagged, full_mix[offset], preferred_element_type=jnp.float32)
        grad_terms.append(
            lax.dot_general(
                lagged, flat_cot, (((0,), (0,)), ((), ())), preferred_element_type=jnp.float32
            )
        )
    encoded = branch.astype(jnp.bfloat16).reshape(pooled.shape)
    mix_grad = scatter_sum(jnp.stack(grad_terms).reshape(-1))
    return (encoded, mix_grad)


def solution(mesh):
    return jax.shard_map(
        local,
        mesh=mesh,
        in_specs=(
            P("tm", None, "fsdp", None),
            P(None, None, None, None, "fsdp"),
            P(None, None, "fsdp"),
            P(None, "tm", "fsdp", None),
        ),
        out_specs=(P(None, "tm", "fsdp", None), P(("tm", "fsdp"))),
        check_vma=False,
    )
```

```python
import jax
import jax.numpy as jnp
from jax import lax
from jax.experimental import pallas as pl
from jax.experimental.pallas import tpu as pltpu
from jax.sharding import PartitionSpec as P

MESH = pl.DeviceIdType.MESH


def from_behind(block, axis, distance):
    devices = range(lax.axis_size(axis))
    route = [(i - distance, i) for i in devices if i - distance in devices]
    return lax.ppermute(block, axis, route)


def with_halo(cells, sides, width):
    for axis, dim in sides:
        count = lax.axis_size(axis)
        ends = count - 1
        head = lax.slice_in_dim(cells, 0, width, axis=dim)
        tail = lax.slice_in_dim(cells, cells.shape[dim] - width, cells.shape[dim], axis=dim)
        cells = jnp.concatenate(
            [
                lax.ppermute(tail, axis, [(i, (i + 1) % count) for i in range(ends)]),
                cells,
                lax.ppermute(head, axis, [((i + 1) % count, i) for i in range(ends)]),
            ],
            axis=dim,
        )
    return cells


def pool_pairs(hidden):
    shaped = hidden.reshape((hidden.shape[0] // 2, 2) + hidden.shape[1:]).astype(jnp.float32)
    return ((shaped[:, 0] + shaped[:, 1]) * 0.5).astype(jnp.bfloat16)


def delayed(block, offset):
    return jnp.pad(block, ((offset, 0), (0, 0), (0, 0), (0, 0)))[: block.shape[0]]


def scatter_kernel(p_ref, o_ref, first, second, summed, s1, r1, s2, r2, l1, l2):
    count, groups = first.shape[0], second.shape[0]
    t, f = lax.axis_index("tm"), lax.axis_index("fsdp")
    barrier = pltpu.get_barrier_semaphore()
    for k in range(1, count):
        pl.semaphore_signal(
            barrier, inc=1, device_id={"tm": lax.rem(t + k, count)}, device_id_type=MESH
        )
    for k in range(1, groups):
        pl.semaphore_signal(
            barrier, inc=1, device_id={"fsdp": lax.rem(f + k, groups)}, device_id_type=MESH
        )
    pl.semaphore_wait(barrier, groups - 1 + count - 1)
    local = pltpu.make_async_copy(p_ref.at[t], first.at[t], l1)
    local.start()
    copies = []
    for k in range(1, count):
        peer = lax.rem(t + k, count)
        copy = pltpu.make_async_remote_copy(
            src_ref=p_ref.at[peer], dst_ref=first.at[t], send_sem=s1.at[k], recv_sem=r1.at[k],
            device_id={"tm": peer}, device_id_type=MESH,
        )
        copy.start()
        copies.append(copy)
    local.wait()
    for copy in copies:
        copy.wait()
    summed[...] = jnp.sum(first[...], axis=0)
    local = pltpu.make_async_copy(summed, second.at[f], l2)
    local.start()
    copies = []
    for k in range(1, groups):
        peer = lax.rem(f + k, groups)
        copy = pltpu.make_async_remote_copy(
            src_ref=summed, dst_ref=second.at[f], send_sem=s2.at[k], recv_sem=r2.at[k],
            device_id={"fsdp": peer}, device_id_type=MESH,
        )
        copy.start()
        copies.append(copy)
    local.wait()
    for copy in copies:
        copy.wait()
    o_ref[...] = jnp.sum(second[...], axis=0)


def scatter_sum(partial):
    groups, count = lax.axis_size("fsdp"), lax.axis_size("tm")
    rows = partial.size // (count * 128)
    out = pl.pallas_call(
        scatter_kernel,
        out_shape=jax.ShapeDtypeStruct((rows, 128), jnp.float32),
        in_specs=[pl.BlockSpec(memory_space=pltpu.VMEM)],
        out_specs=pl.BlockSpec(memory_space=pltpu.VMEM),
        scratch_shapes=[
            pltpu.VMEM((count, rows, 128), jnp.float32),
            pltpu.VMEM((groups, rows, 128), jnp.float32),
            pltpu.VMEM((rows, 128), jnp.float32),
            pltpu.SemaphoreType.DMA((count,)),
            pltpu.SemaphoreType.DMA((count,)),
            pltpu.SemaphoreType.DMA((groups,)),
            pltpu.SemaphoreType.DMA((groups,)),
            pltpu.SemaphoreType.DMA,
            pltpu.SemaphoreType.DMA,
        ],
        compiler_params=pltpu.CompilerParams(collective_id=1, has_side_effects=True),
    )(partial.reshape(count, rows, 128))
    piece = partial.size // (count * groups)
    return lax.dynamic_slice_in_dim(out.reshape(-1), lax.axis_index("fsdp") * piece, piece)


def conv_pool_kernel(h_ref, x_ref, l_ref, r_ref, wall_ref, o_ref, xs_ref, pooled_ref, w_ref, sends, recvs, local_sem):
    height, width, channels = pooled_ref.shape
    count, per_dev = o_ref.shape[0], o_ref.shape[1]
    me = lax.axis_index("tm")
    barrier = pltpu.get_barrier_semaphore()
    for k in range(1, count):
        pl.semaphore_signal(
            barrier, inc=1, device_id={"tm": lax.rem(me + k, count)}, device_id_type=MESH
        )
    depth = x_ref.shape[0]
    groups = lax.axis_size("fsdp")
    for tap in range(9):
        w_ref[tap] = jnp.concatenate(
            [wall_ref[:, a * 9 + tap].reshape(w_ref.shape[1], channels) for a in range(3)], axis=-1
        )
    t, f = lax.axis_index("tm"), lax.axis_index("fsdp")
    rows = 16
    zero_rows = jnp.zeros((3, 2 * depth, 1, width, channels), xs_ref.dtype)
    xs_ref[:, :, pl.ds(0, 1)] = zero_rows
    xs_ref[:, :, pl.ds(height + 1, 1)] = zero_rows
    col = lax.broadcasted_iota(jnp.int32, (rows, width, channels), 1)

    def shift(r, carry):
        top = pl.multiple_of(r * rows, rows)
        for q in range(2 * depth):
            earlier = q < depth
            src = h_ref if earlier else x_ref
            block = src[q % depth, pl.ds(top, rows)].astype(jnp.float32)
            lft = l_ref[q, pl.ds(top, rows)].astype(jnp.float32)[:, None, :]
            rgt = r_ref[q, pl.ds(top, rows)].astype(jnp.float32)[:, None, :]
            lok, rok = f > 0, f < groups - 1
            if earlier:
                block = jnp.where(t > 0, block, 0.0)
                lok, rok = lok & (t > 0), rok & (t > 0)
            lft = jnp.where(lok, lft, 0.0)
            rgt = jnp.where(rok, rgt, 0.0)
            moved = [
                jnp.where(col == 0, lft, pltpu.roll(block, 1, 1)),
                block,
                jnp.where(col == width - 1, rgt, pltpu.roll(block, width - 1, 1)),
            ]
            for c in range(3):
                xs_ref[c, q, pl.ds(top + 1, rows)] = moved[c].astype(xs_ref.dtype)
        return carry

    lax.fori_loop(0, height // rows, shift, 0)
    pl.semaphore_wait(barrier, count - 1)

    chunks, spread = height // rows, rows // per_dev

    def body(step, carry):
        r = lax.rem(step + me // spread + 1, chunks)
        top = pl.multiple_of(r * rows, rows)
        span = rows * width
        acc = jnp.zeros((2 * span, channels), jnp.float32)
        for b in range(3):
            for c in range(3):
                lhs = jnp.concatenate(
                    [
                        jnp.concatenate(
                            [xs_ref[c, j + a, pl.ds(top + b, rows)] for a in range(3)], axis=-1
                        ).reshape(span, 3 * channels)
                        for j in range(2)
                    ],
                    axis=0,
                )
                acc = acc + lax.dot_general(
                    lhs, w_ref[b * 3 + c], (((1,), (1,)), ((), ())),
                    preferred_element_type=jnp.float32,
                )
        silu = (acc / (1.0 + jnp.exp(-acc))).astype(jnp.bfloat16).astype(jnp.float32)
        pooled = ((silu[:span] + silu[span:]) * 0.5).astype(o_ref.dtype)
        pooled_ref[pl.ds(top, rows)] = pooled.reshape(rows, width, channels)
        for i in range(rows // per_dev):
            dest = r * (rows // per_dev) + i
            src = pooled_ref.at[pl.ds(top + i * per_dev, per_dev)]

            @pl.when(dest != me)
            def _():
                pltpu.make_async_remote_copy(
                    src_ref=src, dst_ref=o_ref.at[me], send_sem=sends.at[dest],
                    recv_sem=recvs.at[me], device_id={"tm": dest}, device_id_type=MESH,
                ).start()

            @pl.when(dest == me)
            def _():
                local = pltpu.make_async_copy(src, o_ref.at[me], local_sem)
                local.start()
                local.wait()

        return carry

    lax.fori_loop(0, height // rows, body, 0)

    @pl.loop(1, count)
    def _(k):
        peer = lax.rem(me + k, count)
        copy = pltpu.make_async_remote_copy(
            src_ref=pooled_ref.at[pl.ds(0, per_dev)], dst_ref=o_ref.at[peer],
            send_sem=sends.at[peer], recv_sem=recvs.at[peer],
            device_id={"tm": peer}, device_id_type=MESH,
        )
        copy.wait_send()
        copy.wait_recv()


def conv_pool(halo, frames, left, right, wall):
    depth, height, width, channels = frames.shape
    count = lax.axis_size("tm")
    vmem = pl.BlockSpec(memory_space=pltpu.VMEM)
    cout = wall.shape[0] * wall.shape[2]
    flops = 2 * 2 * height * width * 27 * channels * cout
    return pl.pallas_call(
        conv_pool_kernel,
        out_shape=jax.ShapeDtypeStruct((count, height // count, width, channels), jnp.bfloat16),
        in_specs=[vmem] * 5,
        out_specs=vmem,
        scratch_shapes=[
            pltpu.VMEM((3, 2 * depth, height + 8, width, channels), frames.dtype),
            pltpu.VMEM((height, width, channels), jnp.bfloat16),
            pltpu.VMEM((9, cout, 3 * channels), wall.dtype),
            pltpu.SemaphoreType.DMA((count,)),
            pltpu.SemaphoreType.DMA((count,)),
            pltpu.SemaphoreType.DMA,
        ],
        cost_estimate=pl.CostEstimate(
            flops=flops,
            transcendentals=2 * height * width * channels,
            bytes_accessed=4 * frames.size + wall.size * 2 + height * width * channels * 2,
        ),
        compiler_params=pltpu.CompilerParams(collective_id=3, has_side_effects=True),
    )(halo, frames, left, right, wall)


def prologue_kernel(x_ref, w_ref, m_ref, halo_ref, wall_ref, mall_ref, left_ref, right_ref, lcol_ref, rcol_ref, sends, recvs, wsends, wrecvs, msends, mrecvs, lsems, esends, erecvs):
    lcol_ref[...] = x_ref[:, :, 0, :]
    rcol_ref[...] = x_ref[:, :, x_ref.shape[2] - 1, :]
    count, groups = lax.axis_size("tm"), lax.axis_size("fsdp")
    t, f = lax.axis_index("tm"), lax.axis_index("fsdp")
    t_next, t_prev = lax.rem(t + 1, count), lax.rem(t + count - 1, count)
    f_next, f_prev = lax.rem(f + 1, groups), lax.rem(f + groups - 1, groups)
    peers = [(t_next, f), (t_prev, f)] + [(t, lax.rem(f + k, groups)) for k in range(1, groups)]
    peers += [(a, b) for a in (t_next, t_prev) for b in (f_next, f_prev)]
    barrier = pltpu.get_barrier_semaphore()
    for dev in peers:
        pl.semaphore_signal(barrier, inc=1, device_id=dev, device_id_type=MESH)
    pl.semaphore_wait(barrier, len(peers))
    pieces = sends.shape[0]
    rows = x_ref.shape[1] // pieces
    halo = [
        pltpu.make_async_remote_copy(
            src_ref=x_ref.at[:, pl.ds(i * rows, rows)],
            dst_ref=halo_ref.at[:, pl.ds(i * rows, rows)],
            send_sem=sends.at[i], recv_sem=recvs.at[i],
            device_id=(t_next, f), device_id_type=MESH,
        )
        for i in range(pieces)
    ]

    depth = x_ref.shape[0]
    edges = [
        (rcol_ref, left_ref.at[pl.ds(depth, depth)], (t, f_next)),
        (lcol_ref, right_ref.at[pl.ds(depth, depth)], (t, f_prev)),
        (rcol_ref, left_ref.at[pl.ds(0, depth)], (t_next, f_next)),
        (lcol_ref, right_ref.at[pl.ds(0, depth)], (t_next, f_prev)),
    ]
    edges = [
        pltpu.make_async_remote_copy(
            src_ref=src, dst_ref=dst, send_sem=esends.at[i], recv_sem=erecvs.at[i],
            device_id=dev, device_id_type=MESH,
        )
        for i, (src, dst, dev) in enumerate(edges)
    ]
    for copy in edges[:2]:
        copy.start()
    halo = halo + edges[2:]

    @pl.when(t < count - 1)
    def _():
        for copy in halo:
            copy.start()

    copies = []
    locals_ = [
        pltpu.make_async_copy(w_ref, wall_ref.at[f], lsems.at[0]),
        pltpu.make_async_copy(m_ref, mall_ref.at[f], lsems.at[1]),
    ]
    for copy in locals_:
        copy.start()
    for k in range(1, groups):
        dev = (t, lax.rem(f + k, groups))
        for src, dst, ss, rs in ((w_ref, wall_ref, wsends, wrecvs), (m_ref, mall_ref, msends, mrecvs)):
            copy = pltpu.make_async_remote_copy(
                src_ref=src, dst_ref=dst.at[f], send_sem=ss.at[k], recv_sem=rs.at[k],
                device_id=dev, device_id_type=MESH,
            )
            copy.start()
            copies.append(copy)
    for copy in locals_:
        copy.wait()
    for copy in copies + edges[:2]:
        copy.wait()

    @pl.when(t < count - 1)
    def _():
        for copy in halo:
            copy.wait_send()

    @pl.when(t > 0)
    def _():
        for copy in halo:
            copy.wait_recv()


def prologue(frames, conv_shard, mix_shard):
    groups = lax.axis_size("fsdp")
    depth, height, width, channels = frames.shape
    edge = jax.ShapeDtypeStruct((2 * depth, height, channels), frames.dtype)
    vmem = pl.BlockSpec(memory_space=pltpu.VMEM)
    return pl.pallas_call(
        prologue_kernel,
        out_shape=(
            jax.ShapeDtypeStruct(frames.shape, frames.dtype),
            jax.ShapeDtypeStruct((groups,) + conv_shard.shape, conv_shard.dtype),
            jax.ShapeDtypeStruct((groups,) + mix_shard.shape, mix_shard.dtype),
            edge,
            edge,
        ),
        in_specs=[vmem] * 3,
        out_specs=(vmem,) * 5,
        scratch_shapes=[
            pltpu.VMEM((depth, height, channels), frames.dtype),
            pltpu.VMEM((depth, height, channels), frames.dtype),
            pltpu.SemaphoreType.DMA((4,)),
            pltpu.SemaphoreType.DMA((4,)),
            pltpu.SemaphoreType.DMA((groups,)),
            pltpu.SemaphoreType.DMA((groups,)),
            pltpu.SemaphoreType.DMA((groups,)),
            pltpu.SemaphoreType.DMA((groups,)),
            pltpu.SemaphoreType.DMA((2,)),
            pltpu.SemaphoreType.DMA((4,)),
            pltpu.SemaphoreType.DMA((4,)),
        ],
        compiler_params=pltpu.CompilerParams(collective_id=2, has_side_effects=True),
    )(frames, conv_shard, mix_shard)


def local(frames, conv_weight, mix_weight, cotangent):
    t = lax.axis_index("tm")
    count_frames, height, width, channels = frames.shape
    part = conv_weight.shape[-1]
    conv_shard = jnp.swapaxes(conv_weight, 3, 4).reshape(-1, part, channels)
    mix_shard = jnp.swapaxes(mix_weight, 1, 2)
    previous, wall, mall, left, right = prologue(frames, conv_shard, mix_shard)
    full_mix = jnp.transpose(mall, (1, 3, 0, 2)).reshape(mix_weight.shape[:-1] + (-1,))
    pooled = conv_pool(previous, frames, left, right, wall)
    branch = pooled.astype(jnp.float32).reshape(-1, channels)
    flat_cot = cotangent.reshape(-1, channels)
    grad_terms = []
    for offset in range(3):
        lagged = delayed(pooled, offset).reshape(-1, channels)
        branch = branch + jnp.dot(lagged, full_mix[offset], preferred_element_type=jnp.float32)
        grad_terms.append(
            lax.dot_general(
                lagged, flat_cot, (((0,), (0,)), ((), ())), preferred_element_type=jnp.float32
            )
        )
    encoded = branch.astype(jnp.bfloat16).reshape(pooled.shape)
    mix_grad = scatter_sum(jnp.stack(grad_terms).reshape(-1))
    return (encoded, mix_grad)


def solution(mesh):
    return jax.shard_map(
        local,
        mesh=mesh,
        in_specs=(
            P("tm", None, "fsdp", None),
            P(None, None, None, None, "fsdp"),
            P(None, None, "fsdp"),
            P(None, "tm", "fsdp", None),
        ),
        out_specs=(P(None, "tm", "fsdp", None), P(("tm", "fsdp"))),
        check_vma=False,
    )
```
